256 devices in a mesh: date: 32 (over y, x, core), row: 8 (over z).
Axes of the slice: x: 4, y: 4, z: 8, core: 2. Of those that a mesh axis runs over, the one named last changes fastest.
Arguments:
- slc: float32 [2, 32, 64, 4096], P(None, 'date', 'row'), may hold values from -6 to 6
- offsets: int32 [2, 32], replicated, may hold values from -2 to 2, as said below
- masks: int32 [5, 64, 4096], P(None, 'row', 'date'), may hold values from 0 to 262143, as said below
Outputs:
- linked: float32 [2, 32, 64, 4096], P(None, None, 'row', 'date')
- eigen: float32 [64, 4096], P('row', 'date')
The draws below stay inside these ranges and needn't reach their ends.
Inputs may be any that keep to these rules, and one draw needn't show every extreme that they name: `offsets`: row offset in the first row, column offset in the second; some date has 2 in both and another date -2 in both. `masks`: bit (k mod 18) of word k // 18 tells whether slot k of the pixel's neighbourhood is used; the centre slot 40 is always set; bits of slots 81 and above are zero.
All inputs are finite; a program needn't handle non-finite values.
Results may differ from the reference program's by a relative error of at most 0.00011.
Values sent between devices are 32-bit elements; how exact they have to be, the bound alone decides.
A program may use at most 64 MiB of HBM per device.

```python
import jax
import jax.numpy as jnp
from jax import lax

NDATE = 32
HALF = 4
SHIFT = 2
ITERS = 2
ROWS = 64
COLS = 4096
SLOTS = 81
WORDS = 5


def draw_offsets(key, part):
    base = jax.random.randint(jax.random.fold_in(key, 1), (2, NDATE), -SHIFT, SHIFT + 1).astype(jnp.int32)
    order = jax.random.permutation(jax.random.fold_in(key, 2), NDATE).astype(jnp.int32)
    date_ids = jnp.arange(NDATE, dtype=jnp.int32)
    base = jnp.where((date_ids == order[0])[None, :], SHIFT, base)
    base = jnp.where((date_ids == order[1])[None, :], -SHIFT, base)
    return base.astype(jnp.int32)


def draw_masks(key, part):
    density = jax.random.randint(jax.random.fold_in(key, 1), (ROWS, COLS), 15, 101).astype(jnp.int32)
    centre = SLOTS // 2
    weights = jnp.left_shift(jnp.ones((18,), jnp.int32), jnp.arange(18, dtype=jnp.int32))
    packed = []
    for word_index in range(WORDS):
        uniform_draws = jax.random.randint(jax.random.fold_in(key, 10 + word_index), (18, ROWS, COLS), 0, 100).astype(jnp.int32)
        slot_ids = word_index * 18 + jnp.arange(18, dtype=jnp.int32)
        mask_bits = (uniform_draws < density[None]).astype(jnp.int32)
        mask_bits = jnp.where((slot_ids == centre)[:, None, None], 1, mask_bits)
        mask_bits = jnp.where((slot_ids < SLOTS)[:, None, None], mask_bits, 0)
        packed.append(jnp.sum(mask_bits * weights[:, None, None], axis=0).astype(jnp.int32))
    return jnp.stack(packed).astype(jnp.int32)


def level_of(key, shape, shards, smallest, top_value):
    def one(axis_at, shards_of):
        steps = jax.random.uniform(jax.random.fold_in(jax.random.fold_in(key, 6), axis_at), (shards_of,), jnp.float32, smallest / len(shards), top_value / len(shards))
        return jnp.repeat(jnp.exp(steps), shape[axis_at] // shards_of).reshape((-1,) + (1,) * (len(shape) - axis_at - 1))

    loudness = one(*shards[0])
    for cut in shards[1:]:
        loudness = loudness * one(*cut)
    return loudness


def scatter_about(stream_key, dims, width, reach, cuts=(), held_as=jnp.bfloat16):
    values = jax.random.normal(stream_key, dims, jnp.float32) * width
    if len(cuts) > 0:
        values = level_of(stream_key, dims, cuts, -0.22, 0.18) * values
    return jnp.clip(values, min=-reach, max=reach).astype(held_as)


def setup_inputs(seed: int = 0) -> dict:
    splits = jax.random.split(jax.random.key(seed), 4)
    return {
        "slc": scatter_about(splits[0], (2, NDATE, ROWS, COLS), 1.0, 6.0, ((1, 32), (2, 8)), jnp.float32),
        "offsets": draw_offsets(jax.random.fold_in(splits[3], 71), 0),
        "masks": draw_masks(jax.random.fold_in(splits[3], 71), 0),
    }


TAPS = (-0.0625, 0.5625, 0.5625, -0.0625)
EPSILON = 1e-06

def shift_mix(image_plane, shifts, margin, out_rows, out_cols):
    row_taps = lax.dynamic_slice_in_dim(image_plane, margin - 1 + shifts[0], out_rows + 3, 1)
    row_mixed = TAPS[0] * row_taps[:, 0:out_rows]
    for tap_index in range(1, 4):
        row_mixed = row_mixed + TAPS[tap_index] * row_taps[:, tap_index:tap_index + out_rows]
    col_taps = lax.dynamic_slice_in_dim(row_mixed, margin - 1 + shifts[1], out_cols + 3, 2)
    col_mixed = TAPS[0] * col_taps[:, :, 0:out_cols]
    for tap_index in range(1, 4):
        col_mixed = col_mixed + TAPS[tap_index] * col_taps[:, :, tap_index:tap_index + out_cols]
    return col_mixed

def unpack_bits(mask_words):
    shift_ids = jnp.arange(18, dtype=jnp.int32)
    spread = jnp.right_shift(mask_words[:, None, :], shift_ids[None, :, None]) & 1
    return spread.reshape(-1, mask_words.shape[-1])[:SLOTS].astype(jnp.float32)

def power_norm(vec_real, vec_imag):
    return jnp.sqrt(lax.optimization_barrier(jnp.sum(vec_real * vec_real + vec_imag * vec_imag, axis=0)) + EPSILON)

def link_phases(patches, mask_bits):
    dates = patches.shape[0] // 2
    population = lax.optimization_barrier(jnp.sum(mask_bits, axis=0))
    weighted = patches * mask_bits[None]
    gram_matrix = jnp.einsum('ikp,jkp->ijp', weighted, patches, precision=lax.Precision.HIGHEST) / population
    cov_real = gram_matrix[:dates, :dates] + gram_matrix[dates:, dates:]
    cov_imag = gram_matrix[dates:, :dates] - gram_matrix[:dates, dates:]
    vec_real = jnp.ones((dates, patches.shape[-1]), jnp.float32)
    vec_imag = jnp.zeros((dates, patches.shape[-1]), jnp.float32)
    norm_prev = power_norm(vec_real, vec_imag)
    for step_index in range(ITERS):
        norm_prev = power_norm(vec_real, vec_imag)
        next_real = jnp.einsum('tup,up->tp', cov_real, vec_real, precision=lax.Precision.HIGHEST) - jnp.einsum('tup,up->tp', cov_imag, vec_imag, precision=lax.Precision.HIGHEST)
        next_imag = jnp.einsum('tup,up->tp', cov_real, vec_imag, precision=lax.Precision.HIGHEST) + jnp.einsum('tup,up->tp', cov_imag, vec_real, precision=lax.Precision.HIGHEST)
        vec_real, vec_imag = (next_real, next_imag)
    norm_last = power_norm(vec_real, vec_imag)
    linked = jnp.stack([vec_real, vec_imag]) * (jnp.sqrt(jnp.float32(dates)) / norm_last)
    return (linked, norm_last / norm_prev)

def reference(slc, offsets, masks):
    margin = SHIFT + 2
    padded_raw = jnp.pad(slc, ((0, 0), (0, 0), (margin, margin), (margin, margin)))
    resampled = jax.vmap(lambda image_plane, shifts: shift_mix(image_plane, shifts, margin, ROWS, COLS), in_axes=(1, 1), out_axes=1)(padded_raw, offsets)
    window = jnp.pad(resampled, ((0, 0), (0, 0), (HALF, HALF), (HALF, HALF)))
    side = 2 * HALF + 1

    def one_row(row_index):
        row_block = lax.dynamic_slice_in_dim(window, row_index, side, 2)
        patches = jnp.stack([row_block[..., col_step:col_step + COLS] for col_step in range(side)], axis=3)
        patches = patches.reshape(2 * NDATE, SLOTS, COLS)
        mask_bits = unpack_bits(lax.dynamic_index_in_dim(masks, row_index, 1, keepdims=False))
        return link_phases(patches, mask_bits)
    linked_rows, eigen_rows = lax.map(one_row, jnp.arange(ROWS, dtype=jnp.int32))
    return (jnp.transpose(linked_rows, (1, 2, 0, 3)), eigen_rows)
```

```python
import functools

import jax
import jax.numpy as jnp
from jax import lax
from jax.experimental import pallas as pl
from jax.experimental.pallas import tpu as pltpu
from jax.sharding import PartitionSpec as P

NDATE = 32
COLS = 128
ROWS = 8
PLANES = 2 * NDATE
EPSILON = 1e-06
MESH = pl.DeviceIdType.MESH
F32 = jnp.float32
BF16 = jnp.bfloat16


def iota(shape, axis):
    return lax.broadcasted_iota(jnp.int32, shape, axis)


def pack_rim(slc_ref, rim_ref):
    lane = iota((ROWS, COLS), 1)
    row = iota((ROWS, COLS), 0)
    for dest in range(NDATE):
        for part in range(2):
            if dest > 0:
                left = slc_ref[part, :, (dest - 1) * COLS : dest * COLS]
            else:
                left = jnp.zeros((ROWS, COLS), F32)
            if dest < NDATE - 1:
                right = slc_ref[part, :, (dest + 1) * COLS : (dest + 2) * COLS]
            else:
                right = jnp.zeros((ROWS, COLS), F32)
            both = jnp.where(lane < 8, right, left)
            spread = pltpu.roll(both, 8, 1, stride=16, stride_axis=0)
            spread = jnp.where(lane // 16 == row, spread, 0.0)
            rim_ref[dest, part : part + 1, :] = jnp.sum(spread, axis=0, keepdims=True)


def pack_kernel(slc_ref, rim_ref):
    pack_rim(slc_ref, rim_ref)


def exchange_kernel(
    slc_ref, rim_in, main_ref, rim_ref, own_sem, send_sem, recv_sem, fwd_send, fwd_recv
):
    me = lax.axis_index("date")
    z = lax.axis_index("row")
    last_z = lax.axis_size("row") - 1
    block, place = me // 8, me % 8

    barrier = pltpu.get_barrier_semaphore()
    for s in range(1, NDATE):
        pl.semaphore_signal(
            barrier, inc=1, device_id={"date": (me + s) % NDATE}, device_id_type=MESH
        )

    for s in (1, last_z):
        pl.semaphore_signal(
            barrier, inc=1, device_id={"row": (z + s) % (last_z + 1)}, device_id_type=MESH
        )
    pl.semaphore_wait(barrier, NDATE + 1)

    own = [
        pltpu.make_async_copy(
            slc_ref.at[:, :, pl.ds(pl.multiple_of(me * COLS, COLS), COLS)],
            main_ref.at[1, me],
            own_sem.at[0],
        ),
        pltpu.make_async_copy(rim_in.at[me], rim_ref.at[1, me], own_sem.at[1]),
    ]
    for copy in own:
        copy.start()

    sends = []
    for g in range(4):
        for j in range(8):
            if g == 0 and j == 0:
                continue
            dest = ((block + g) % 4) * 8 + (place + j) % 8
            for which, src, dst in (
                (
                    0,
                    slc_ref.at[:, :, pl.ds(pl.multiple_of(dest * COLS, COLS), COLS)],
                    main_ref.at[1, me],
                ),
                (1, rim_in.at[dest], rim_ref.at[1, me]),
            ):
                copy = pltpu.make_async_remote_copy(
                    src_ref=src,
                    dst_ref=dst,
                    send_sem=send_sem.at[which, g, j],
                    recv_sem=recv_sem.at[which, g, j],
                    device_id={"date": dest},
                    device_id_type=MESH,
                )
                copy.start()
                sends.append((g, j, copy))

    for copy in own:
        copy.wait()

    def forwards(g, side):
        group = (block + 4 - g) % 4
        slot, to = (2, z - 1) if side == 0 else (0, z + 1)
        first = pl.multiple_of(group * 8, 8)
        return [
            pltpu.make_async_remote_copy(
                src_ref=ref.at[1, pl.ds(first, 8)],
                dst_ref=ref.at[slot, pl.ds(first, 8)],
                send_sem=fwd_send.at[which, side, g],
                recv_sem=fwd_recv.at[which, side, g],
                device_id={"row": to},
                device_id_type=MESH,
            )
            for which, ref in ((0, main_ref), (1, rim_ref))
        ]

    for g in range(4):
        for step, _, copy in sends:
            if step == g:
                copy.wait_recv()

        @pl.when(z > 0)
        def _(g=g):
            for copy in forwards(g, 0):
                copy.start()

        @pl.when(z < last_z)
        def _(g=g):
            for copy in forwards(g, 1):
                copy.start()

    for _, _, copy in sends:
        copy.wait_send()
    for g in range(4):

        @pl.when(z > 0)
        def _(g=g):
            for copy in forwards(g, 0):
                copy.wait_send()
            for copy in forwards(g, 1):
                copy.wait_recv()

        @pl.when(z < last_z)
        def _(g=g):
            for copy in forwards(g, 1):
                copy.wait_send()
            for copy in forwards(g, 0):
                copy.wait_recv()


def exchange(slc):
    rim_in = pl.pallas_call(
        pack_kernel,
        out_shape=jax.ShapeDtypeStruct((NDATE, 2, COLS), F32),
        name="pack",
    )(slc)
    return pl.pallas_call(
        exchange_kernel,
        out_shape=(
            jax.ShapeDtypeStruct((3, NDATE, 2, ROWS, COLS), F32),
            jax.ShapeDtypeStruct((3, NDATE, 2, COLS), F32),
        ),
        in_specs=[pl.BlockSpec(memory_space=pl.ANY)] * 2,
        out_specs=(pl.BlockSpec(memory_space=pl.ANY),) * 2,
        scratch_shapes=[
            pltpu.SemaphoreType.DMA((2,)),
            pltpu.SemaphoreType.DMA((2, 4, 8)),
            pltpu.SemaphoreType.DMA((2, 4, 8)),
            pltpu.SemaphoreType.DMA((2, 2, 4)),
            pltpu.SemaphoreType.DMA((2, 2, 4)),
        ],
        compiler_params=pltpu.CompilerParams(collective_id=0, has_side_effects=True),
        name="exchange",
    )(slc, rim_in)


WIN = 16
GROUPS = 17


def split(x):
    high = x.astype(BF16).astype(F32)
    return high, x - high


def date_vectors(offs_ref, axis):
    if axis == 0:
        row = iota((8, COLS), 0)
        out = []
        for part in range(4):
            vec = jnp.zeros((8, COLS), jnp.int32)
            for s in range(8):
                vec = jnp.where(row == s, offs_ref[0, part * 8 + s] + 2, vec)
            out.append(vec)
        return out
    lane = iota((8, COLS), 1) % NDATE
    vec = jnp.zeros((8, COLS), jnp.int32)
    row_vec = jnp.zeros((8, COLS), jnp.int32)
    for s in range(NDATE):
        vec = jnp.where(lane == s, offs_ref[1, s] + 2, vec)
        row_vec = jnp.where(lane == s, offs_ref[0, s] + 2, row_vec)
    return vec, row_vec


def mix_rows(rows, steps):
    bit0, bit1, bit2 = (steps & 1) != 0, (steps & 2) != 0, steps == 4
    one = [jnp.where(bit0, rows[i + 1], rows[i]) for i in range(22)]
    two = [jnp.where(bit1, one[i + 2], one[i]) for i in range(19)]
    base = [jnp.where(bit2, rows[i + 4], two[i]) for i in range(19)]
    return [
        0.5625 * (base[i + 1] + base[i + 2]) - 0.0625 * (base[i] + base[i + 3]) for i in range(WIN)
    ]


def link_kernel(
    pos_ref,
    offs_ref,
    main_ref,
    rim_ref,
    mask_ref,
    out_ref,
    eigen_ref,
    mixed,
    tall,
    rim_tall,
    keys,
    plain,
    sums,
    slots,
    vecs,
):
    date_pos, row_pos, last_date, last_row = (pos_ref[i] for i in range(4))
    lane8 = iota((8, COLS), 1)
    sub8 = iota((8, COLS), 0)

    row_steps = date_vectors(offs_ref, 0)
    col_steps, lane_row_steps = date_vectors(offs_ref, 1)
    for part in range(2):
        for eight in range(4):
            rows = []
            for i in range(23):
                slot, row = (i + 1) // 8, (i + 1) % 8
                start = ((slot * NDATE + eight * 8) * 2 + part) * ROWS + row
                x = main_ref[pl.ds(start, 8, stride=2 * ROWS), :]
                if slot == 0:
                    x = jnp.where(row_pos > 0, x, 0.0)
                if slot == 2:
                    x = jnp.where(row_pos < last_row, x, 0.0)
                rows.append(x)
            for i, x in enumerate(mix_rows(rows, row_steps[eight])):
                mixed[i, part * NDATE + eight * 8 : part * NDATE + eight * 8 + 8, :] = x

    for slot in range(3):
        x = jnp.concatenate([rim_ref[slot, :, 0, :], rim_ref[slot, :, 1, :]], axis=0)
        if slot == 0:
            x = jnp.where(row_pos > 0, x, 0.0)
        if slot == 2:
            x = jnp.where(row_pos < last_row, x, 0.0)
        rim_tall[slot] = jnp.concatenate([x, x], axis=0).T
    for side in range(2):
        rows = []
        for i in range(23):
            slot, row = (i + 1) // 8, (i + 1) % 8
            rows.append(rim_tall[slot, 16 * row + 8 * side : 16 * row + 8 * side + 8, :])
        done = mix_rows(rows, lane_row_steps)
        for m in range(8):
            tall[m, 136 * side : 136 * side + 8, :] = jnp.where(
                lane8 < PLANES, done[2 * m], done[2 * m + 1]
            )

    for m in range(8):
        tall[m, 8:136, :] = jnp.concatenate([mixed[2 * m], mixed[2 * m + 1]], axis=0).T
    for m in range(8):
        row = 8 * row_pos - 4 + 2 * m + (lane8 >= PLANES).astype(jnp.int32)
        inside = (row >= 0) & (row < 8 * (last_row + 1))
        weights = []
        for s in range(8):
            w = jnp.zeros((8, COLS), F32)
            for tap, value in enumerate((-0.0625, 0.5625, 0.5625, -0.0625)):
                w = jnp.where(col_steps + tap == s, value, w)
            weights.append(jnp.where(inside, w, 0.0))
        for g in range(GROUPS):
            x = weights[0] * tall[m, 8 * g + 1 : 8 * g + 9, :]
            for s in range(1, 8):
                x = x + weights[s] * tall[m, 8 * g + 1 + s : 8 * g + 9 + s, :]
            if g == 0:
                x = jnp.where((sub8 >= 4) | (date_pos > 0), x, 0.0)
            if g == GROUPS - 1:
                x = jnp.where((sub8 < 4) | (date_pos < last_date), x, 0.0)
            other = pltpu.roll(x, PLANES, 1)
            a = jnp.where(lane8 < PLANES, x, other)
            b = jnp.where(lane8 < PLANES, other, x)
            z = jnp.concatenate([a, b], axis=0)
            high, low = split(z)
            lane16 = iota((16, COLS), 1)
            first = g * COLS + 16 * m
            keys[first : first + 16, :] = jnp.where(lane16 < PLANES, high, low).astype(BF16)
            plain[first : first + 16, :] = z

    k_in = iota((COLS, COLS), 0) // NDATE % 2
    k_out = iota((COLS, COLS), 1) // PLANES
    adder = jnp.where(k_in == k_out, 1.0, 0.0).astype(BF16)
    for g in range(GROUPS):
        rows = slice(g * COLS, (g + 1) * COLS)
        total = jnp.dot(keys[rows, :], adder, preferred_element_type=F32)
        high, low = split(plain[rows, :] * total)
        sums[rows, :COLS] = high.astype(BF16)
        sums[rows, COLS:] = low.astype(BF16)

    population = jnp.zeros((8, COLS), jnp.int32)
    for w in range(5):
        population = population + lax.population_count(mask_ref[w])
    population = population.astype(F32)
    zero8 = jnp.zeros((8, COLS), jnp.int32)
    for r in range(8):
        pieces = []
        for n in range(WIN):
            i = n - r
            if 0 <= i <= 8:
                nine = (mask_ref[i // 2, r : r + 1, :] >> (9 * (i % 2))) & 511
                pieces.append(jnp.broadcast_to(nine, (8, COLS)))
            else:
                pieces.append(zero8)
        slots[r] = jnp.concatenate(pieces, axis=0).T

    across = lane8 % 8 - sub8
    shift0 = jnp.where(across >= 0, across, 31)
    shift1 = jnp.where(across <= 0, across + 8, 31)
    lane64 = iota((64, COLS), 1)
    quarter = lane64 // NDATE
    outer = (quarter == 0) | (quarter == 3)
    sign_a = jnp.where(quarter % 2 == 0, 1.0, -1.0)

    def one_block(blk, carry):
        q0 = pl.multiple_of(blk * COLS, COLS)
        c0 = pl.multiple_of(blk * 8, 8)
        near = keys[pl.ds(q0, 2 * COLS), :]
        bits = []
        for r in range(8):
            w = slots[r, pl.ds(c0, 8), :]
            bits.append(jnp.concatenate([(w >> shift0) & 1, (w >> shift1) & 1], axis=1))
        mask = jnp.concatenate(bits, axis=0).astype(F32)
        u = jnp.dot(mask.astype(BF16), sums[pl.ds(q0, 2 * COLS), :], preferred_element_type=F32)
        u = u[:, :COLS] + u[:, COLS:]
        same = jnp.where(lane64 < PLANES, u, pltpu.roll(u, PLANES, 1))
        cross = jnp.where(outer, pltpu.roll(u, 32, 1), pltpu.roll(u, 96, 1))
        v = same + sign_a * cross
        turned = sign_a * pltpu.roll(v, 32, 1)
        both = jnp.concatenate([v, turned], axis=0)
        high, low = split(both)
        left = jnp.concatenate([high, low], axis=1).astype(BF16)
        right = jnp.concatenate([near, near], axis=1)
        a = lax.dot_general(
            left, right, (((1,), (1,)), ((), ())), preferred_element_type=F32
        )
        a = a * jnp.concatenate([mask, mask], axis=0)
        high, low = split(a)
        c = jnp.dot(high.astype(BF16), near, preferred_element_type=F32) + jnp.dot(
            low.astype(BF16), near, preferred_element_type=F32
        )
        c = c + pltpu.roll(c, PLANES, 1)
        v2 = c[:64] - sign_a * pltpu.roll(c[64:], 32, 1)
        both = jnp.where(lane64 < PLANES, v2, v)
        for r in range(8):
            vecs[r, pl.ds(c0, 8), :] = both[8 * r : 8 * r + 8, :]
        return carry

    lax.fori_loop(0, 16, one_block, 0)

    for r in range(8):
        x = vecs[r].T
        pop = population[r : r + 1, :]
        inv = 1.0 / pop
        n1 = jnp.sum(x[PLANES:] * x[PLANES:], axis=0, keepdims=True) * (inv * inv)
        inv2 = inv * inv
        x2 = x[:PLANES] * inv2
        n2 = jnp.sum(x2 * x2, axis=0, keepdims=True)
        root2 = jnp.sqrt(n2 + EPSILON)
        root1 = jnp.sqrt(n1 + EPSILON)
        eigen_ref[r : r + 1, :] = root2 / root1
        out_ref[pl.ds(r, PLANES, stride=ROWS), :] = x2 * (jnp.sqrt(F32(NDATE)) / root2)


def link(pos, offsets, main, rim, masks):
    smem = pl.BlockSpec(memory_space=pltpu.SMEM)
    vmem = pl.BlockSpec(memory_space=pltpu.VMEM)
    linked, eigen = pl.pallas_call(
        link_kernel,
        out_shape=(
            jax.ShapeDtypeStruct((PLANES * ROWS, COLS), F32),
            jax.ShapeDtypeStruct((ROWS, COLS), F32),
        ),
        in_specs=[smem, smem, vmem, vmem, vmem],
        out_specs=(vmem, vmem),
        scratch_shapes=[
            pltpu.VMEM((WIN, PLANES, COLS), F32),
            pltpu.VMEM((8, 144, COLS), F32),
            pltpu.VMEM((3, COLS, COLS), F32),
            pltpu.VMEM((GROUPS * COLS, COLS), BF16),
            pltpu.VMEM((GROUPS * COLS, COLS), F32),
            pltpu.VMEM((GROUPS * COLS, 2 * COLS), BF16),
            pltpu.VMEM((8, COLS, COLS), jnp.int32),
            pltpu.VMEM((8, COLS, COLS), F32),
        ],
        compiler_params=pltpu.CompilerParams(vmem_limit_bytes=48 * 1024 * 1024),
        name="link",
    )(pos, offsets, main.reshape(-1, COLS), rim, masks)
    return linked.reshape(2, NDATE, ROWS, COLS), eigen


def on_device(slc, offsets, masks):
    main, rim = exchange(slc[:, 0])
    pos = jnp.stack(
        [
            lax.axis_index("date"),
            lax.axis_index("row"),
            jnp.int32(lax.axis_size("date") - 1),
            jnp.int32(lax.axis_size("row") - 1),
        ]
    ).astype(jnp.int32)
    return link(pos, offsets, main, rim, masks)


def solution(mesh):
    in_specs = (P(None, "date", "row", None), P(), P(None, "row", "date"))
    out_specs = (P(None, None, "row", "date"), P("row", "date"))
    return jax.shard_map(
        on_device, mesh=mesh, in_specs=in_specs, out_specs=out_specs, check_vma=False
    )
```

```python
import functools

import jax
import jax.numpy as jnp
from jax import lax
from jax.experimental import pallas as pl
from jax.experimental.pallas import tpu as pltpu
from jax.sharding import PartitionSpec as P

NDATE = 32
COLS = 128
ROWS = 8
PLANES = 2 * NDATE
EPSILON = 1e-06
MESH = pl.DeviceIdType.MESH
F32 = jnp.float32
BF16 = jnp.bfloat16


def iota(shape, axis):
    return lax.broadcasted_iota(jnp.int32, shape, axis)


def pack_rim(slc_ref, rim_ref):
    lane = iota((ROWS, COLS), 1)
    row = iota((ROWS, COLS), 0)
    for dest in range(NDATE):
        for part in range(2):
            if dest > 0:
                left = slc_ref[part, :, (dest - 1) * COLS : dest * COLS]
            else:
                left = jnp.zeros((ROWS, COLS), F32)
            if dest < NDATE - 1:
                right = slc_ref[part, :, (dest + 1) * COLS : (dest + 2) * COLS]
            else:
                right = jnp.zeros((ROWS, COLS), F32)
            both = jnp.where(lane < 8, right, left)
            spread = pltpu.roll(both, 8, 1, stride=16, stride_axis=0)
            spread = jnp.where(lane // 16 == row, spread, 0.0)
            rim_ref[dest, part : part + 1, :] = jnp.sum(spread, axis=0, keepdims=True)


def pack_kernel(slc_ref, rim_ref):
    pack_rim(slc_ref, rim_ref)


def exchange_kernel(
    slc_ref, rim_in, main_ref, rim_ref, own_sem, send_sem, recv_sem, fwd_send, fwd_recv
):
    me = lax.axis_index("date")
    z = lax.axis_index("row")
    last_z = lax.axis_size("row") - 1
    block, place = me // 8, me % 8

    barrier = pltpu.get_barrier_semaphore()
    for s in range(1, NDATE):
        pl.semaphore_signal(
            barrier, inc=1, device_id={"date": (me + s) % NDATE}, device_id_type=MESH
        )

    for s in (1, last_z):
        pl.semaphore_signal(
            barrier, inc=1, device_id={"row": (z + s) % (last_z + 1)}, device_id_type=MESH
        )
    pl.semaphore_wait(barrier, NDATE + 1)

    own = [
        pltpu.make_async_copy(
            slc_ref.at[:, :, pl.ds(pl.multiple_of(me * COLS, COLS), COLS)],
            main_ref.at[1, me],
            own_sem.at[0],
        ),
        pltpu.make_async_copy(rim_in.at[me], rim_ref.at[1, me], own_sem.at[1]),
    ]
    for copy in own:
        copy.start()

    sends = []
    for g in range(4):
        for j in range(8):
            if g == 0 and j == 0:
                continue
            dest = ((block + g) % 4) * 8 + (place + j) % 8
            for which, src, dst in (
                (
                    0,
                    slc_ref.at[:, :, pl.ds(pl.multiple_of(dest * COLS, COLS), COLS)],
                    main_ref.at[1, me],
                ),
                (1, rim_in.at[dest], rim_ref.at[1, me]),
            ):
                copy = pltpu.make_async_remote_copy(
                    src_ref=src,
                    dst_ref=dst,
                    send_sem=send_sem.at[which, g, j],
                    recv_sem=recv_sem.at[which, g, j],
                    device_id={"date": dest},
                    device_id_type=MESH,
                )
                copy.start()
                sends.append((g, j, copy))

    for copy in own:
        copy.wait()

    def forwards(g, side):
        group = (block + 4 - g) % 4
        slot, to = (2, z - 1) if side == 0 else (0, z + 1)
        first = pl.multiple_of(group * 8, 8)
        return [
            pltpu.make_async_remote_copy(
                src_ref=ref.at[1, pl.ds(first, 8)],
                dst_ref=ref.at[slot, pl.ds(first, 8)],
                send_sem=fwd_send.at[which, side, g],
                recv_sem=fwd_recv.at[which, side, g],
                device_id={"row": to},
                device_id_type=MESH,
            )
            for which, ref in ((0, main_ref), (1, rim_ref))
        ]

    for g in range(4):
        for step, _, copy in sends:
            if step == g:
                copy.wait_recv()

        @pl.when(z > 0)
        def _(g=g):
            for copy in forwards(g, 0):
                copy.start()

        @pl.when(z < last_z)
        def _(g=g):
            for copy in forwards(g, 1):
                copy.start()

    for _, _, copy in sends:
        copy.wait_send()
    for g in range(4):

        @pl.when(z > 0)
        def _(g=g):
            for copy in forwards(g, 0):
                copy.wait_send()
            for copy in forwards(g, 1):
                copy.wait_recv()

        @pl.when(z < last_z)
        def _(g=g):
            for copy in forwards(g, 1):
                copy.wait_send()
            for copy in forwards(g, 0):
                copy.wait_recv()


def exchange(slc):
    rim_in = pl.pallas_call(
        pack_kernel,
        out_shape=jax.ShapeDtypeStruct((NDATE, 2, COLS), F32),
        name="pack",
    )(slc)
    return pl.pallas_call(
        exchange_kernel,
        out_shape=(
            jax.ShapeDtypeStruct((3, NDATE, 2, ROWS, COLS), F32),
            jax.ShapeDtypeStruct((3, NDATE, 2, COLS), F32),
        ),
        in_specs=[pl.BlockSpec(memory_space=pl.ANY)] * 2,
        out_specs=(pl.BlockSpec(memory_space=pl.ANY),) * 2,
        scratch_shapes=[
            pltpu.SemaphoreType.DMA((2,)),
            pltpu.SemaphoreType.DMA((2, 4, 8)),
            pltpu.SemaphoreType.DMA((2, 4, 8)),
            pltpu.SemaphoreType.DMA((2, 2, 4)),
            pltpu.SemaphoreType.DMA((2, 2, 4)),
        ],
        compiler_params=pltpu.CompilerParams(collective_id=0, has_side_effects=True),
        name="exchange",
    )(slc, rim_in)


WIN = 16
GROUPS = 17


def split(x):
    high = x.astype(BF16).astype(F32)
    return high, x - high


def date_vectors(offs_ref, axis):
    if axis == 0:
        row = iota((8, COLS), 0)
        out = []
        for part in range(4):
            vec = jnp.zeros((8, COLS), jnp.int32)
            for s in range(8):
                vec = jnp.where(row == s, offs_ref[0, part * 8 + s] + 2, vec)
            out.append(vec)
        return out
    lane = iota((8, COLS), 1) % NDATE
    vec = jnp.zeros((8, COLS), jnp.int32)
    row_vec = jnp.zeros((8, COLS), jnp.int32)
    for s in range(NDATE):
        vec = jnp.where(lane == s, offs_ref[1, s] + 2, vec)
        row_vec = jnp.where(lane == s, offs_ref[0, s] + 2, row_vec)
    return vec, row_vec


def mix_rows(rows, steps):
    bit0, bit1, bit2 = (steps & 1) != 0, (steps & 2) != 0, steps == 4
    one = [jnp.where(bit0, rows[i + 1], rows[i]) for i in range(22)]
    two = [jnp.where(bit1, one[i + 2], one[i]) for i in range(19)]
    base = [jnp.where(bit2, rows[i + 4], two[i]) for i in range(19)]
    return [
        0.5625 * (base[i + 1] + base[i + 2]) - 0.0625 * (base[i] + base[i + 3]) for i in range(WIN)
    ]


def link_kernel(
    pos_ref,
    offs_ref,
    main_ref,
    rim_ref,
    mask_ref,
    out_ref,
    eigen_ref,
    mixed,
    tall,
    rim_tall,
    keys,
    plain,
    sums,
    slots,
    vecs,
):
    date_pos, row_pos, last_date, last_row = (pos_ref[i] for i in range(4))
    lane8 = iota((8, COLS), 1)
    sub8 = iota((8, COLS), 0)

    row_steps = date_vectors(offs_ref, 0)
    col_steps, lane_row_steps = date_vectors(offs_ref, 1)
    for part in range(2):
        for eight in range(4):
            rows = []
            for i in range(23):
                slot, row = (i + 1) // 8, (i + 1) % 8
                start = ((slot * NDATE + eight * 8) * 2 + part) * ROWS + row
                x = main_ref[pl.ds(start, 8, stride=2 * ROWS), :]
                if slot == 0:
                    x = jnp.where(row_pos > 0, x, 0.0)
                if slot == 2:
                    x = jnp.where(row_pos < last_row, x, 0.0)
                rows.append(x)
            for i, x in enumerate(mix_rows(rows, row_steps[eight])):
                mixed[i, part * NDATE + eight * 8 : part * NDATE + eight * 8 + 8, :] = x

    for slot in range(3):
        x = jnp.concatenate([rim_ref[slot, :, 0, :], rim_ref[slot, :, 1, :]], axis=0)
        if slot == 0:
            x = jnp.where(row_pos > 0, x, 0.0)
        if slot == 2:
            x = jnp.where(row_pos < last_row, x, 0.0)
        rim_tall[slot] = jnp.concatenate([x, x], axis=0).T
    for side in range(2):
        rows = []
        for i in range(23):
            slot, row = (i + 1) // 8, (i + 1) % 8
            rows.append(rim_tall[slot, 16 * row + 8 * side : 16 * row + 8 * side + 8, :])
        done = mix_rows(rows, lane_row_steps)
        for m in range(8):
            tall[m, 136 * side : 136 * side + 8, :] = jnp.where(
                lane8 < PLANES, done[2 * m], done[2 * m + 1]
            )

    for m in range(8):
        tall[m, 8:136, :] = jnp.concatenate([mixed[2 * m], mixed[2 * m + 1]], axis=0).T
    for m in range(8):
        row = 8 * row_pos - 4 + 2 * m + (lane8 >= PLANES).astype(jnp.int32)
        inside = (row >= 0) & (row < 8 * (last_row + 1))
        weights = []
        for s in range(8):
            w = jnp.zeros((8, COLS), F32)
            for tap, value in enumerate((-0.0625, 0.5625, 0.5625, -0.0625)):
                w = jnp.where(col_steps + tap == s, value, w)
            weights.append(jnp.where(inside, w, 0.0))
        for g in range(GROUPS):
            x = weights[0] * tall[m, 8 * g + 1 : 8 * g + 9, :]
            for s in range(1, 8):
                x = x + weights[s] * tall[m, 8 * g + 1 + s : 8 * g + 9 + s, :]
            if g == 0:
                x = jnp.where((sub8 >= 4) | (date_pos > 0), x, 0.0)
            if g == GROUPS - 1:
                x = jnp.where((sub8 < 4) | (date_pos < last_date), x, 0.0)
            other = pltpu.roll(x, PLANES, 1)
            a = jnp.where(lane8 < PLANES, x, other)
            b = jnp.where(lane8 < PLANES, other, x)
            z = jnp.concatenate([a, b], axis=0)
            high, low = split(z)
            lane16 = iota((16, COLS), 1)
            first = g * COLS + 16 * m
            keys[first : first + 16, :] = jnp.where(lane16 < PLANES, high, low).astype(BF16)
            plain[first : first + 16, :] = z

    k_in = iota((COLS, COLS), 0) // NDATE % 2
    k_out = iota((COLS, COLS), 1) // PLANES
    adder = jnp.where(k_in == k_out, 1.0, 0.0).astype(BF16)
    for g in range(GROUPS):
        rows = slice(g * COLS, (g + 1) * COLS)
        total = jnp.dot(keys[rows, :], adder, preferred_element_type=F32)
        high, low = split(plain[rows, :] * total)
        sums[rows, :COLS] = high.astype(BF16)
        sums[rows, COLS:] = low.astype(BF16)

    population = jnp.zeros((8, COLS), jnp.int32)
    for w in range(5):
        population = population + lax.population_count(mask_ref[w])
    population = population.astype(F32)
    zero8 = jnp.zeros((8, COLS), jnp.int32)
    for r in range(8):
        pieces = []
        for n in range(WIN):
            i = n - r
            if 0 <= i <= 8:
                nine = (mask_ref[i // 2, r : r + 1, :] >> (9 * (i % 2))) & 511
                pieces.append(jnp.broadcast_to(nine, (8, COLS)))
            else:
                pieces.append(zero8)
        slots[r] = jnp.concatenate(pieces, axis=0).T

    across = lane8 % 8 - sub8
    shift0 = jnp.where(across >= 0, across, 31)
    shift1 = jnp.where(across <= 0, across + 8, 31)
    lane64 = iota((64, COLS), 1)
    quarter = lane64 // NDATE
    outer = (quarter == 0) | (quarter == 3)
    sign_a = jnp.where(quarter % 2 == 0, 1.0, -1.0)

    def one_block(blk, carry):
        q0 = pl.multiple_of(blk * COLS, COLS)
        c0 = pl.multiple_of(blk * 8, 8)
        near = keys[pl.ds(q0, 2 * COLS), :]
        bits = []
        for r in range(8):
            w = slots[r, pl.ds(c0, 8), :]
            bits.append(jnp.concatenate([(w >> shift0) & 1, (w >> shift1) & 1], axis=1))
        mask = jnp.concatenate(bits, axis=0).astype(F32)
        u = jnp.dot(mask.astype(BF16), sums[pl.ds(q0, 2 * COLS), :], preferred_element_type=F32)
        u = u[:, :COLS] + u[:, COLS:]
        same = jnp.where(lane64 < PLANES, u, pltpu.roll(u, PLANES, 1))
        cross = jnp.where(outer, pltpu.roll(u, 32, 1), pltpu.roll(u, 96, 1))
        v = same + sign_a * cross
        turned = sign_a * pltpu.roll(v, 32, 1)
        both = jnp.concatenate([v, turned], axis=0)
        high, low = split(both)
        left = jnp.concatenate([high, low], axis=1).astype(BF16)
        right = jnp.concatenate([near, near], axis=1)
        a = lax.dot_general(
            left, right, (((1,), (1,)), ((), ())), preferred_element_type=F32
        )
        a = a * jnp.concatenate([mask, mask], axis=0)
        high, low = split(a)
        c = jnp.dot(high.astype(BF16), near, preferred_element_type=F32) + jnp.dot(
            low.astype(BF16), near, preferred_element_type=F32
        )
        c = c + pltpu.roll(c, PLANES, 1)
        v2 = c[:64] - sign_a * pltpu.roll(c[64:], 32, 1)
        both = jnp.where(lane64 < PLANES, v2, v)
        for r in range(8):
            vecs[r, pl.ds(c0, 8), :] = both[8 * r : 8 * r + 8, :]
        return carry

    lax.fori_loop(0, 16, one_block, 0, unroll=16)

    for r in range(8):
        x = vecs[r].T
        pop = population[r : r + 1, :]
        inv = 1.0 / pop
        n1 = jnp.sum(x[PLANES:] * x[PLANES:], axis=0, keepdims=True) * (inv * inv)
        inv2 = inv * inv
        x2 = x[:PLANES] * inv2
        n2 = jnp.sum(x2 * x2, axis=0, keepdims=True)
        root2 = jnp.sqrt(n2 + EPSILON)
        root1 = jnp.sqrt(n1 + EPSILON)
        eigen_ref[r : r + 1, :] = root2 / root1
        out_ref[pl.ds(r, PLANES, stride=ROWS), :] = x2 * (jnp.sqrt(F32(NDATE)) / root2)


def link(pos, offsets, main, rim, masks):
    smem = pl.BlockSpec(memory_space=pltpu.SMEM)
    vmem = pl.BlockSpec(memory_space=pltpu.VMEM)
    linked, eigen = pl.pallas_call(
        link_kernel,
        out_shape=(
            jax.ShapeDtypeStruct((PLANES * ROWS, COLS), F32),
            jax.ShapeDtypeStruct((ROWS, COLS), F32),
        ),
        in_specs=[smem, smem, vmem, vmem, vmem],
        out_specs=(vmem, vmem),
        scratch_shapes=[
            pltpu.VMEM((WIN, PLANES, COLS), F32),
            pltpu.VMEM((8, 144, COLS), F32),
            pltpu.VMEM((3, COLS, COLS), F32),
            pltpu.VMEM((GROUPS * COLS, COLS), BF16),
            pltpu.VMEM((GROUPS * COLS, COLS), F32),
            pltpu.VMEM((GROUPS * COLS, 2 * COLS), BF16),
            pltpu.VMEM((8, COLS, COLS), jnp.int32),
            pltpu.VMEM((8, COLS, COLS), F32),
        ],
        compiler_params=pltpu.CompilerParams(vmem_limit_bytes=48 * 1024 * 1024),
        name="link",
    )(pos, offsets, main.reshape(-1, COLS), rim, masks)
    return linked.reshape(2, NDATE, ROWS, COLS), eigen


def on_device(slc, offsets, masks):
    main, rim = exchange(slc[:, 0])
    pos = jnp.stack(
        [
            lax.axis_index("date"),
            lax.axis_index("row"),
            jnp.int32(lax.axis_size("date") - 1),
            jnp.int32(lax.axis_size("row") - 1),
        ]
    ).astype(jnp.int32)
    return link(pos, offsets, main, rim, masks)


def solution(mesh):
    in_specs = (P(None, "date", "row", None), P(), P(None, "row", "date"))
    out_specs = (P(None, None, "row", "date"), P("row", "date"))
    return jax.shard_map(
        on_device, mesh=mesh, in_specs=in_specs, out_specs=out_specs, check_vma=False
    )
```

```python
import jax
import jax.numpy as jnp
from jax import lax
from jax.experimental import pallas as pl
from jax.experimental.pallas import tpu as pltpu
from jax.sharding import PartitionSpec as P

NDATE = 32
COLS = 128
ROWS = 8
PLANES = 2 * NDATE
EPSILON = 1e-06
MESH = pl.DeviceIdType.MESH
F32 = jnp.float32
BF16 = jnp.bfloat16


def iota(shape, axis):
    return lax.broadcasted_iota(jnp.int32, shape, axis)


def pack_rim(slc_ref, rim_ref):
    lane = iota((ROWS, COLS), 1)
    row = iota((ROWS, COLS), 0)
    for dest in range(NDATE):
        for part in range(2):
            if dest > 0:
                left = slc_ref[part, :, (dest - 1) * COLS : dest * COLS]
            else:
                left = jnp.zeros((ROWS, COLS), F32)
            if dest < NDATE - 1:
                right = slc_ref[part, :, (dest + 1) * COLS : (dest + 2) * COLS]
            else:
                right = jnp.zeros((ROWS, COLS), F32)
            both = jnp.where(lane < 8, right, left)
            spread = pltpu.roll(both, 8, 1, stride=16, stride_axis=0)
            spread = jnp.where(lane // 16 == row, spread, 0.0)
            rim_ref[dest, part : part + 1, :] = jnp.sum(spread, axis=0, keepdims=True)


NEAR_LAST = sorted(
    ((g, j) for g in range(4) for j in range(8) if (g, j) != (0, 0)),
    key=lambda s: -(min(s[0], 4 - s[0]) + min(s[1] // 2, 4 - s[1] // 2)),
)


def peer(date, g, j):
    return (date // 8 + g) % 4 * 8 + (date % 8 + j) % 8


WIN = 16
GROUPS = 17


def split(x):
    high = x.astype(BF16).astype(F32)
    return high, x - high


def date_vectors(offs_ref, axis):
    if axis == 0:
        row = iota((8, COLS), 0)
        out = []
        for part in range(4):
            vec = jnp.zeros((8, COLS), jnp.int32)
            for s in range(8):
                vec = jnp.where(row == s, offs_ref[0, part * 8 + s] + 2, vec)
            out.append(vec)
        return out
    lane = iota((8, COLS), 1) % NDATE
    vec = jnp.zeros((8, COLS), jnp.int32)
    row_vec = jnp.zeros((8, COLS), jnp.int32)
    for s in range(NDATE):
        vec = jnp.where(lane == s, offs_ref[1, s] + 2, vec)
        row_vec = jnp.where(lane == s, offs_ref[0, s] + 2, row_vec)
    return vec, row_vec


def mix_rows(rows, steps):
    bit0, bit1, bit2 = (steps & 1) != 0, (steps & 2) != 0, steps == 4
    one = [jnp.where(bit0, rows[i + 1], rows[i]) for i in range(22)]
    two = [jnp.where(bit1, one[i + 2], one[i]) for i in range(19)]
    base = [jnp.where(bit2, rows[i + 4], two[i]) for i in range(19)]
    return [
        0.5625 * (base[i + 1] + base[i + 2]) - 0.0625 * (base[i] + base[i + 3]) for i in range(WIN)
    ]


def kernel(
    offs_ref,
    slc_ref,
    mask_ref,
    out_ref,
    eigen_ref,
    slc_here,
    rim_here,
    main_ref,
    rim_ref,
    mixed,
    tall,
    rim_tall,
    keys,
    plain,
    sums,
    slots,
    vecs,
    own_sem,
    send_sem,
    recv_sem,
    fwd_send,
    fwd_recv,
):
    date_pos, row_pos = lax.axis_index("date"), lax.axis_index("row")
    last_date, last_row = lax.axis_size("date") - 1, lax.axis_size("row") - 1
    lane8 = iota((8, COLS), 1)
    sub8 = iota((8, COLS), 0)

    load = pltpu.make_async_copy(slc_ref, slc_here, own_sem.at[2])
    load.start()
    barrier = pltpu.get_barrier_semaphore()
    for g, j in NEAR_LAST:
        pl.semaphore_signal(
            barrier, inc=1, device_id={"date": peer(date_pos, g, j)}, device_id_type=MESH
        )
    for s in (1, last_row):
        pl.semaphore_signal(
            barrier, inc=1, device_id={"row": (row_pos + s) % (last_row + 1)}, device_id_type=MESH
        )

    load.wait()
    pack_rim(slc_here, rim_here)

    population = jnp.zeros((8, COLS), jnp.int32)
    for w in range(5):
        population = population + lax.population_count(mask_ref[w])
    population = population.astype(F32)
    zero8 = jnp.zeros((8, COLS), jnp.int32)
    for r in range(8):
        pieces = []
        for n in range(WIN):
            i = n - r
            if 0 <= i <= 8:
                nine = (mask_ref[i // 2, r : r + 1, :] >> (9 * (i % 2))) & 511
                pieces.append(jnp.broadcast_to(nine, (8, COLS)))
            else:
                pieces.append(zero8)
        slots[r] = jnp.concatenate(pieces, axis=0).T

    pl.semaphore_wait(barrier, NDATE + 1)

    def part(which, date):
        return (
            (slc_ref.at[:, :, pl.ds(pl.multiple_of(date * COLS, COLS), COLS)], main_ref)
            if which == 0
            else (rim_here.at[date], rim_ref)
        )

    sends = {}
    for g, j in NEAR_LAST:
        dest = peer(date_pos, g, j)
        for which in range(2):
            src, ref = part(which, dest)
            copy = pltpu.make_async_remote_copy(
                src_ref=src,
                dst_ref=ref.at[1, date_pos],
                send_sem=send_sem.at[which, g, j],
                recv_sem=recv_sem.at[which, g, j],
                device_id={"date": dest},
                device_id_type=MESH,
            )
            copy.start()
            sends[which, g, j] = copy
    own = []
    for which in range(2):
        src, ref = part(which, date_pos)
        own.append(pltpu.make_async_copy(src, ref.at[1, date_pos], own_sem.at[which]))
    for copy in own:
        copy.start()

    def forwards(g, side):
        first = pl.multiple_of((date_pos // 8 + 4 - g) % 4 * 8, 8)
        slot, to = (2, row_pos - 1) if side == 0 else (0, row_pos + 1)
        return [
            pltpu.make_async_remote_copy(
                src_ref=ref.at[1, pl.ds(first, 8)],
                dst_ref=ref.at[slot, pl.ds(first, 8)],
                send_sem=fwd_send.at[which, side, g],
                recv_sem=fwd_recv.at[which, side, g],
                device_id={"row": to},
                device_id_type=MESH,
            )
            for which, ref in ((0, main_ref), (1, rim_ref))
        ]

    for copy in own:
        copy.wait()
    for g in (0, 1, 3, 2):
        for j in range(8):
            for which in range(2):
                if (which, g, j) in sends:
                    sends[which, g, j].wait_recv()

        @pl.when(row_pos > 0)
        def _(g=g):
            for copy in forwards(g, 0):
                copy.start()

        @pl.when(row_pos < last_row)
        def _(g=g):
            for copy in forwards(g, 1):
                copy.start()

    for copy in sends.values():
        copy.wait_send()
    for g in (0, 1, 3, 2):

        @pl.when(row_pos > 0)
        def _(g=g):
            for copy in forwards(g, 0):
                copy.wait_send()
            for copy in forwards(g, 1):
                copy.wait_recv()

        @pl.when(row_pos < last_row)
        def _(g=g):
            for copy in forwards(g, 1):
                copy.wait_send()
            for copy in forwards(g, 0):
                copy.wait_recv()

    main_rows = main_ref.reshape(-1, COLS)
    row_steps = date_vectors(offs_ref, 0)
    col_steps, lane_row_steps = date_vectors(offs_ref, 1)
    for part in range(2):
        for eight in range(4):
            rows = []
            for i in range(23):
                slot, row = (i + 1) // 8, (i + 1) % 8
                start = ((slot * NDATE + eight * 8) * 2 + part) * ROWS + row
                x = main_rows[pl.ds(start, 8, stride=2 * ROWS), :]
                if slot == 0:
                    x = jnp.where(row_pos > 0, x, 0.0)
                if slot == 2:
                    x = jnp.where(row_pos < last_row, x, 0.0)
                rows.append(x)
            for i, x in enumerate(mix_rows(rows, row_steps[eight])):
                mixed[i, part * NDATE + eight * 8 : part * NDATE + eight * 8 + 8, :] = x

    for slot in range(3):
        x = jnp.concatenate([rim_ref[slot, :, 0, :], rim_ref[slot, :, 1, :]], axis=0)
        if slot == 0:
            x = jnp.where(row_pos > 0, x, 0.0)
        if slot == 2:
            x = jnp.where(row_pos < last_row, x, 0.0)
        rim_tall[slot] = jnp.concatenate([x, x], axis=0).T
    for side in range(2):
        rows = []
        for i in range(23):
            slot, row = (i + 1) // 8, (i + 1) % 8
            rows.append(rim_tall[slot, 16 * row + 8 * side : 16 * row + 8 * side + 8, :])
        done = mix_rows(rows, lane_row_steps)
        for m in range(8):
            tall[m, 136 * side : 136 * side + 8, :] = jnp.where(
                lane8 < PLANES, done[2 * m], done[2 * m + 1]
            )

    for m in range(8):
        tall[m, 8:136, :] = jnp.concatenate([mixed[2 * m], mixed[2 * m + 1]], axis=0).T
    for m in range(8):
        row = 8 * row_pos - 4 + 2 * m + (lane8 >= PLANES).astype(jnp.int32)
        inside = (row >= 0) & (row < 8 * (last_row + 1))
        weights = []
        for s in range(8):
            w = jnp.zeros((8, COLS), F32)
            for tap, value in enumerate((-0.0625, 0.5625, 0.5625, -0.0625)):
                w = jnp.where(col_steps + tap == s, value, w)
            weights.append(jnp.where(inside, w, 0.0))
        for g in range(GROUPS):
            x = weights[0] * tall[m, 8 * g + 1 : 8 * g + 9, :]
            for s in range(1, 8):
                x = x + weights[s] * tall[m, 8 * g + 1 + s : 8 * g + 9 + s, :]
            if g == 0:
                x = jnp.where((sub8 >= 4) | (date_pos > 0), x, 0.0)
            if g == GROUPS - 1:
                x = jnp.where((sub8 < 4) | (date_pos < last_date), x, 0.0)
            other = pltpu.roll(x, PLANES, 1)
            a = jnp.where(lane8 < PLANES, x, other)
            b = jnp.where(lane8 < PLANES, other, x)
            z = jnp.concatenate([a, b], axis=0)
            high, low = split(z)
            lane16 = iota((16, COLS), 1)
            first = g * COLS + 16 * m
            keys[first : first + 16, :] = jnp.where(lane16 < PLANES, high, low).astype(BF16)
            plain[first : first + 16, :] = z

    k_in = iota((COLS, COLS), 0) // NDATE % 2
    k_out = iota((COLS, COLS), 1) // PLANES
    adder = jnp.where(k_in == k_out, 1.0, 0.0).astype(BF16)
    for g in range(GROUPS):
        rows = slice(g * COLS, (g + 1) * COLS)
        total = jnp.dot(keys[rows, :], adder, preferred_element_type=F32)
        high, low = split(plain[rows, :] * total)
        sums[rows, :COLS] = high.astype(BF16)
        sums[rows, COLS:] = low.astype(BF16)

    across = lane8 % 8 - sub8
    shift0 = jnp.where(across >= 0, across, 31)
    shift1 = jnp.where(across <= 0, across + 8, 31)
    lane64 = iota((64, COLS), 1)
    quarter = lane64 // NDATE
    outer = (quarter == 0) | (quarter == 3)
    sign_a = jnp.where(quarter % 2 == 0, 1.0, -1.0)

    def one_block(blk, carry):
        q0 = pl.multiple_of(blk * COLS, COLS)
        c0 = pl.multiple_of(blk * 8, 8)
        near = keys[pl.ds(q0, 2 * COLS), :]
        bits = []
        for r in range(8):
            w = slots[r, pl.ds(c0, 8), :]
            bits.append(jnp.concatenate([(w >> shift0) & 1, (w >> shift1) & 1], axis=1))
        mask = jnp.concatenate(bits, axis=0).astype(F32)
        u = jnp.dot(mask.astype(BF16), sums[pl.ds(q0, 2 * COLS), :], preferred_element_type=F32)
        u = u[:, :COLS] + u[:, COLS:]
        same = jnp.where(lane64 < PLANES, u, pltpu.roll(u, PLANES, 1))
        cross = jnp.where(outer, pltpu.roll(u, 32, 1), pltpu.roll(u, 96, 1))
        v = same + sign_a * cross
        turned = sign_a * pltpu.roll(v, 32, 1)
        both = jnp.concatenate([v, turned], axis=0)
        high, low = split(both)
        left = jnp.concatenate([high, low], axis=1).astype(BF16)
        right = jnp.concatenate([near, near], axis=1)
        a = lax.dot_general(
            left, right, (((1,), (1,)), ((), ())), preferred_element_type=F32
        )
        a = a * jnp.concatenate([mask, mask], axis=0)
        high, low = split(a)
        c = jnp.dot(high.astype(BF16), near, preferred_element_type=F32) + jnp.dot(
            low.astype(BF16), near, preferred_element_type=F32
        )
        c = c + pltpu.roll(c, PLANES, 1)
        v2 = c[:64] - sign_a * pltpu.roll(c[64:], 32, 1)
        both = jnp.where(lane64 < PLANES, v2, v)
        for r in range(8):
            vecs[r, pl.ds(c0, 8), :] = both[8 * r : 8 * r + 8, :]
        return carry

    lax.fori_loop(0, 16, one_block, 0, unroll=16)

    for r in range(8):
        x = vecs[r].T
        pop = population[r : r + 1, :]
        inv = 1.0 / pop
        n1 = jnp.sum(x[PLANES:] * x[PLANES:], axis=0, keepdims=True) * (inv * inv)
        inv2 = inv * inv
        x2 = x[:PLANES] * inv2
        n2 = jnp.sum(x2 * x2, axis=0, keepdims=True)
        root2 = jnp.sqrt(n2 + EPSILON)
        root1 = jnp.sqrt(n1 + EPSILON)
        eigen_ref[r : r + 1, :] = root2 / root1
        out_ref[pl.ds(r, PLANES, stride=ROWS), :] = x2 * (jnp.sqrt(F32(NDATE)) / root2)


def on_device(slc, offsets, masks):
    smem = pl.BlockSpec(memory_space=pltpu.SMEM)
    vmem = pl.BlockSpec(memory_space=pltpu.VMEM)
    linked, eigen = pl.pallas_call(
        kernel,
        out_shape=(
            jax.ShapeDtypeStruct((PLANES * ROWS, COLS), F32),
            jax.ShapeDtypeStruct((ROWS, COLS), F32),
        ),
        in_specs=[smem, pl.BlockSpec(memory_space=pl.ANY), vmem],
        out_specs=(vmem, vmem),
        scratch_shapes=[
            pltpu.VMEM((2, ROWS, NDATE * COLS), F32),
            pltpu.VMEM((NDATE, 2, COLS), F32),
            pltpu.VMEM((3, NDATE, 2, ROWS, COLS), F32),
            pltpu.VMEM((3, NDATE, 2, COLS), F32),
            pltpu.VMEM((WIN, PLANES, COLS), F32),
            pltpu.VMEM((8, 144, COLS), F32),
            pltpu.VMEM((3, COLS, COLS), F32),
            pltpu.VMEM((GROUPS * COLS, COLS), BF16),
            pltpu.VMEM((GROUPS * COLS, COLS), F32),
            pltpu.VMEM((GROUPS * COLS, 2 * COLS), BF16),
            pltpu.VMEM((8, COLS, COLS), jnp.int32),
            pltpu.VMEM((8, COLS, COLS), F32),
            pltpu.SemaphoreType.DMA((3,)),
            pltpu.SemaphoreType.DMA((2, 4, 8)),
            pltpu.SemaphoreType.DMA((2, 4, 8)),
            pltpu.SemaphoreType.DMA((2, 2, 4)),
            pltpu.SemaphoreType.DMA((2, 2, 4)),
        ],
        compiler_params=pltpu.CompilerParams(
            collective_id=0, has_side_effects=True, vmem_limit_bytes=48 * 1024 * 1024
        ),
        name="phase_linking",
    )(offsets, slc[:, 0], masks)
    return linked.reshape(2, NDATE, ROWS, COLS), eigen


def solution(mesh):
    in_specs = (P(None, "date", "row", None), P(), P(None, "row", "date"))
    out_specs = (P(None, None, "row", "date"), P("row", "date"))
    return jax.shard_map(
        on_device, mesh=mesh, in_specs=in_specs, out_specs=out_specs, check_vma=False
    )
```

```python
import jax
import jax.numpy as jnp
from jax import lax
from jax.experimental import pallas as pl
from jax.experimental.pallas import tpu as pltpu
from jax.sharding import PartitionSpec as P

NDATE = 32
COLS = 128
ROWS = 8
PLANES = 2 * NDATE
EPSILON = 1e-06
MESH = pl.DeviceIdType.MESH
F32 = jnp.float32
BF16 = jnp.bfloat16


def iota(shape, axis):
    return lax.broadcasted_iota(jnp.int32, shape, axis)


def pack_rim(slc_ref, rim_ref):
    lane = iota((ROWS, COLS), 1)
    row = iota((ROWS, COLS), 0)
    for dest in range(NDATE):
        for part in range(2):
            if dest > 0:
                left = slc_ref[part, :, (dest - 1) * COLS : dest * COLS]
            else:
                left = jnp.zeros((ROWS, COLS), F32)
            if dest < NDATE - 1:
                right = slc_ref[part, :, (dest + 1) * COLS : (dest + 2) * COLS]
            else:
                right = jnp.zeros((ROWS, COLS), F32)
            both = jnp.where(lane < 8, right, left)
            spread = pltpu.roll(both, 8, 1, stride=16, stride_axis=0)
            spread = jnp.where(lane // 16 == row, spread, 0.0)
            rim_ref[dest, part : part + 1, :] = jnp.sum(spread, axis=0, keepdims=True)


def hops(step):
    return min(step[0], 4 - step[0]) + min(step[1], 4 - step[1])


CHIPS = sorted(((g, i) for g in range(4) for i in range(4)), key=hops)
SENDS = [(g, i, k) for g, i in CHIPS for k in range(2) if (g, i, k) != (0, 0, 0)]


def peer(date, g, i, k):
    return (date // 8 + g) % 4 * 8 + (date // 2 + i) % 4 * 2 + (date + k) % 2


WIN = 16
GROUPS = 17


def split(x):
    high = x.astype(BF16).astype(F32)
    return high, x - high


def date_vectors(offs_ref, axis):
    if axis == 0:
        row = iota((8, COLS), 0)
        out = []
        for part in range(4):
            vec = jnp.zeros((8, COLS), jnp.int32)
            for s in range(8):
                vec = jnp.where(row == s, offs_ref[0, part * 8 + s] + 2, vec)
            out.append(vec)
        return out
    lane = iota((8, COLS), 1) % NDATE
    vec = jnp.zeros((8, COLS), jnp.int32)
    row_vec = jnp.zeros((8, COLS), jnp.int32)
    for s in range(NDATE):
        vec = jnp.where(lane == s, offs_ref[1, s] + 2, vec)
        row_vec = jnp.where(lane == s, offs_ref[0, s] + 2, row_vec)
    return vec, row_vec


def mix_rows(rows, steps):
    bit0, bit1, bit2 = (steps & 1) != 0, (steps & 2) != 0, steps == 4
    one = [jnp.where(bit0, rows[i + 1], rows[i]) for i in range(22)]
    two = [jnp.where(bit1, one[i + 2], one[i]) for i in range(19)]
    base = [jnp.where(bit2, rows[i + 4], two[i]) for i in range(19)]
    return [
        0.5625 * (base[i + 1] + base[i + 2]) - 0.0625 * (base[i] + base[i + 3]) for i in range(WIN)
    ]


def kernel(
    offs_in,
    slc_ref,
    mask_in,
    out_ref,
    eigen_ref,
    offs_ref,
    mask_ref,
    slc_here,
    rim_here,
    main_ref,
    rim_ref,
    mixed,
    tall,
    rim_tall,
    keys,
    plain,
    sums,
    slots,
    vecs,
    own_sem,
    send_sem,
    recv_sem,
    fwd_send,
    fwd_recv,
):
    date_pos, row_pos = lax.axis_index("date"), lax.axis_index("row")
    last_date, last_row = lax.axis_size("date") - 1, lax.axis_size("row") - 1
    lane8 = iota((8, COLS), 1)
    sub8 = iota((8, COLS), 0)

    load = pltpu.make_async_copy(slc_ref, slc_here, own_sem.at[2])
    load_mask = pltpu.make_async_copy(mask_in, mask_ref, own_sem.at[3])
    load_offs = pltpu.make_async_copy(offs_in, offs_ref, own_sem.at[4])
    load.start()
    load_mask.start()
    load_offs.start()
    barrier = pltpu.get_barrier_semaphore()
    for s in (1, last_row):
        pl.semaphore_signal(
            barrier, inc=1, device_id={"row": (row_pos + s) % (last_row + 1)}, device_id_type=MESH
        )
    for g, i, k in SENDS[::-1]:
        pl.semaphore_signal(
            barrier, inc=1, device_id={"date": peer(date_pos, g, i, k)}, device_id_type=MESH
        )

    load.wait()
    pack_rim(slc_here, rim_here)
    load_mask.wait()
    load_offs.wait()

    population = jnp.zeros((8, COLS), jnp.int32)
    for w in range(5):
        population = population + lax.population_count(mask_ref[w])
    population = population.astype(F32)
    zero8 = jnp.zeros((8, COLS), jnp.int32)
    for r in range(8):
        pieces = []
        for n in range(WIN):
            i = n - r
            if 0 <= i <= 8:
                nine = (mask_ref[i // 2, r : r + 1, :] >> (9 * (i % 2))) & 511
                pieces.append(jnp.broadcast_to(nine, (8, COLS)))
            else:
                pieces.append(zero8)
        slots[r] = jnp.concatenate(pieces, axis=0).T

    pl.semaphore_wait(barrier, NDATE + 1)

    def part(which, date):
        return (
            (slc_here.at[:, :, pl.ds(pl.multiple_of(date * COLS, COLS), COLS)], main_ref)
            if which == 0
            else (rim_here.at[date], rim_ref)
        )

    def send(which, g, i, k):
        dest = peer(date_pos, g, i, k)
        src, ref = part(which, dest)
        return pltpu.make_async_remote_copy(
            src_ref=src,
            dst_ref=ref.at[1, date_pos],
            send_sem=send_sem.at[which, g, 2 * i + k],
            recv_sem=recv_sem.at[which, g, 2 * i + k],
            device_id={"date": dest},
            device_id_type=MESH,
        )

    mains = {step: send(0, *step) for step in SENDS}
    rims = {step: send(1, *step) for step in SENDS}
    for copy in mains.values():
        copy.start()
    own = []
    for which in range(2):
        src, ref = part(which, date_pos)
        own.append(pltpu.make_async_copy(src, ref.at[1, date_pos], own_sem.at[which]))
    for copy in own:
        copy.start()
    for copy in rims.values():
        copy.start()

    def forward(side, number, first, count, ref):
        slot, to = (2, row_pos - 1) if side == 0 else (0, row_pos + 1)
        return pltpu.make_async_remote_copy(
            src_ref=ref.at[1, pl.ds(first, count)],
            dst_ref=ref.at[slot, pl.ds(first, count)],
            send_sem=fwd_send.at[side, number],
            recv_sem=fwd_recv.at[side, number],
            device_id={"row": to},
            device_id_type=MESH,
        )

    def forwards(side):
        out = []
        for number, (g, i) in enumerate(CHIPS):
            first = (date_pos // 8 + 4 - g) % 4 * 8 + (date_pos // 2 + 4 - i) % 4 * 2
            out.append(forward(side, number, first, 2, main_ref))
        return out + [forward(side, len(CHIPS), 0, NDATE, rim_ref)]

    before, after = forwards(0), forwards(1)
    for number in range(len(CHIPS) + 1):
        if number < len(CHIPS):
            g, i = CHIPS[number]
            for k in range(2):
                if (g, i, k) in mains:
                    mains[g, i, k].wait_recv()
                else:
                    own[0].wait()
        else:
            own[1].wait()
            for copy in rims.values():
                copy.wait_recv()

        @pl.when(row_pos > 0)
        def _(number=number):
            before[number].start()

        @pl.when(row_pos < last_row)
        def _(number=number):
            after[number].start()

    for step in SENDS:
        mains[step].wait_send()
        rims[step].wait_send()

    @pl.when(row_pos > 0)
    def _():
        for number in range(len(CHIPS) + 1):
            before[number].wait_send()
            after[number].wait_recv()

    @pl.when(row_pos < last_row)
    def _():
        for number in range(len(CHIPS) + 1):
            after[number].wait_send()
            before[number].wait_recv()

    main_rows = main_ref.reshape(-1, COLS)
    row_steps = date_vectors(offs_ref, 0)
    col_steps, lane_row_steps = date_vectors(offs_ref, 1)
    for part in range(2):
        for eight in range(4):
            rows = []
            for i in range(23):
                slot, row = (i + 1) // 8, (i + 1) % 8
                start = ((slot * NDATE + eight * 8) * 2 + part) * ROWS + row
                x = main_rows[pl.ds(start, 8, stride=2 * ROWS), :]
                if slot == 0:
                    x = jnp.where(row_pos > 0, x, 0.0)
                if slot == 2:
                    x = jnp.where(row_pos < last_row, x, 0.0)
                rows.append(x)
            for i, x in enumerate(mix_rows(rows, row_steps[eight])):
                mixed[i, part * NDATE + eight * 8 : part * NDATE + eight * 8 + 8, :] = x

    for slot in range(3):
        x = jnp.concatenate([rim_ref[slot, :, 0, :], rim_ref[slot, :, 1, :]], axis=0)
        if slot == 0:
            x = jnp.where(row_pos > 0, x, 0.0)
        if slot == 2:
            x = jnp.where(row_pos < last_row, x, 0.0)
        rim_tall[slot] = jnp.concatenate([x, x], axis=0).T
    for side in range(2):
        rows = []
        for i in range(23):
            slot, row = (i + 1) // 8, (i + 1) % 8
            rows.append(rim_tall[slot, 16 * row + 8 * side : 16 * row + 8 * side + 8, :])
        done = mix_rows(rows, lane_row_steps)
        for m in range(8):
            tall[m, 136 * side : 136 * side + 8, :] = jnp.where(
                lane8 < PLANES, done[2 * m], done[2 * m + 1]
            )

    for m in range(8):
        tall[m, 8:136, :] = jnp.concatenate([mixed[2 * m], mixed[2 * m + 1]], axis=0).T
    for m in range(8):
        row = 8 * row_pos - 4 + 2 * m + (lane8 >= PLANES).astype(jnp.int32)
        inside = (row >= 0) & (row < 8 * (last_row + 1))
        weights = []
        for s in range(8):
            w = jnp.zeros((8, COLS), F32)
            for tap, value in enumerate((-0.0625, 0.5625, 0.5625, -0.0625)):
                w = jnp.where(col_steps + tap == s, value, w)
            weights.append(jnp.where(inside, w, 0.0))
        for g in range(GROUPS):
            x = weights[0] * tall[m, 8 * g + 1 : 8 * g + 9, :]
            for s in range(1, 8):
                x = x + weights[s] * tall[m, 8 * g + 1 + s : 8 * g + 9 + s, :]
            if g == 0:
                x = jnp.where((sub8 >= 4) | (date_pos > 0), x, 0.0)
            if g == GROUPS - 1:
                x = jnp.where((sub8 < 4) | (date_pos < last_date), x, 0.0)
            other = pltpu.roll(x, PLANES, 1)
            a = jnp.where(lane8 < PLANES, x, other)
            b = jnp.where(lane8 < PLANES, other, x)
            z = jnp.concatenate([a, b], axis=0)
            high, low = split(z)
            lane16 = iota((16, COLS), 1)
            first = g * COLS + 16 * m
            keys[first : first + 16, :] = jnp.where(lane16 < PLANES, high, low).astype(BF16)
            plain[first : first + 16, :] = z

    k_in = iota((COLS, COLS), 0) // NDATE % 2
    k_out = iota((COLS, COLS), 1) // PLANES
    adder = jnp.where(k_in == k_out, 1.0, 0.0).astype(BF16)
    for g in range(GROUPS):
        rows = slice(g * COLS, (g + 1) * COLS)
        total = jnp.dot(keys[rows, :], adder, preferred_element_type=F32)
        high, low = split(plain[rows, :] * total)
        sums[rows, :COLS] = high.astype(BF16)
        sums[rows, COLS:] = low.astype(BF16)

    across = lane8 % 8 - sub8
    shift0 = jnp.where(across >= 0, across, 31)
    shift1 = jnp.where(across <= 0, across + 8, 31)
    lane64 = iota((64, COLS), 1)
    quarter = lane64 // NDATE
    outer = (quarter == 0) | (quarter == 3)
    sign_a = jnp.where(quarter % 2 == 0, 1.0, -1.0)

    def one_block(blk, carry):
        q0 = pl.multiple_of(blk * COLS, COLS)
        c0 = pl.multiple_of(blk * 8, 8)
        near = keys[pl.ds(q0, 2 * COLS), :]
        bits = []
        for r in range(8):
            w = slots[r, pl.ds(c0, 8), :]
            bits.append(jnp.concatenate([(w >> shift0) & 1, (w >> shift1) & 1], axis=1))
        mask = jnp.concatenate(bits, axis=0).astype(F32)
        u = jnp.dot(mask.astype(BF16), sums[pl.ds(q0, 2 * COLS), :], preferred_element_type=F32)
        u = u[:, :COLS] + u[:, COLS:]
        same = jnp.where(lane64 < PLANES, u, pltpu.roll(u, PLANES, 1))
        cross = jnp.where(outer, pltpu.roll(u, 32, 1), pltpu.roll(u, 96, 1))
        v = same + sign_a * cross
        turned = sign_a * pltpu.roll(v, 32, 1)
        both = jnp.concatenate([v, turned], axis=0)
        high, low = split(both)
        left = jnp.concatenate([high, low], axis=1).astype(BF16)
        right = jnp.concatenate([near, near], axis=1)
        a = lax.dot_general(
            left, right, (((1,), (1,)), ((), ())), preferred_element_type=F32
        )
        a = a * jnp.concatenate([mask, mask], axis=0)
        high, low = split(a)
        c = jnp.dot(high.astype(BF16), near, preferred_element_type=F32) + jnp.dot(
            low.astype(BF16), near, preferred_element_type=F32
        )
        c = c + pltpu.roll(c, PLANES, 1)
        v2 = c[:64] - sign_a * pltpu.roll(c[64:], 32, 1)
        both = jnp.where(lane64 < PLANES, v2, v)
        for r in range(8):
            vecs[r, pl.ds(c0, 8), :] = both[8 * r : 8 * r + 8, :]
        return carry

    lax.fori_loop(0, 16, one_block, 0, unroll=16)

    for r in range(8):
        x = vecs[r].T
        pop = population[r : r + 1, :]
        inv = 1.0 / pop
        n1 = jnp.sum(x[PLANES:] * x[PLANES:], axis=0, keepdims=True) * (inv * inv)
        inv2 = inv * inv
        x2 = x[:PLANES] * inv2
        n2 = jnp.sum(x2 * x2, axis=0, keepdims=True)
        root2 = jnp.sqrt(n2 + EPSILON)
        root1 = jnp.sqrt(n1 + EPSILON)
        eigen_ref[r : r + 1, :] = root2 / root1
        out_ref[pl.ds(r, PLANES, stride=ROWS), :] = x2 * (jnp.sqrt(F32(NDATE)) / root2)


def on_device(slc, offsets, masks):
    hbm = pl.BlockSpec(memory_space=pltpu.HBM)
    vmem = pl.BlockSpec(memory_space=pltpu.VMEM)
    linked, eigen = pl.pallas_call(
        kernel,
        out_shape=(
            jax.ShapeDtypeStruct((PLANES * ROWS, COLS), F32),
            jax.ShapeDtypeStruct((ROWS, COLS), F32),
        ),
        in_specs=[hbm, hbm, hbm],
        out_specs=(vmem, vmem),
        scratch_shapes=[
            pltpu.SMEM((2, NDATE), jnp.int32),
            pltpu.VMEM((5, ROWS, COLS), jnp.int32),
            pltpu.VMEM((2, ROWS, NDATE * COLS), F32),
            pltpu.VMEM((NDATE, 2, COLS), F32),
            pltpu.VMEM((3, NDATE, 2, ROWS, COLS), F32),
            pltpu.VMEM((3, NDATE, 2, COLS), F32),
            pltpu.VMEM((WIN, PLANES, COLS), F32),
            pltpu.VMEM((8, 144, COLS), F32),
            pltpu.VMEM((3, COLS, COLS), F32),
            pltpu.VMEM((GROUPS * COLS, COLS), BF16),
            pltpu.VMEM((GROUPS * COLS, COLS), F32),
            pltpu.VMEM((GROUPS * COLS, 2 * COLS), BF16),
            pltpu.VMEM((8, COLS, COLS), jnp.int32),
            pltpu.VMEM((8, COLS, COLS), F32),
            pltpu.SemaphoreType.DMA((5,)),
            pltpu.SemaphoreType.DMA((2, 4, 8)),
            pltpu.SemaphoreType.DMA((2, 4, 8)),
            pltpu.SemaphoreType.DMA((2, 17)),
            pltpu.SemaphoreType.DMA((2, 17)),
        ],
        compiler_params=pltpu.CompilerParams(
            collective_id=0, has_side_effects=True, vmem_limit_bytes=48 * 1024 * 1024
        ),
        name="phase_linking",
    )(*(pltpu.with_memory_space_constraint(x, pltpu.HBM) for x in (offsets, slc[:, 0], masks)))
    return linked.reshape(2, NDATE, ROWS, COLS), eigen


def solution(mesh):
    in_specs = (P(None, "date", "row", None), P(), P(None, "row", "date"))
    out_specs = (P(None, None, "row", "date"), P("row", "date"))
    return jax.shard_map(
        on_device, mesh=mesh, in_specs=in_specs, out_specs=out_specs, check_vma=False
    )
```

```python
import jax
import jax.numpy as jnp
from jax import lax
from jax.experimental import pallas as pl
from jax.experimental.pallas import tpu as pltpu
from jax.sharding import PartitionSpec as P

NDATE = 32
COLS = 128
ROWS = 8
PLANES = 2 * NDATE
EPSILON = 1e-06
MESH = pl.DeviceIdType.MESH
F32 = jnp.float32
BF16 = jnp.bfloat16


def iota(shape, axis):
    return lax.broadcasted_iota(jnp.int32, shape, axis)


def pack_rim(slc_ref, rim_ref):
    lane = iota((ROWS, COLS), 1)
    row = iota((ROWS, COLS), 0)
    for dest in range(NDATE):
        for part in range(2):
            if dest > 0:
                left = slc_ref[part, :, (dest - 1) * COLS : dest * COLS]
            else:
                left = jnp.zeros((ROWS, COLS), F32)
            if dest < NDATE - 1:
                right = slc_ref[part, :, (dest + 1) * COLS : (dest + 2) * COLS]
            else:
                right = jnp.zeros((ROWS, COLS), F32)
            both = jnp.where(lane < 8, right, left)
            spread = pltpu.roll(both, 8, 1, stride=16, stride_axis=0)
            spread = jnp.where(lane // 16 == row, spread, 0.0)
            rim_ref[dest, part : part + 1, :] = jnp.sum(spread, axis=0, keepdims=True)


def hops(step):
    return min(step[0], 4 - step[0]) + min(step[1], 4 - step[1])


CHIPS = sorted(((g, i) for g in range(4) for i in range(4)), key=hops)
SENDS = [(g, i, k) for g, i in CHIPS for k in range(2) if (g, i, k) != (0, 0, 0)]


def peer(date, g, i, k):
    return (date // 8 + g) % 4 * 8 + (date // 2 + i) % 4 * 2 + (date + k) % 2


WIN = 16
GROUPS = 17


def split(x):
    high = x.astype(BF16).astype(F32)
    return high, x - high


def date_vectors(offs_ref, axis):
    if axis == 0:
        row = iota((8, COLS), 0)
        out = []
        for part in range(4):
            vec = jnp.zeros((8, COLS), jnp.int32)
            for s in range(8):
                vec = jnp.where(row == s, offs_ref[0, part * 8 + s] + 2, vec)
            out.append(vec)
        return out
    lane = iota((8, COLS), 1) % NDATE
    vec = jnp.zeros((8, COLS), jnp.int32)
    row_vec = jnp.zeros((8, COLS), jnp.int32)
    for s in range(NDATE):
        vec = jnp.where(lane == s, offs_ref[1, s] + 2, vec)
        row_vec = jnp.where(lane == s, offs_ref[0, s] + 2, row_vec)
    return vec, row_vec


def mix_rows(rows, steps):
    bit0, bit1, bit2 = (steps & 1) != 0, (steps & 2) != 0, steps == 4
    one = [jnp.where(bit0, rows[i + 1], rows[i]) for i in range(22)]
    two = [jnp.where(bit1, one[i + 2], one[i]) for i in range(19)]
    base = [jnp.where(bit2, rows[i + 4], two[i]) for i in range(19)]
    return [
        0.5625 * (base[i + 1] + base[i + 2]) - 0.0625 * (base[i] + base[i + 3]) for i in range(WIN)
    ]


def kernel(
    offs_in,
    slc_ref,
    mask_in,
    out_ref,
    eigen_ref,
    offs_ref,
    mask_ref,
    slc_here,
    rim_here,
    main_ref,
    rim_ref,
    mixed,
    tall,
    rim_tall,
    keys,
    plain,
    sums,
    slots,
    vecs,
    own_sem,
    send_sem,
    recv_sem,
    fwd_send,
    fwd_recv,
):
    date_pos, row_pos = lax.axis_index("date"), lax.axis_index("row")
    last_date, last_row = lax.axis_size("date") - 1, lax.axis_size("row") - 1
    lane8 = iota((8, COLS), 1)
    sub8 = iota((8, COLS), 0)

    load = pltpu.make_async_copy(slc_ref, slc_here, own_sem.at[2])
    load_mask = pltpu.make_async_copy(mask_in, mask_ref, own_sem.at[3])
    load_offs = pltpu.make_async_copy(offs_in, offs_ref, own_sem.at[4])
    load.start()
    load_mask.start()
    load_offs.start()
    barrier = pltpu.get_barrier_semaphore()
    for s in (1, last_row):
        pl.semaphore_signal(
            barrier, inc=1, device_id={"row": (row_pos + s) % (last_row + 1)}, device_id_type=MESH
        )
    for g, i, k in SENDS[::-1]:
        pl.semaphore_signal(
            barrier, inc=1, device_id={"date": peer(date_pos, g, i, k)}, device_id_type=MESH
        )

    load.wait()
    pack_rim(slc_here, rim_here)
    load_mask.wait()
    load_offs.wait()

    population = jnp.zeros((8, COLS), jnp.int32)
    for w in range(5):
        population = population + lax.population_count(mask_ref[w])
    population = population.astype(F32)
    zero8 = jnp.zeros((8, COLS), jnp.int32)
    for r in range(8):
        pieces = []
        for n in range(WIN):
            i = n - r
            if 0 <= i <= 8:
                nine = (mask_ref[i // 2, r : r + 1, :] >> (9 * (i % 2))) & 511
                pieces.append(jnp.broadcast_to(nine, (8, COLS)))
            else:
                pieces.append(zero8)
        slots[r] = jnp.concatenate(pieces, axis=0).T

    pl.semaphore_wait(barrier, NDATE + 1)

    def part(which, date):
        return (
            (slc_here.at[:, :, pl.ds(pl.multiple_of(date * COLS, COLS), COLS)], main_ref)
            if which == 0
            else (rim_here.at[date], rim_ref)
        )

    def send(which, g, i, k):
        dest = peer(date_pos, g, i, k)
        src, ref = part(which, dest)
        return pltpu.make_async_remote_copy(
            src_ref=src,
            dst_ref=ref.at[1, date_pos],
            send_sem=send_sem.at[which, g, 2 * i + k],
            recv_sem=recv_sem.at[which, g, 2 * i + k],
            device_id={"date": dest},
            device_id_type=MESH,
        )

    mains = {step: send(0, *step) for step in SENDS}
    rims = {step: send(1, *step) for step in SENDS}
    for copy in mains.values():
        copy.start()
    own = []
    for which in range(2):
        src, ref = part(which, date_pos)
        own.append(pltpu.make_async_copy(src, ref.at[1, date_pos], own_sem.at[which]))
    for copy in own:
        copy.start()
    for copy in rims.values():
        copy.start()

    def forward(side, number, first, count, ref):
        slot, to = (2, row_pos - 1) if side == 0 else (0, row_pos + 1)
        return pltpu.make_async_remote_copy(
            src_ref=ref.at[1, pl.ds(first, count)],
            dst_ref=ref.at[slot, pl.ds(first, count)],
            send_sem=fwd_send.at[side, number],
            recv_sem=fwd_recv.at[side, number],
            device_id={"row": to},
            device_id_type=MESH,
        )

    def forwards(side):
        out = []
        for number, (g, i) in enumerate(CHIPS):
            first = (date_pos // 8 + 4 - g) % 4 * 8 + (date_pos // 2 + 4 - i) % 4 * 2
            out.append(forward(side, number, first, 2, main_ref))
        return out + [forward(side, len(CHIPS), 0, NDATE, rim_ref)]

    before, after = forwards(0), forwards(1)
    for number in range(len(CHIPS) + 1):
        if number < len(CHIPS):
            g, i = CHIPS[number]
            for k in range(2):
                if (g, i, k) in mains:
                    mains[g, i, k].wait_recv()
                else:
                    own[0].wait()
        else:
            own[1].wait()
            for copy in rims.values():
                copy.wait_recv()

        @pl.when(row_pos > 0)
        def _(number=number):
            before[number].start()

        @pl.when(row_pos < last_row)
        def _(number=number):
            after[number].start()

    for step in SENDS:
        mains[step].wait_send()
        rims[step].wait_send()

    @pl.when(row_pos > 0)
    def _():
        for number in range(len(CHIPS) + 1):
            before[number].wait_send()
            after[number].wait_recv()

    @pl.when(row_pos < last_row)
    def _():
        for number in range(len(CHIPS) + 1):
            after[number].wait_send()
            before[number].wait_recv()

    main_rows = main_ref.reshape(-1, COLS)
    row_steps = date_vectors(offs_ref, 0)
    col_steps, lane_row_steps = date_vectors(offs_ref, 1)
    for part in range(2):
        for eight in range(4):
            rows = []
            for i in range(23):
                slot, row = (i + 1) // 8, (i + 1) % 8
                start = ((slot * NDATE + eight * 8) * 2 + part) * ROWS + row
                x = main_rows[pl.ds(start, 8, stride=2 * ROWS), :]
                if slot == 0:
                    x = jnp.where(row_pos > 0, x, 0.0)
                if slot == 2:
                    x = jnp.where(row_pos < last_row, x, 0.0)
                rows.append(x)
            for i, x in enumerate(mix_rows(rows, row_steps[eight])):
                mixed[i, part * NDATE + eight * 8 : part * NDATE + eight * 8 + 8, :] = x

    for slot in range(3):
        x = jnp.concatenate([rim_ref[slot, :, 0, :], rim_ref[slot, :, 1, :]], axis=0)
        if slot == 0:
            x = jnp.where(row_pos > 0, x, 0.0)
        if slot == 2:
            x = jnp.where(row_pos < last_row, x, 0.0)
        rim_tall[slot] = jnp.concatenate([x, x], axis=0).T
    for side in range(2):
        rows = []
        for i in range(23):
            slot, row = (i + 1) // 8, (i + 1) % 8
            rows.append(rim_tall[slot, 16 * row + 8 * side : 16 * row + 8 * side + 8, :])
        done = mix_rows(rows, lane_row_steps)
        for m in range(8):
            tall[m, 136 * side : 136 * side + 8, :] = jnp.where(
                lane8 < PLANES, done[2 * m], done[2 * m + 1]
            )

    for m in range(8):
        tall[m, 8:136, :] = jnp.concatenate([mixed[2 * m], mixed[2 * m + 1]], axis=0).T
    for m in range(8):
        row = 8 * row_pos - 4 + 2 * m + (lane8 >= PLANES).astype(jnp.int32)
        inside = (row >= 0) & (row < 8 * (last_row + 1))
        weights = []
        for s in range(8):
            w = jnp.zeros((8, COLS), F32)
            for tap, value in enumerate((-0.0625, 0.5625, 0.5625, -0.0625)):
                w = jnp.where(col_steps + tap == s, value, w)
            weights.append(jnp.where(inside, w, 0.0))
        for g in range(GROUPS):
            x = weights[0] * tall[m, 8 * g + 1 : 8 * g + 9, :]
            for s in range(1, 8):
                x = x + weights[s] * tall[m, 8 * g + 1 + s : 8 * g + 9 + s, :]
            if g == 0:
                x = jnp.where((sub8 >= 4) | (date_pos > 0), x, 0.0)
            if g == GROUPS - 1:
                x = jnp.where((sub8 < 4) | (date_pos < last_date), x, 0.0)
            other = pltpu.roll(x, PLANES, 1)
            a = jnp.where(lane8 < PLANES, x, other)
            b = jnp.where(lane8 < PLANES, other, x)
            z = jnp.concatenate([a, b], axis=0)
            high, low = split(z)
            lane16 = iota((16, COLS), 1)
            first = g * COLS + 16 * m
            keys[first : first + 16, :] = jnp.where(lane16 < PLANES, high, low).astype(BF16)
            plain[first : first + 16, :] = z

    k_in = iota((COLS, COLS), 0) // NDATE % 2
    k_out = iota((COLS, COLS), 1) // PLANES
    adder = jnp.where(k_in == k_out, 1.0, 0.0).astype(BF16)
    for g in range(GROUPS):
        rows = slice(g * COLS, (g + 1) * COLS)
        total = jnp.dot(keys[rows, :], adder, preferred_element_type=F32)
        high, low = split(plain[rows, :] * total)
        sums[rows, :COLS] = high.astype(BF16)
        sums[rows, COLS:] = low.astype(BF16)

    across = lane8 % 8 - sub8
    shift0 = jnp.where(across >= 0, across, 31)
    shift1 = jnp.where(across <= 0, across + 8, 31)
    lane64 = iota((64, COLS), 1)
    quarter = lane64 // NDATE
    outer = (quarter == 0) | (quarter == 3)
    sign_a = jnp.where(quarter % 2 == 0, 1.0, -1.0)

    def first(blk):
        q0 = blk * COLS
        bits = []
        for r in range(8):
            w = slots[r, blk * 8 : blk * 8 + 8, :]
            bits.append(jnp.concatenate([(w >> shift0) & 1, (w >> shift1) & 1], axis=1))
        mask = jnp.concatenate(bits, axis=0).astype(F32)
        u = jnp.dot(mask.astype(BF16), sums[q0 : q0 + 2 * COLS, :], preferred_element_type=F32)
        return mask, u

    def second(blk, u):
        q0 = blk * COLS
        near = keys[q0 : q0 + 2 * COLS, :]
        u = u[:, :COLS] + u[:, COLS:]
        same = jnp.where(lane64 < PLANES, u, pltpu.roll(u, PLANES, 1))
        cross = jnp.where(outer, pltpu.roll(u, 32, 1), pltpu.roll(u, 96, 1))
        v = same + sign_a * cross
        turned = sign_a * pltpu.roll(v, 32, 1)
        both = jnp.concatenate([v, turned], axis=0)
        high, low = split(both)
        left = jnp.concatenate([high, low], axis=1).astype(BF16)
        right = jnp.concatenate([near, near], axis=1)
        a = lax.dot_general(
            left, right, (((1,), (1,)), ((), ())), preferred_element_type=F32
        )
        return v, a

    def third(blk, mask, a):
        q0 = blk * COLS
        near = keys[q0 : q0 + 2 * COLS, :]
        a = a * jnp.concatenate([mask, mask], axis=0)
        high, low = split(a)
        both = jnp.concatenate([high.astype(BF16), low.astype(BF16)], axis=0)
        return jnp.dot(both, near, preferred_element_type=F32)

    def fourth(blk, v, c):
        c = c[:128] + c[128:]
        c = c + pltpu.roll(c, PLANES, 1)
        v2 = c[:64] - sign_a * pltpu.roll(c[64:], 32, 1)
        both = jnp.where(lane64 < PLANES, v2, v)
        for r in range(8):
            vecs[r, blk * 8 : blk * 8 + 8, :] = both[8 * r : 8 * r + 8, :]

    blocks = range(16)
    ones = [first(b) for b in blocks]
    twos = [second(b, ones[b][1]) for b in blocks]
    threes = [third(b, ones[b][0], twos[b][1]) for b in blocks]
    for b in blocks:
        fourth(b, twos[b][0], threes[b])

    for r in range(8):
        x = vecs[r].T
        pop = population[r : r + 1, :]
        inv = 1.0 / pop
        n1 = jnp.sum(x[PLANES:] * x[PLANES:], axis=0, keepdims=True) * (inv * inv)
        inv2 = inv * inv
        x2 = x[:PLANES] * inv2
        n2 = jnp.sum(x2 * x2, axis=0, keepdims=True)
        root2 = jnp.sqrt(n2 + EPSILON)
        root1 = jnp.sqrt(n1 + EPSILON)
        eigen_ref[r : r + 1, :] = root2 / root1
        out_ref[pl.ds(r, PLANES, stride=ROWS), :] = x2 * (jnp.sqrt(F32(NDATE)) / root2)


def on_device(slc, offsets, masks):
    hbm = pl.BlockSpec(memory_space=pltpu.HBM)
    vmem = pl.BlockSpec(memory_space=pltpu.VMEM)
    linked, eigen = pl.pallas_call(
        kernel,
        out_shape=(
            jax.ShapeDtypeStruct((PLANES * ROWS, COLS), F32),
            jax.ShapeDtypeStruct((ROWS, COLS), F32),
        ),
        in_specs=[hbm, hbm, hbm],
        out_specs=(vmem, vmem),
        scratch_shapes=[
            pltpu.SMEM((2, NDATE), jnp.int32),
            pltpu.VMEM((5, ROWS, COLS), jnp.int32),
            pltpu.VMEM((2, ROWS, NDATE * COLS), F32),
            pltpu.VMEM((NDATE, 2, COLS), F32),
            pltpu.VMEM((3, NDATE, 2, ROWS, COLS), F32),
            pltpu.VMEM((3, NDATE, 2, COLS), F32),
            pltpu.VMEM((WIN, PLANES, COLS), F32),
            pltpu.VMEM((8, 144, COLS), F32),
            pltpu.VMEM((3, COLS, COLS), F32),
            pltpu.VMEM((GROUPS * COLS, COLS), BF16),
            pltpu.VMEM((GROUPS * COLS, COLS), F32),
            pltpu.VMEM((GROUPS * COLS, 2 * COLS), BF16),
            pltpu.VMEM((8, COLS, COLS), jnp.int32),
            pltpu.VMEM((8, COLS, COLS), F32),
            pltpu.SemaphoreType.DMA((5,)),
            pltpu.SemaphoreType.DMA((2, 4, 8)),
            pltpu.SemaphoreType.DMA((2, 4, 8)),
            pltpu.SemaphoreType.DMA((2, 17)),
            pltpu.SemaphoreType.DMA((2, 17)),
        ],
        compiler_params=pltpu.CompilerParams(
            collective_id=0, has_side_effects=True, vmem_limit_bytes=48 * 1024 * 1024
        ),
        name="phase_linking",
    )(*(pltpu.with_memory_space_constraint(x, pltpu.HBM) for x in (offsets, slc[:, 0], masks)))
    return linked.reshape(2, NDATE, ROWS, COLS), eigen


def solution(mesh):
    in_specs = (P(None, "date", "row", None), P(), P(None, "row", "date"))
    out_specs = (P(None, None, "row", "date"), P("row", "date"))
    return jax.shard_map(
        on_device, mesh=mesh, in_specs=in_specs, out_specs=out_specs, check_vma=False
    )
```

```python
import jax
import jax.numpy as jnp
from jax import lax
from jax.experimental import pallas as pl
from jax.experimental.pallas import tpu as pltpu
from jax.sharding import PartitionSpec as P

NDATE = 32
COLS = 128
ROWS = 8
PLANES = 2 * NDATE
EPSILON = 1e-06
MESH = pl.DeviceIdType.MESH
F32 = jnp.float32
BF16 = jnp.bfloat16


def iota(shape, axis):
    return lax.broadcasted_iota(jnp.int32, shape, axis)


def pack_rim(slc_ref, rim_ref):
    lane = iota((ROWS, COLS), 1)
    row = iota((ROWS, COLS), 0)
    for dest in range(NDATE):
        for part in range(2):
            if dest > 0:
                left = slc_ref[part, :, (dest - 1) * COLS : dest * COLS]
            else:
                left = jnp.zeros((ROWS, COLS), F32)
            if dest < NDATE - 1:
                right = slc_ref[part, :, (dest + 1) * COLS : (dest + 2) * COLS]
            else:
                right = jnp.zeros((ROWS, COLS), F32)
            both = jnp.where(lane < 8, right, left)
            spread = pltpu.roll(both, 8, 1, stride=16, stride_axis=0)
            spread = jnp.where(lane // 16 == row, spread, 0.0)
            rim_ref[dest, part : part + 1, :] = jnp.sum(spread, axis=0, keepdims=True)


def hops(step):
    return min(step[0], 4 - step[0]) + min(step[1], 4 - step[1])


CHIPS = sorted(((g, i) for g in range(4) for i in range(4)), key=hops)
FAR = CHIPS[11:]
NEAR = CHIPS[:11]
SENDS = [(g, i, k) for g, i in CHIPS for k in range(2) if (g, i, k) != (0, 0, 0)]


def peer(date, g, i, k):
    return (date // 8 + g) % 4 * 8 + (date // 2 + i) % 4 * 2 + (date + k) % 2


WIN = 16
GROUPS = 17


def split(x):
    high = x.astype(BF16).astype(F32)
    return high, x - high


def date_vectors(offs_ref, axis):
    if axis == 0:
        row = iota((8, COLS), 0)
        out = []
        for part in range(4):
            vec = jnp.zeros((8, COLS), jnp.int32)
            for s in range(8):
                vec = jnp.where(row == s, offs_ref[0, part * 8 + s] + 2, vec)
            out.append(vec)
        return out
    lane = iota((8, COLS), 1) % NDATE
    vec = jnp.zeros((8, COLS), jnp.int32)
    row_vec = jnp.zeros((8, COLS), jnp.int32)
    for s in range(NDATE):
        vec = jnp.where(lane == s, offs_ref[1, s] + 2, vec)
        row_vec = jnp.where(lane == s, offs_ref[0, s] + 2, row_vec)
    return vec, row_vec


def mix_rows(rows, steps):
    bit0, bit1, bit2 = (steps & 1) != 0, (steps & 2) != 0, steps == 4
    one = [jnp.where(bit0, rows[i + 1], rows[i]) for i in range(22)]
    two = [jnp.where(bit1, one[i + 2], one[i]) for i in range(19)]
    base = [jnp.where(bit2, rows[i + 4], two[i]) for i in range(19)]
    return [
        0.5625 * (base[i + 1] + base[i + 2]) - 0.0625 * (base[i] + base[i + 3]) for i in range(WIN)
    ]


def kernel(
    offs_in,
    slc_ref,
    mask_in,
    out_ref,
    eigen_ref,
    offs_ref,
    mask_ref,
    slc_here,
    rim_here,
    main_ref,
    rim_ref,
    slab,
    mixed,
    tall,
    rim_tall,
    keys,
    plain,
    sums,
    slots,
    vecs,
    own_sem,
    send_sem,
    recv_sem,
    fwd_send,
    fwd_recv,
    hop_send,
    hop_recv,
    far_send,
    far_recv,
):
    date_pos, row_pos = lax.axis_index("date"), lax.axis_index("row")
    last_date, last_row = lax.axis_size("date") - 1, lax.axis_size("row") - 1
    lane8 = iota((8, COLS), 1)
    sub8 = iota((8, COLS), 0)

    load = pltpu.make_async_copy(slc_ref, slc_here, own_sem.at[2])
    load_mask = pltpu.make_async_copy(mask_in, mask_ref, own_sem.at[3])
    load_offs = pltpu.make_async_copy(offs_in, offs_ref, own_sem.at[4])
    load.start()
    load_mask.start()
    load_offs.start()
    barrier = pltpu.get_barrier_semaphore()
    for s in (1, last_row):
        pl.semaphore_signal(
            barrier, inc=1, device_id={"row": (row_pos + s) % (last_row + 1)}, device_id_type=MESH
        )
    for g, i, k in SENDS[::-1]:
        pl.semaphore_signal(
            barrier, inc=1, device_id={"date": peer(date_pos, g, i, k)}, device_id_type=MESH
        )

    load.wait()
    pl.semaphore_wait(barrier, NDATE + 1)

    def part(which, date):
        return (
            (slc_here.at[:, :, pl.ds(pl.multiple_of(date * COLS, COLS), COLS)], main_ref)
            if which == 0
            else (rim_here.at[date], rim_ref)
        )

    def send(which, g, i, k):
        dest = peer(date_pos, g, i, k)
        src, ref = part(which, dest)
        return pltpu.make_async_remote_copy(
            src_ref=src,
            dst_ref=ref.at[1, date_pos],
            send_sem=send_sem.at[which, g, 2 * i + k],
            recv_sem=recv_sem.at[which, g, 2 * i + k],
            device_id={"date": dest},
            device_id_type=MESH,
        )

    def sends_to(side):
        return row_pos > 0 if side == 0 else row_pos < last_row

    def gets_from(side):
        return row_pos < last_row if side == 0 else row_pos > 0

    def hop(side, n):
        g, i = FAR[n]
        chip = (date_pos // 8 + g) % 4 * 4 + (date_pos // 2 + i) % 4
        cols = pl.ds(pl.multiple_of(chip * 2 * COLS, 2 * COLS), 2 * COLS)
        return pltpu.make_async_remote_copy(
            src_ref=slc_here.at[:, :, cols],
            dst_ref=slab.at[side, :, :, cols],
            send_sem=hop_send.at[side, n],
            recv_sem=hop_recv.at[side, n],
            device_id={"row": row_pos - 1 if side == 0 else row_pos + 1},
            device_id_type=MESH,
        )

    def far(side, n, k):
        dest = peer(date_pos, *FAR[n], k)
        return pltpu.make_async_remote_copy(
            src_ref=slab.at[side, :, :, pl.ds(pl.multiple_of(dest * COLS, COLS), COLS)],
            dst_ref=main_ref.at[2 - 2 * side, date_pos],
            send_sem=far_send.at[side, n, k],
            recv_sem=far_recv.at[side, n, k],
            device_id={"date": dest},
            device_id_type=MESH,
        )

    hops_out = [[hop(side, n) for n in range(len(FAR))] for side in range(2)]
    fars = [[far(side, n, k) for n in range(len(FAR)) for k in range(2)] for side in range(2)]
    for side in range(2):

        @pl.when(sends_to(side))
        def _(side=side):
            for copy in hops_out[side]:
                copy.start()

    mains = {step: send(0, *step) for step in SENDS}
    rims = {step: send(1, *step) for step in SENDS}
    for copy in mains.values():
        copy.start()
    pack_rim(slc_here, rim_here)
    own = []
    for which in range(2):
        src, ref = part(which, date_pos)
        own.append(pltpu.make_async_copy(src, ref.at[1, date_pos], own_sem.at[which]))
    for copy in own:
        copy.start()
    for copy in rims.values():
        copy.start()

    load_mask.wait()
    load_offs.wait()
    population = jnp.zeros((8, COLS), jnp.int32)
    for w in range(5):
        population = population + lax.population_count(mask_ref[w])
    population = population.astype(F32)
    zero8 = jnp.zeros((8, COLS), jnp.int32)
    for r in range(8):
        pieces = []
        for n in range(WIN):
            i = n - r
            if 0 <= i <= 8:
                nine = (mask_ref[i // 2, r : r + 1, :] >> (9 * (i % 2))) & 511
                pieces.append(jnp.broadcast_to(nine, (8, COLS)))
            else:
                pieces.append(zero8)
        slots[r] = jnp.concatenate(pieces, axis=0).T


    def forward(side, number, first, count, ref):
        slot, to = (2, row_pos - 1) if side == 0 else (0, row_pos + 1)
        return pltpu.make_async_remote_copy(
            src_ref=ref.at[1, pl.ds(first, count)],
            dst_ref=ref.at[slot, pl.ds(first, count)],
            send_sem=fwd_send.at[side, number],
            recv_sem=fwd_recv.at[side, number],
            device_id={"row": to},
            device_id_type=MESH,
        )

    def forwards(side):
        out = []
        for number, (g, i) in enumerate(NEAR):
            first = (date_pos // 8 + 4 - g) % 4 * 8 + (date_pos // 2 + 4 - i) % 4 * 2
            out.append(forward(side, number, first, 2, main_ref))
        return out + [forward(side, len(NEAR), 0, NDATE, rim_ref)]

    before, after = forwards(0), forwards(1)
    for number in range(len(NEAR) + 1):
        if number < len(NEAR):
            g, i = NEAR[number]
            for k in range(2):
                if (g, i, k) in mains:
                    mains[g, i, k].wait_recv()
                else:
                    own[0].wait()
        else:
            own[1].wait()
            for copy in rims.values():
                copy.wait_recv()

        @pl.when(row_pos > 0)
        def _(number=number):
            before[number].start()

        @pl.when(row_pos < last_row)
        def _(number=number):
            after[number].start()

        if number < len(FAR):
            for side in range(2):

                @pl.when(gets_from(side))
                def _(side=side, number=number):
                    hops_out[side][number].wait_recv()
                    fars[side][2 * number].start()
                    fars[side][2 * number + 1].start()

    for g, i in FAR:
        for k in range(2):
            mains[g, i, k].wait_recv()
    for side in range(2):

        @pl.when(sends_to(side))
        def _(side=side):
            for copy in hops_out[side]:
                copy.wait_send()

        @pl.when(gets_from(side))
        def _(side=side):
            for copy in fars[side]:
                copy.wait()

    for step in SENDS:
        mains[step].wait_send()
        rims[step].wait_send()

    @pl.when(row_pos > 0)
    def _():
        for number in range(len(NEAR) + 1):
            before[number].wait_send()
            after[number].wait_recv()

    @pl.when(row_pos < last_row)
    def _():
        for number in range(len(NEAR) + 1):
            after[number].wait_send()
            before[number].wait_recv()

    main_rows = main_ref.reshape(-1, COLS)
    row_steps = date_vectors(offs_ref, 0)
    col_steps, lane_row_steps = date_vectors(offs_ref, 1)
    for part in range(2):
        for eight in range(4):
            rows = []
            for i in range(23):
                slot, row = (i + 1) // 8, (i + 1) % 8
                start = ((slot * NDATE + eight * 8) * 2 + part) * ROWS + row
                x = main_rows[pl.ds(start, 8, stride=2 * ROWS), :]
                if slot == 0:
                    x = jnp.where(row_pos > 0, x, 0.0)
                if slot == 2:
                    x = jnp.where(row_pos < last_row, x, 0.0)
                rows.append(x)
            for i, x in enumerate(mix_rows(rows, row_steps[eight])):
                mixed[i, part * NDATE + eight * 8 : part * NDATE + eight * 8 + 8, :] = x

    for slot in range(3):
        x = jnp.concatenate([rim_ref[slot, :, 0, :], rim_ref[slot, :, 1, :]], axis=0)
        if slot == 0:
            x = jnp.where(row_pos > 0, x, 0.0)
        if slot == 2:
            x = jnp.where(row_pos < last_row, x, 0.0)
        rim_tall[slot] = jnp.concatenate([x, x], axis=0).T
    for side in range(2):
        rows = []
        for i in range(23):
            slot, row = (i + 1) // 8, (i + 1) % 8
            rows.append(rim_tall[slot, 16 * row + 8 * side : 16 * row + 8 * side + 8, :])
        done = mix_rows(rows, lane_row_steps)
        for m in range(8):
            tall[m, 136 * side : 136 * side + 8, :] = jnp.where(
                lane8 < PLANES, done[2 * m], done[2 * m + 1]
            )

    for m in range(8):
        tall[m, 8:136, :] = jnp.concatenate([mixed[2 * m], mixed[2 * m + 1]], axis=0).T
    for m in range(8):
        row = 8 * row_pos - 4 + 2 * m + (lane8 >= PLANES).astype(jnp.int32)
        inside = (row >= 0) & (row < 8 * (last_row + 1))
        weights = []
        for s in range(8):
            w = jnp.zeros((8, COLS), F32)
            for tap, value in enumerate((-0.0625, 0.5625, 0.5625, -0.0625)):
                w = jnp.where(col_steps + tap == s, value, w)
            weights.append(jnp.where(inside, w, 0.0))
        for g in range(GROUPS):
            x = weights[0] * tall[m, 8 * g + 1 : 8 * g + 9, :]
            for s in range(1, 8):
                x = x + weights[s] * tall[m, 8 * g + 1 + s : 8 * g + 9 + s, :]
            if g == 0:
                x = jnp.where((sub8 >= 4) | (date_pos > 0), x, 0.0)
            if g == GROUPS - 1:
                x = jnp.where((sub8 < 4) | (date_pos < last_date), x, 0.0)
            other = pltpu.roll(x, PLANES, 1)
            a = jnp.where(lane8 < PLANES, x, other)
            b = jnp.where(lane8 < PLANES, other, x)
            z = jnp.concatenate([a, b], axis=0)
            high, low = split(z)
            lane16 = iota((16, COLS), 1)
            first = g * COLS + 16 * m
            keys[first : first + 16, :] = jnp.where(lane16 < PLANES, high, low).astype(BF16)
            plain[first : first + 16, :] = z

    k_in = iota((COLS, COLS), 0) // NDATE % 2
    k_out = iota((COLS, COLS), 1) // PLANES
    adder = jnp.where(k_in == k_out, 1.0, 0.0).astype(BF16)
    for g in range(GROUPS):
        rows = slice(g * COLS, (g + 1) * COLS)
        total = jnp.dot(keys[rows, :], adder, preferred_element_type=F32)
        high, low = split(plain[rows, :] * total)
        sums[rows, :COLS] = high.astype(BF16)
        sums[rows, COLS:] = low.astype(BF16)

    across = lane8 % 8 - sub8
    shift0 = jnp.where(across >= 0, across, 31)
    shift1 = jnp.where(across <= 0, across + 8, 31)
    lane64 = iota((64, COLS), 1)
    quarter = lane64 // NDATE
    outer = (quarter == 0) | (quarter == 3)
    sign_a = jnp.where(quarter % 2 == 0, 1.0, -1.0)

    def first(blk):
        q0 = blk * COLS
        bits = []
        for r in range(8):
            w = slots[r, blk * 8 : blk * 8 + 8, :]
            bits.append(jnp.concatenate([(w >> shift0) & 1, (w >> shift1) & 1], axis=1))
        mask = jnp.concatenate(bits, axis=0).astype(F32)
        u = jnp.dot(mask.astype(BF16), sums[q0 : q0 + 2 * COLS, :], preferred_element_type=F32)
        return mask, u

    def second(blk, u):
        q0 = blk * COLS
        near = keys[q0 : q0 + 2 * COLS, :]
        u = u[:, :COLS] + u[:, COLS:]
        same = jnp.where(lane64 < PLANES, u, pltpu.roll(u, PLANES, 1))
        cross = jnp.where(outer, pltpu.roll(u, 32, 1), pltpu.roll(u, 96, 1))
        v = same + sign_a * cross
        turned = sign_a * pltpu.roll(v, 32, 1)
        both = jnp.concatenate([v, turned], axis=0)
        high, low = split(both)
        left = jnp.concatenate([high, low], axis=1).astype(BF16)
        right = jnp.concatenate([near, near], axis=1)
        a = lax.dot_general(
            left, right, (((1,), (1,)), ((), ())), preferred_element_type=F32
        )
        return v, a

    def third(blk, mask, a):
        q0 = blk * COLS
        near = keys[q0 : q0 + 2 * COLS, :]
        a = a * jnp.concatenate([mask, mask], axis=0)
        high, low = split(a)
        both = jnp.concatenate([high.astype(BF16), low.astype(BF16)], axis=0)
        return jnp.dot(both, near, preferred_element_type=F32)

    def fourth(blk, v, c):
        c = c[:128] + c[128:]
        c = c + pltpu.roll(c, PLANES, 1)
        v2 = c[:64] - sign_a * pltpu.roll(c[64:], 32, 1)
        both = jnp.where(lane64 < PLANES, v2, v)
        for r in range(8):
            vecs[r, blk * 8 : blk * 8 + 8, :] = both[8 * r : 8 * r + 8, :]

    blocks = range(16)
    ones = [first(b) for b in blocks]
    twos = [second(b, ones[b][1]) for b in blocks]
    threes = [third(b, ones[b][0], twos[b][1]) for b in blocks]
    for b in blocks:
        fourth(b, twos[b][0], threes[b])

    for r in range(8):
        x = vecs[r].T
        pop = population[r : r + 1, :]
        inv = 1.0 / pop
        n1 = jnp.sum(x[PLANES:] * x[PLANES:], axis=0, keepdims=True) * (inv * inv)
        inv2 = inv * inv
        x2 = x[:PLANES] * inv2
        n2 = jnp.sum(x2 * x2, axis=0, keepdims=True)
        root2 = jnp.sqrt(n2 + EPSILON)
        root1 = jnp.sqrt(n1 + EPSILON)
        eigen_ref[r : r + 1, :] = root2 / root1
        out_ref[pl.ds(r, PLANES, stride=ROWS), :] = x2 * (jnp.sqrt(F32(NDATE)) / root2)


def on_device(slc, offsets, masks):
    hbm = pl.BlockSpec(memory_space=pltpu.HBM)
    vmem = pl.BlockSpec(memory_space=pltpu.VMEM)
    linked, eigen = pl.pallas_call(
        kernel,
        out_shape=(
            jax.ShapeDtypeStruct((PLANES * ROWS, COLS), F32),
            jax.ShapeDtypeStruct((ROWS, COLS), F32),
        ),
        in_specs=[hbm, hbm, hbm],
        out_specs=(vmem, vmem),
        scratch_shapes=[
            pltpu.SMEM((2, NDATE), jnp.int32),
            pltpu.VMEM((5, ROWS, COLS), jnp.int32),
            pltpu.VMEM((2, ROWS, NDATE * COLS), F32),
            pltpu.VMEM((NDATE, 2, COLS), F32),
            pltpu.VMEM((3, NDATE, 2, ROWS, COLS), F32),
            pltpu.VMEM((3, NDATE, 2, COLS), F32),
            pltpu.VMEM((2, 2, ROWS, NDATE * COLS), F32),
            pltpu.VMEM((WIN, PLANES, COLS), F32),
            pltpu.VMEM((8, 144, COLS), F32),
            pltpu.VMEM((3, COLS, COLS), F32),
            pltpu.VMEM((GROUPS * COLS, COLS), BF16),
            pltpu.VMEM((GROUPS * COLS, COLS), F32),
            pltpu.VMEM((GROUPS * COLS, 2 * COLS), BF16),
            pltpu.VMEM((8, COLS, COLS), jnp.int32),
            pltpu.VMEM((8, COLS, COLS), F32),
            pltpu.SemaphoreType.DMA((5,)),
            pltpu.SemaphoreType.DMA((2, 4, 8)),
            pltpu.SemaphoreType.DMA((2, 4, 8)),
            pltpu.SemaphoreType.DMA((2, len(NEAR) + 1)),
            pltpu.SemaphoreType.DMA((2, len(NEAR) + 1)),
            pltpu.SemaphoreType.DMA((2, len(FAR))),
            pltpu.SemaphoreType.DMA((2, len(FAR))),
            pltpu.SemaphoreType.DMA((2, len(FAR), 2)),
            pltpu.SemaphoreType.DMA((2, len(FAR), 2)),
        ],
        compiler_params=pltpu.CompilerParams(
            collective_id=0, has_side_effects=True, vmem_limit_bytes=48 * 1024 * 1024
        ),
        name="phase_linking",
    )(*(pltpu.with_memory_space_constraint(x, pltpu.HBM) for x in (offsets, slc[:, 0], masks)))
    return linked.reshape(2, NDATE, ROWS, COLS), eigen


def solution(mesh):
    in_specs = (P(None, "date", "row", None), P(), P(None, "row", "date"))
    out_specs = (P(None, None, "row", "date"), P("row", "date"))
    return jax.shard_map(
        on_device, mesh=mesh, in_specs=in_specs, out_specs=out_specs, check_vma=False
    )
```

```python
import jax
import jax.numpy as jnp
from jax import lax
from jax.experimental import pallas as pl
from jax.experimental.pallas import tpu as pltpu
from jax.sharding import PartitionSpec as P

NDATE = 32
COLS = 128
ROWS = 8
PLANES = 2 * NDATE
EPSILON = 1e-06
MESH = pl.DeviceIdType.MESH
F32 = jnp.float32
BF16 = jnp.bfloat16


def iota(shape, axis):
    return lax.broadcasted_iota(jnp.int32, shape, axis)


def pack_rim(slc_ref, rim_ref):
    lane = iota((ROWS, COLS), 1)
    row = iota((ROWS, COLS), 0)
    for dest in range(NDATE):
        for part in range(2):
            if dest > 0:
                left = slc_ref[part, :, (dest - 1) * COLS : dest * COLS]
            else:
                left = jnp.zeros((ROWS, COLS), F32)
            if dest < NDATE - 1:
                right = slc_ref[part, :, (dest + 1) * COLS : (dest + 2) * COLS]
            else:
                right = jnp.zeros((ROWS, COLS), F32)
            both = jnp.where(lane < 8, right, left)
            spread = pltpu.roll(both, 8, 1, stride=16, stride_axis=0)
            spread = jnp.where(lane // 16 == row, spread, 0.0)
            rim_ref[dest, part : part + 1, :] = jnp.sum(spread, axis=0, keepdims=True)


def hops(step):
    return min(step[0], 4 - step[0]) + min(step[1], 4 - step[1])


CHIPS = sorted(((g, i) for g in range(4) for i in range(4)), key=hops)
FAR = CHIPS[12:]
NEAR = CHIPS[:12]
SENDS = [(g, i, k) for g, i in CHIPS for k in range(2) if (g, i, k) != (0, 0, 0)]


def peer(date, g, i, k):
    return (date // 8 + g) % 4 * 8 + (date // 2 + i) % 4 * 2 + (date + k) % 2


WIN = 16
GROUPS = 17


def split(x):
    high = x.astype(BF16).astype(F32)
    return high, x - high


def date_vectors(offs_ref, axis):
    if axis == 0:
        row = iota((8, COLS), 0)
        out = []
        for part in range(4):
            vec = jnp.zeros((8, COLS), jnp.int32)
            for s in range(8):
                vec = jnp.where(row == s, offs_ref[0, part * 8 + s] + 2, vec)
            out.append(vec)
        return out
    lane = iota((8, COLS), 1) % NDATE
    vec = jnp.zeros((8, COLS), jnp.int32)
    row_vec = jnp.zeros((8, COLS), jnp.int32)
    for s in range(NDATE):
        vec = jnp.where(lane == s, offs_ref[1, s] + 2, vec)
        row_vec = jnp.where(lane == s, offs_ref[0, s] + 2, row_vec)
    return vec, row_vec


def mix_rows(rows, steps):
    bit0, bit1, bit2 = (steps & 1) != 0, (steps & 2) != 0, steps == 4
    one = [jnp.where(bit0, rows[i + 1], rows[i]) for i in range(22)]
    two = [jnp.where(bit1, one[i + 2], one[i]) for i in range(19)]
    base = [jnp.where(bit2, rows[i + 4], two[i]) for i in range(19)]
    return [
        0.5625 * (base[i + 1] + base[i + 2]) - 0.0625 * (base[i] + base[i + 3]) for i in range(WIN)
    ]


def kernel(
    offs_in,
    slc_ref,
    mask_in,
    out_ref,
    eigen_ref,
    offs_ref,
    mask_ref,
    slc_here,
    rim_here,
    main_ref,
    rim_ref,
    slab,
    mixed,
    tall,
    rim_tall,
    keys,
    plain,
    sums,
    slots,
    vecs,
    own_sem,
    send_sem,
    recv_sem,
    fwd_send,
    fwd_recv,
    hop_send,
    hop_recv,
    far_send,
    far_recv,
):
    date_pos, row_pos = lax.axis_index("date"), lax.axis_index("row")
    last_date, last_row = lax.axis_size("date") - 1, lax.axis_size("row") - 1
    lane8 = iota((8, COLS), 1)
    sub8 = iota((8, COLS), 0)

    load = pltpu.make_async_copy(slc_ref, slc_here, own_sem.at[2])
    load_mask = pltpu.make_async_copy(mask_in, mask_ref, own_sem.at[3])
    load_offs = pltpu.make_async_copy(offs_in, offs_ref, own_sem.at[4])
    load.start()
    load_mask.start()
    load_offs.start()
    barrier = pltpu.get_barrier_semaphore()
    for s in (1, last_row):
        pl.semaphore_signal(
            barrier, inc=1, device_id={"row": (row_pos + s) % (last_row + 1)}, device_id_type=MESH
        )
    for g, i, k in SENDS[::-1]:
        pl.semaphore_signal(
            barrier, inc=1, device_id={"date": peer(date_pos, g, i, k)}, device_id_type=MESH
        )

    load.wait()
    pl.semaphore_wait(barrier, NDATE + 1)

    def part(which, date):
        return (
            (slc_here.at[:, :, pl.ds(pl.multiple_of(date * COLS, COLS), COLS)], main_ref)
            if which == 0
            else (rim_here.at[date], rim_ref)
        )

    def send(which, g, i, k):
        dest = peer(date_pos, g, i, k)
        src, ref = part(which, dest)
        return pltpu.make_async_remote_copy(
            src_ref=src,
            dst_ref=ref.at[1, date_pos],
            send_sem=send_sem.at[which, g, 2 * i + k],
            recv_sem=recv_sem.at[which, g, 2 * i + k],
            device_id={"date": dest},
            device_id_type=MESH,
        )

    def sends_to(side):
        return row_pos > 0 if side == 0 else row_pos < last_row

    def gets_from(side):
        return row_pos < last_row if side == 0 else row_pos > 0

    def hop(side, n):
        g, i = FAR[n]
        chip = (date_pos // 8 + g) % 4 * 4 + (date_pos // 2 + i) % 4
        cols = pl.ds(pl.multiple_of(chip * 2 * COLS, 2 * COLS), 2 * COLS)
        return pltpu.make_async_remote_copy(
            src_ref=slc_here.at[:, :, cols],
            dst_ref=slab.at[side, :, :, cols],
            send_sem=hop_send.at[side, n],
            recv_sem=hop_recv.at[side, n],
            device_id={"row": row_pos - 1 if side == 0 else row_pos + 1},
            device_id_type=MESH,
        )

    def far(side, n, k):
        dest = peer(date_pos, *FAR[n], k)
        return pltpu.make_async_remote_copy(
            src_ref=slab.at[side, :, :, pl.ds(pl.multiple_of(dest * COLS, COLS), COLS)],
            dst_ref=main_ref.at[2 - 2 * side, date_pos],
            send_sem=far_send.at[side, n, k],
            recv_sem=far_recv.at[side, n, k],
            device_id={"date": dest},
            device_id_type=MESH,
        )

    hops_out = [[hop(side, n) for n in range(len(FAR))] for side in range(2)]
    fars = [[far(side, n, k) for n in range(len(FAR)) for k in range(2)] for side in range(2)]
    for side in range(2):

        @pl.when(sends_to(side))
        def _(side=side):
            for copy in hops_out[side]:
                copy.start()

    mains = {step: send(0, *step) for step in SENDS}
    rims = {step: send(1, *step) for step in SENDS}
    for copy in mains.values():
        copy.start()
    pack_rim(slc_here, rim_here)
    own = []
    for which in range(2):
        src, ref = part(which, date_pos)
        own.append(pltpu.make_async_copy(src, ref.at[1, date_pos], own_sem.at[which]))
    for copy in own:
        copy.start()
    for copy in rims.values():
        copy.start()

    load_mask.wait()
    load_offs.wait()
    population = jnp.zeros((8, COLS), jnp.int32)
    for w in range(5):
        population = population + lax.population_count(mask_ref[w])
    population = population.astype(F32)
    zero8 = jnp.zeros((8, COLS), jnp.int32)
    for r in range(8):
        pieces = []
        for n in range(WIN):
            i = n - r
            if 0 <= i <= 8:
                nine = (mask_ref[i // 2, r : r + 1, :] >> (9 * (i % 2))) & 511
                pieces.append(jnp.broadcast_to(nine, (8, COLS)))
            else:
                pieces.append(zero8)
        slots[r] = jnp.concatenate(pieces, axis=0).T


    def forward(side, number, first, count, ref):
        slot, to = (2, row_pos - 1) if side == 0 else (0, row_pos + 1)
        return pltpu.make_async_remote_copy(
            src_ref=ref.at[1, pl.ds(first, count)],
            dst_ref=ref.at[slot, pl.ds(first, count)],
            send_sem=fwd_send.at[side, number],
            recv_sem=fwd_recv.at[side, number],
            device_id={"row": to},
            device_id_type=MESH,
        )

    def forwards(side):
        out = []
        for number, (g, i) in enumerate(NEAR):
            first = (date_pos // 8 + 4 - g) % 4 * 8 + (date_pos // 2 + 4 - i) % 4 * 2
            out.append(forward(side, number, first, 2, main_ref))
        return out + [forward(side, len(NEAR), 0, NDATE, rim_ref)]

    before, after = forwards(0), forwards(1)
    for number in range(len(NEAR) + 1):
        if number < len(NEAR):
            g, i = NEAR[number]
            for k in range(2):
                if (g, i, k) in mains:
                    mains[g, i, k].wait_recv()
                else:
                    own[0].wait()
        else:
            own[1].wait()
            for copy in rims.values():
                copy.wait_recv()

        @pl.when(row_pos > 0)
        def _(number=number):
            before[number].start()

        @pl.when(row_pos < last_row)
        def _(number=number):
            after[number].start()

        if number < len(FAR):
            for side in range(2):

                @pl.when(gets_from(side))
                def _(side=side, number=number):
                    hops_out[side][number].wait_recv()
                    fars[side][2 * number].start()
                    fars[side][2 * number + 1].start()

    for g, i in FAR:
        for k in range(2):
            mains[g, i, k].wait_recv()
    for side in range(2):

        @pl.when(gets_from(side))
        def _(side=side):
            for copy in fars[side]:
                copy.wait_recv()
            for copy in (before, after)[side][:-1]:
                copy.wait_recv()

    main_rows = main_ref.reshape(-1, COLS)
    row_steps = date_vectors(offs_ref, 0)
    col_steps, lane_row_steps = date_vectors(offs_ref, 1)
    for part in range(2):
        for eight in range(4):
            rows = []
            for i in range(23):
                slot, row = (i + 1) // 8, (i + 1) % 8
                start = ((slot * NDATE + eight * 8) * 2 + part) * ROWS + row
                x = main_rows[pl.ds(start, 8, stride=2 * ROWS), :]
                if slot == 0:
                    x = jnp.where(row_pos > 0, x, 0.0)
                if slot == 2:
                    x = jnp.where(row_pos < last_row, x, 0.0)
                rows.append(x)
            for i, x in enumerate(mix_rows(rows, row_steps[eight])):
                mixed[i, part * NDATE + eight * 8 : part * NDATE + eight * 8 + 8, :] = x

    for m in range(8):
        tall[m, 8:136, :] = jnp.concatenate([mixed[2 * m], mixed[2 * m + 1]], axis=0).T
    for side in range(2):

        @pl.when(gets_from(side))
        def _(side=side):
            (before, after)[side][-1].wait_recv()

    for slot in range(3):
        x = jnp.concatenate([rim_ref[slot, :, 0, :], rim_ref[slot, :, 1, :]], axis=0)
        if slot == 0:
            x = jnp.where(row_pos > 0, x, 0.0)
        if slot == 2:
            x = jnp.where(row_pos < last_row, x, 0.0)
        rim_tall[slot] = jnp.concatenate([x, x], axis=0).T
    for side in range(2):
        rows = []
        for i in range(23):
            slot, row = (i + 1) // 8, (i + 1) % 8
            rows.append(rim_tall[slot, 16 * row + 8 * side : 16 * row + 8 * side + 8, :])
        done = mix_rows(rows, lane_row_steps)
        for m in range(8):
            tall[m, 136 * side : 136 * side + 8, :] = jnp.where(
                lane8 < PLANES, done[2 * m], done[2 * m + 1]
            )

    for m in range(8):
        row = 8 * row_pos - 4 + 2 * m + (lane8 >= PLANES).astype(jnp.int32)
        inside = (row >= 0) & (row < 8 * (last_row + 1))
        weights = []
        for s in range(8):
            w = jnp.zeros((8, COLS), F32)
            for tap, value in enumerate((-0.0625, 0.5625, 0.5625, -0.0625)):
                w = jnp.where(col_steps + tap == s, value, w)
            weights.append(jnp.where(inside, w, 0.0))
        for g in range(GROUPS):
            x = weights[0] * tall[m, 8 * g + 1 : 8 * g + 9, :]
            for s in range(1, 8):
                x = x + weights[s] * tall[m, 8 * g + 1 + s : 8 * g + 9 + s, :]
            if g == 0:
                x = jnp.where((sub8 >= 4) | (date_pos > 0), x, 0.0)
            if g == GROUPS - 1:
                x = jnp.where((sub8 < 4) | (date_pos < last_date), x, 0.0)
            other = pltpu.roll(x, PLANES, 1)
            a = jnp.where(lane8 < PLANES, x, other)
            b = jnp.where(lane8 < PLANES, other, x)
            z = jnp.concatenate([a, b], axis=0)
            high, low = split(z)
            lane16 = iota((16, COLS), 1)
            first = g * COLS + 16 * m
            keys[first : first + 16, :] = jnp.where(lane16 < PLANES, high, low).astype(BF16)
            plain[first : first + 16, :] = z

    k_in = iota((COLS, COLS), 0) // NDATE % 2
    k_out = iota((COLS, COLS), 1) // PLANES
    adder = jnp.where(k_in == k_out, 1.0, 0.0).astype(BF16)
    for g in range(GROUPS):
        rows = slice(g * COLS, (g + 1) * COLS)
        total = jnp.dot(keys[rows, :], adder, preferred_element_type=F32)
        high, low = split(plain[rows, :] * total)
        sums[rows, :COLS] = high.astype(BF16)
        sums[rows, COLS:] = low.astype(BF16)

    across = lane8 % 8 - sub8
    shift0 = jnp.where(across >= 0, across, 31)
    shift1 = jnp.where(across <= 0, across + 8, 31)
    lane64 = iota((64, COLS), 1)
    quarter = lane64 // NDATE
    outer = (quarter == 0) | (quarter == 3)
    sign_a = jnp.where(quarter % 2 == 0, 1.0, -1.0)

    def first(blk):
        q0 = blk * COLS
        bits = []
        for r in range(8):
            w = slots[r, blk * 8 : blk * 8 + 8, :]
            bits.append(jnp.concatenate([(w >> shift0) & 1, (w >> shift1) & 1], axis=1))
        mask = jnp.concatenate(bits, axis=0).astype(F32)
        u = jnp.dot(mask.astype(BF16), sums[q0 : q0 + 2 * COLS, :], preferred_element_type=F32)
        return mask, u

    def second(blk, u):
        q0 = blk * COLS
        near = keys[q0 : q0 + 2 * COLS, :]
        u = u[:, :COLS] + u[:, COLS:]
        same = jnp.where(lane64 < PLANES, u, pltpu.roll(u, PLANES, 1))
        cross = jnp.where(outer, pltpu.roll(u, 32, 1), pltpu.roll(u, 96, 1))
        v = same + sign_a * cross
        turned = sign_a * pltpu.roll(v, 32, 1)
        both = jnp.concatenate([v, turned], axis=0)
        high, low = split(both)
        left = jnp.concatenate([high, low], axis=1).astype(BF16)
        right = jnp.concatenate([near, near], axis=1)
        a = lax.dot_general(
            left, right, (((1,), (1,)), ((), ())), preferred_element_type=F32
        )
        return v, a

    def third(blk, mask, a):
        q0 = blk * COLS
        near = keys[q0 : q0 + 2 * COLS, :]
        a = a * jnp.concatenate([mask, mask], axis=0)
        high, low = split(a)
        both = jnp.concatenate([high.astype(BF16), low.astype(BF16)], axis=0)
        return jnp.dot(both, near, preferred_element_type=F32)

    def fourth(blk, v, c):
        c = c[:128] + c[128:]
        c = c + pltpu.roll(c, PLANES, 1)
        v2 = c[:64] - sign_a * pltpu.roll(c[64:], 32, 1)
        both = jnp.where(lane64 < PLANES, v2, v)
        for r in range(8):
            vecs[r, blk * 8 : blk * 8 + 8, :] = both[8 * r : 8 * r + 8, :]

    blocks = range(16)
    ones = [first(b) for b in blocks]
    twos = [second(b, ones[b][1]) for b in blocks]
    threes = [third(b, ones[b][0], twos[b][1]) for b in blocks]
    for b in blocks:
        fourth(b, twos[b][0], threes[b])

    for r in range(8):
        x = vecs[r].T
        pop = population[r : r + 1, :]
        inv = 1.0 / pop
        n1 = jnp.sum(x[PLANES:] * x[PLANES:], axis=0, keepdims=True) * (inv * inv)
        inv2 = inv * inv
        x2 = x[:PLANES] * inv2
        n2 = jnp.sum(x2 * x2, axis=0, keepdims=True)
        root2 = jnp.sqrt(n2 + EPSILON)
        root1 = jnp.sqrt(n1 + EPSILON)
        eigen_ref[r : r + 1, :] = root2 / root1
        out_ref[pl.ds(r, PLANES, stride=ROWS), :] = x2 * (jnp.sqrt(F32(NDATE)) / root2)

    for step in SENDS:
        mains[step].wait_send()
        rims[step].wait_send()
    for side in range(2):

        @pl.when(sends_to(side))
        def _(side=side):
            for copy in hops_out[side] + (before, after)[side]:
                copy.wait_send()

        @pl.when(gets_from(side))
        def _(side=side):
            for copy in fars[side]:
                copy.wait_send()


def hand_out(linked_ref, eigen_ref, linked_out, eigen_out, sem):
    copies = [
        pltpu.make_async_copy(linked_ref, linked_out, sem.at[0]),
        pltpu.make_async_copy(eigen_ref, eigen_out, sem.at[1]),
    ]
    for copy in copies:
        copy.start()
    for copy in copies:
        copy.wait()


def on_device(slc, offsets, masks):
    hbm = pl.BlockSpec(memory_space=pltpu.HBM)
    vmem = pl.BlockSpec(memory_space=pltpu.VMEM)
    linked, eigen = pl.pallas_call(
        kernel,
        out_shape=(
            jax.ShapeDtypeStruct((PLANES * ROWS, COLS), F32),
            jax.ShapeDtypeStruct((ROWS, COLS), F32),
        ),
        in_specs=[hbm, hbm, hbm],
        out_specs=(vmem, vmem),
        scratch_shapes=[
            pltpu.SMEM((2, NDATE), jnp.int32),
            pltpu.VMEM((5, ROWS, COLS), jnp.int32),
            pltpu.VMEM((2, ROWS, NDATE * COLS), F32),
            pltpu.VMEM((NDATE, 2, COLS), F32),
            pltpu.VMEM((3, NDATE, 2, ROWS, COLS), F32),
            pltpu.VMEM((3, NDATE, 2, COLS), F32),
            pltpu.VMEM((2, 2, ROWS, NDATE * COLS), F32),
            pltpu.VMEM((WIN, PLANES, COLS), F32),
            pltpu.VMEM((8, 144, COLS), F32),
            pltpu.VMEM((3, COLS, COLS), F32),
            pltpu.VMEM((GROUPS * COLS, COLS), BF16),
            pltpu.VMEM((GROUPS * COLS, COLS), F32),
            pltpu.VMEM((GROUPS * COLS, 2 * COLS), BF16),
            pltpu.VMEM((8, COLS, COLS), jnp.int32),
            pltpu.VMEM((8, COLS, COLS), F32),
            pltpu.SemaphoreType.DMA((5,)),
            pltpu.SemaphoreType.DMA((2, 4, 8)),
            pltpu.SemaphoreType.DMA((2, 4, 8)),
            pltpu.SemaphoreType.DMA((2, len(NEAR) + 1)),
            pltpu.SemaphoreType.DMA((2, len(NEAR) + 1)),
            pltpu.SemaphoreType.DMA((2, len(FAR))),
            pltpu.SemaphoreType.DMA((2, len(FAR))),
            pltpu.SemaphoreType.DMA((2, len(FAR), 2)),
            pltpu.SemaphoreType.DMA((2, len(FAR), 2)),
        ],
        compiler_params=pltpu.CompilerParams(
            collective_id=0, has_side_effects=True, vmem_limit_bytes=48 * 1024 * 1024
        ),
        name="phase_linking",
    )(*(pltpu.with_memory_space_constraint(x, pltpu.HBM) for x in (offsets, slc[:, 0], masks)))
    linked, eigen = pl.pallas_call(
        hand_out,
        out_shape=(
            jax.ShapeDtypeStruct((PLANES * ROWS, COLS), F32),
            jax.ShapeDtypeStruct((ROWS, COLS), F32),
        ),
        in_specs=[vmem, vmem],
        out_specs=(hbm, hbm),
        scratch_shapes=[pltpu.SemaphoreType.DMA((2,))],
        name="hand_out",
    )(*(pltpu.with_memory_space_constraint(x, pltpu.VMEM) for x in (linked, eigen)))
    return linked.reshape(2, NDATE, ROWS, COLS), eigen


def solution(mesh):
    in_specs = (P(None, "date", "row", None), P(), P(None, "row", "date"))
    out_specs = (P(None, None, "row", "date"), P("row", "date"))
    return jax.shard_map(
        on_device, mesh=mesh, in_specs=in_specs, out_specs=out_specs, check_vma=False
    )
```

```python
import jax
import jax.numpy as jnp
from jax import lax
from jax.experimental import pallas as pl
from jax.experimental.pallas import tpu as pltpu
from jax.sharding import PartitionSpec as P

NDATE = 32
COLS = 128
ROWS = 8
PLANES = 2 * NDATE
EPSILON = 1e-06
MESH = pl.DeviceIdType.MESH
F32 = jnp.float32
BF16 = jnp.bfloat16


def iota(shape, axis):
    return lax.broadcasted_iota(jnp.int32, shape, axis)


def pack_rim(slc_ref, rim_ref):
    lane = iota((ROWS, COLS), 1)
    row = iota((ROWS, COLS), 0)
    for dest in range(NDATE):
        for part in range(2):
            if dest > 0:
                left = slc_ref[part, :, (dest - 1) * COLS : dest * COLS]
            else:
                left = jnp.zeros((ROWS, COLS), F32)
            if dest < NDATE - 1:
                right = slc_ref[part, :, (dest + 1) * COLS : (dest + 2) * COLS]
            else:
                right = jnp.zeros((ROWS, COLS), F32)
            both = jnp.where(lane < 8, right, left)
            spread = pltpu.roll(both, 8, 1, stride=16, stride_axis=0)
            spread = jnp.where(lane // 16 == row, spread, 0.0)
            rim_ref[dest, part : part + 1, :] = jnp.sum(spread, axis=0, keepdims=True)


def hops(step):
    return min(step[0], 4 - step[0]) + min(step[1], 4 - step[1])


CHIPS = sorted(((g, i) for g in range(4) for i in range(4)), key=hops)
FAR = CHIPS[12:]
NEAR = CHIPS[:12]
SENDS = [(g, i, k) for g, i in CHIPS for k in range(2) if (g, i, k) != (0, 0, 0)]


def peer(date, g, i, k):
    return (date // 8 + g) % 4 * 8 + (date // 2 + i) % 4 * 2 + (date + k) % 2


WIN = 16
GROUPS = 17


def split(x):
    high = x.astype(BF16).astype(F32)
    return high, x - high


def date_vectors(offs_ref, axis):
    if axis == 0:
        row = iota((8, COLS), 0)
        out = []
        for part in range(4):
            vec = jnp.zeros((8, COLS), jnp.int32)
            for s in range(8):
                vec = jnp.where(row == s, offs_ref[0, part * 8 + s] + 2, vec)
            out.append(vec)
        return out
    lane = iota((8, COLS), 1) % NDATE
    vec = jnp.zeros((8, COLS), jnp.int32)
    row_vec = jnp.zeros((8, COLS), jnp.int32)
    for s in range(NDATE):
        vec = jnp.where(lane == s, offs_ref[1, s] + 2, vec)
        row_vec = jnp.where(lane == s, offs_ref[0, s] + 2, row_vec)
    return vec, row_vec


def mix_rows(rows, steps):
    bit0, bit1, bit2 = (steps & 1) != 0, (steps & 2) != 0, steps == 4
    one = [jnp.where(bit0, rows[i + 1], rows[i]) for i in range(22)]
    two = [jnp.where(bit1, one[i + 2], one[i]) for i in range(19)]
    base = [jnp.where(bit2, rows[i + 4], two[i]) for i in range(19)]
    return [
        0.5625 * (base[i + 1] + base[i + 2]) - 0.0625 * (base[i] + base[i + 3]) for i in range(WIN)
    ]


def all_of(ref, sem):
    pltpu.make_async_copy(ref, ref, sem).wait()


def kernel(
    offs_in,
    slc_ref,
    mask_in,
    out_ref,
    eigen_ref,
    offs_ref,
    mask_ref,
    slc_here,
    rim_here,
    main_ref,
    rim_ref,
    slab,
    mixed,
    tall,
    rim_tall,
    keys,
    plain,
    sums,
    slots,
    vecs,
    own_sem,
    send_sem,
    recv_sem,
    fwd_send,
    fwd_recv,
    hop_send,
    hop_recv,
    far_send,
    far_recv,
):
    date_pos, row_pos = lax.axis_index("date"), lax.axis_index("row")
    last_date, last_row = lax.axis_size("date") - 1, lax.axis_size("row") - 1
    lane8 = iota((8, COLS), 1)
    sub8 = iota((8, COLS), 0)

    load = pltpu.make_async_copy(slc_ref, slc_here, own_sem.at[2])
    load_mask = pltpu.make_async_copy(mask_in, mask_ref, own_sem.at[3])
    load_offs = pltpu.make_async_copy(offs_in, offs_ref, own_sem.at[4])
    load.start()
    load_mask.start()
    load_offs.start()
    barrier = pltpu.get_barrier_semaphore()
    for s in (1, last_row):
        pl.semaphore_signal(
            barrier, inc=1, device_id={"row": (row_pos + s) % (last_row + 1)}, device_id_type=MESH
        )
    for g, i, k in SENDS[::-1]:
        pl.semaphore_signal(
            barrier, inc=1, device_id={"date": peer(date_pos, g, i, k)}, device_id_type=MESH
        )

    load.wait()
    pl.semaphore_wait(barrier, NDATE + 1)

    def part(which, date):
        return (
            (slc_here.at[:, :, pl.ds(pl.multiple_of(date * COLS, COLS), COLS)], main_ref)
            if which == 0
            else (rim_here.at[date], rim_ref)
        )

    def send(which, g, i, k):
        dest = peer(date_pos, g, i, k)
        src, ref = part(which, dest)
        return pltpu.make_async_remote_copy(
            src_ref=src,
            dst_ref=ref.at[1, date_pos],
            send_sem=send_sem.at[which],
            recv_sem=own_sem.at[1]
            if which
            else own_sem.at[5]
            if (g, i) in FAR
            else recv_sem.at[g, 2 * i + k],
            device_id={"date": dest},
            device_id_type=MESH,
        )

    def sends_to(side):
        return row_pos > 0 if side == 0 else row_pos < last_row

    def gets_from(side):
        return row_pos < last_row if side == 0 else row_pos > 0

    def hop(side, n):
        g, i = FAR[n]
        chip = (date_pos // 8 + g) % 4 * 4 + (date_pos // 2 + i) % 4
        cols = pl.ds(pl.multiple_of(chip * 2 * COLS, 2 * COLS), 2 * COLS)
        return pltpu.make_async_remote_copy(
            src_ref=slc_here.at[:, :, cols],
            dst_ref=slab.at[side, :, :, cols],
            send_sem=hop_send.at[side],
            recv_sem=hop_recv.at[side, n],
            device_id={"row": row_pos - 1 if side == 0 else row_pos + 1},
            device_id_type=MESH,
        )

    def far(side, n, k):
        dest = peer(date_pos, *FAR[n], k)
        return pltpu.make_async_remote_copy(
            src_ref=slab.at[side, :, :, pl.ds(pl.multiple_of(dest * COLS, COLS), COLS)],
            dst_ref=main_ref.at[2 - 2 * side, date_pos],
            send_sem=far_send.at[side],
            recv_sem=far_recv.at[side],
            device_id={"date": dest},
            device_id_type=MESH,
        )

    hops_out = [[hop(side, n) for n in range(len(FAR))] for side in range(2)]
    fars = [[far(side, n, k) for n in range(len(FAR)) for k in range(2)] for side in range(2)]
    for side in range(2):

        @pl.when(sends_to(side))
        def _(side=side):
            for copy in hops_out[side]:
                copy.start()

    mains = {step: send(0, *step) for step in SENDS}
    rims = {step: send(1, *step) for step in SENDS}
    for copy in mains.values():
        copy.start()
    pack_rim(slc_here, rim_here)
    own = []
    for which in range(2):
        src, ref = part(which, date_pos)
        own.append(pltpu.make_async_copy(src, ref.at[1, date_pos], own_sem.at[which]))
    for copy in own:
        copy.start()
    for copy in rims.values():
        copy.start()

    load_mask.wait()
    load_offs.wait()
    population = jnp.zeros((8, COLS), jnp.int32)
    for w in range(5):
        population = population + lax.population_count(mask_ref[w])
    population = population.astype(F32)
    zero8 = jnp.zeros((8, COLS), jnp.int32)
    for r in range(8):
        pieces = []
        for n in range(WIN):
            i = n - r
            if 0 <= i <= 8:
                nine = (mask_ref[i // 2, r : r + 1, :] >> (9 * (i % 2))) & 511
                pieces.append(jnp.broadcast_to(nine, (8, COLS)))
            else:
                pieces.append(zero8)
        slots[r] = jnp.concatenate(pieces, axis=0).T


    def forward(side, number, first, count, ref):
        slot, to = (2, row_pos - 1) if side == 0 else (0, row_pos + 1)
        return pltpu.make_async_remote_copy(
            src_ref=ref.at[1, pl.ds(first, count)],
            dst_ref=ref.at[slot, pl.ds(first, count)],
            send_sem=fwd_send.at[side, number // len(NEAR)],
            recv_sem=fwd_recv.at[side, number // len(NEAR)],
            device_id={"row": to},
            device_id_type=MESH,
        )

    def forwards(side):
        out = []
        for number, (g, i) in enumerate(NEAR):
            first = (date_pos // 8 + 4 - g) % 4 * 8 + (date_pos // 2 + 4 - i) % 4 * 2
            out.append(forward(side, number, first, 2, main_ref))
        return out + [forward(side, len(NEAR), 0, NDATE, rim_ref)]

    before, after = forwards(0), forwards(1)
    for number in range(len(NEAR) + 1):
        if number < len(NEAR):
            g, i = NEAR[number]
            for k in range(2):
                if (g, i, k) in mains:
                    mains[g, i, k].wait_recv()
                else:
                    own[0].wait()
        else:
            all_of(rim_ref.at[1], own_sem.at[1])

        @pl.when(row_pos > 0)
        def _(number=number):
            before[number].start()

        @pl.when(row_pos < last_row)
        def _(number=number):
            after[number].start()

        if number < len(FAR):
            for side in range(2):

                @pl.when(gets_from(side))
                def _(side=side, number=number):
                    hops_out[side][number].wait_recv()
                    fars[side][2 * number].start()
                    fars[side][2 * number + 1].start()

    all_of(main_ref.at[1, pl.ds(0, NDATE - 1)], send_sem.at[0])
    all_of(rim_ref.at[1, pl.ds(0, NDATE - 1)], send_sem.at[1])
    all_of(main_ref.at[1, pl.ds(0, 2 * len(FAR))], own_sem.at[5])
    for side in range(2):

        @pl.when(gets_from(side))
        def _(side=side):
            all_of(main_ref.at[1, pl.ds(0, 2 * len(FAR))], far_send.at[side])
            all_of(main_ref.at[1, pl.ds(0, 2 * len(FAR))], far_recv.at[side])
            all_of(main_ref.at[1, pl.ds(0, 2 * len(NEAR))], fwd_recv.at[side, 0])

    main_rows = main_ref.reshape(-1, COLS)
    row_steps = date_vectors(offs_ref, 0)
    col_steps, lane_row_steps = date_vectors(offs_ref, 1)
    for part in range(2):
        for eight in range(4):
            rows = []
            for i in range(23):
                slot, row = (i + 1) // 8, (i + 1) % 8
                start = ((slot * NDATE + eight * 8) * 2 + part) * ROWS + row
                x = main_rows[pl.ds(start, 8, stride=2 * ROWS), :]
                if slot == 0:
                    x = jnp.where(row_pos > 0, x, 0.0)
                if slot == 2:
                    x = jnp.where(row_pos < last_row, x, 0.0)
                rows.append(x)
            for i, x in enumerate(mix_rows(rows, row_steps[eight])):
                mixed[i, part * NDATE + eight * 8 : part * NDATE + eight * 8 + 8, :] = x

    for m in range(8):
        tall[m, 8:136, :] = jnp.concatenate([mixed[2 * m], mixed[2 * m + 1]], axis=0).T
    for side in range(2):

        @pl.when(gets_from(side))
        def _(side=side):
            all_of(rim_ref.at[1], fwd_recv.at[side, 1])

    for slot in range(3):
        x = jnp.concatenate([rim_ref[slot, :, 0, :], rim_ref[slot, :, 1, :]], axis=0)
        if slot == 0:
            x = jnp.where(row_pos > 0, x, 0.0)
        if slot == 2:
            x = jnp.where(row_pos < last_row, x, 0.0)
        rim_tall[slot] = jnp.concatenate([x, x], axis=0).T
    for side in range(2):
        rows = []
        for i in range(23):
            slot, row = (i + 1) // 8, (i + 1) % 8
            rows.append(rim_tall[slot, 16 * row + 8 * side : 16 * row + 8 * side + 8, :])
        done = mix_rows(rows, lane_row_steps)
        for m in range(8):
            tall[m, 136 * side : 136 * side + 8, :] = jnp.where(
                lane8 < PLANES, done[2 * m], done[2 * m + 1]
            )

    for m in range(8):
        row = 8 * row_pos - 4 + 2 * m + (lane8 >= PLANES).astype(jnp.int32)
        inside = (row >= 0) & (row < 8 * (last_row + 1))
        weights = []
        for s in range(8):
            w = jnp.zeros((8, COLS), F32)
            for tap, value in enumerate((-0.0625, 0.5625, 0.5625, -0.0625)):
                w = jnp.where(col_steps + tap == s, value, w)
            weights.append(jnp.where(inside, w, 0.0))
        for g in range(GROUPS):
            x = weights[0] * tall[m, 8 * g + 1 : 8 * g + 9, :]
            for s in range(1, 8):
                x = x + weights[s] * tall[m, 8 * g + 1 + s : 8 * g + 9 + s, :]
            if g == 0:
                x = jnp.where((sub8 >= 4) | (date_pos > 0), x, 0.0)
            if g == GROUPS - 1:
                x = jnp.where((sub8 < 4) | (date_pos < last_date), x, 0.0)
            other = pltpu.roll(x, PLANES, 1)
            a = jnp.where(lane8 < PLANES, x, other)
            b = jnp.where(lane8 < PLANES, other, x)
            z = jnp.concatenate([a, b], axis=0)
            high, low = split(z)
            lane16 = iota((16, COLS), 1)
            first = g * COLS + 16 * m
            keys[first : first + 16, :] = jnp.where(lane16 < PLANES, high, low).astype(BF16)
            plain[first : first + 16, :] = z

    k_in = iota((COLS, COLS), 0) // NDATE % 2
    k_out = iota((COLS, COLS), 1) // PLANES
    adder = jnp.where(k_in == k_out, 1.0, 0.0).astype(BF16)
    for g in range(GROUPS):
        rows = slice(g * COLS, (g + 1) * COLS)
        total = jnp.dot(keys[rows, :], adder, preferred_element_type=F32)
        high, low = split(plain[rows, :] * total)
        sums[rows, :COLS] = high.astype(BF16)
        sums[rows, COLS:] = low.astype(BF16)

    across = lane8 % 8 - sub8
    shift0 = jnp.where(across >= 0, across, 31)
    shift1 = jnp.where(across <= 0, across + 8, 31)
    lane64 = iota((64, COLS), 1)
    quarter = lane64 // NDATE
    outer = (quarter == 0) | (quarter == 3)
    sign_a = jnp.where(quarter % 2 == 0, 1.0, -1.0)

    def first(blk):
        q0 = blk * COLS
        bits = []
        for r in range(8):
            w = slots[r, blk * 8 : blk * 8 + 8, :]
            bits.append(jnp.concatenate([(w >> shift0) & 1, (w >> shift1) & 1], axis=1))
        mask = jnp.concatenate(bits, axis=0).astype(F32)
        u = jnp.dot(mask.astype(BF16), sums[q0 : q0 + 2 * COLS, :], preferred_element_type=F32)
        return mask, u

    def second(blk, u):
        q0 = blk * COLS
        near = keys[q0 : q0 + 2 * COLS, :]
        u = u[:, :COLS] + u[:, COLS:]
        same = jnp.where(lane64 < PLANES, u, pltpu.roll(u, PLANES, 1))
        cross = jnp.where(outer, pltpu.roll(u, 32, 1), pltpu.roll(u, 96, 1))
        v = same + sign_a * cross
        turned = sign_a * pltpu.roll(v, 32, 1)
        both = jnp.concatenate([v, turned], axis=0)
        high, low = split(both)
        left = jnp.concatenate([high, low], axis=1).astype(BF16)
        right = jnp.concatenate([near, near], axis=1)
        a = lax.dot_general(
            left, right, (((1,), (1,)), ((), ())), preferred_element_type=F32
        )
        return v, a

    def third(blk, mask, a):
        q0 = blk * COLS
        near = keys[q0 : q0 + 2 * COLS, :]
        a = a * jnp.concatenate([mask, mask], axis=0)
        high, low = split(a)
        both = jnp.concatenate([high.astype(BF16), low.astype(BF16)], axis=0)
        return jnp.dot(both, near, preferred_element_type=F32)

    def fourth(blk, v, c):
        c = c[:128] + c[128:]
        c = c + pltpu.roll(c, PLANES, 1)
        v2 = c[:64] - sign_a * pltpu.roll(c[64:], 32, 1)
        both = jnp.where(lane64 < PLANES, v2, v)
        for r in range(8):
            vecs[r, blk * 8 : blk * 8 + 8, :] = both[8 * r : 8 * r + 8, :]

    blocks = range(16)
    ones = [first(b) for b in blocks]
    twos = [second(b, ones[b][1]) for b in blocks]
    threes = [third(b, ones[b][0], twos[b][1]) for b in blocks]
    for b in blocks:
        fourth(b, twos[b][0], threes[b])

    for r in range(8):
        x = vecs[r].T
        pop = population[r : r + 1, :]
        inv = 1.0 / pop
        n1 = jnp.sum(x[PLANES:] * x[PLANES:], axis=0, keepdims=True) * (inv * inv)
        inv2 = inv * inv
        x2 = x[:PLANES] * inv2
        n2 = jnp.sum(x2 * x2, axis=0, keepdims=True)
        root2 = jnp.sqrt(n2 + EPSILON)
        root1 = jnp.sqrt(n1 + EPSILON)
        eigen_ref[r : r + 1, :] = root2 / root1
        out_ref[pl.ds(r, PLANES, stride=ROWS), :] = x2 * (jnp.sqrt(F32(NDATE)) / root2)

    for side in range(2):

        @pl.when(sends_to(side))
        def _(side=side):
            all_of(main_ref.at[1, pl.ds(0, 2 * len(FAR))], hop_send.at[side])
            all_of(main_ref.at[1, pl.ds(0, 2 * len(NEAR))], fwd_send.at[side, 0])
            all_of(rim_ref.at[1], fwd_send.at[side, 1])


def hand_out(linked_ref, eigen_ref, linked_out, eigen_out, sem):
    copies = [
        pltpu.make_async_copy(linked_ref, linked_out, sem.at[0]),
        pltpu.make_async_copy(eigen_ref, eigen_out, sem.at[1]),
    ]
    for copy in copies:
        copy.start()
    for copy in copies:
        copy.wait()


def on_device(slc, offsets, masks):
    hbm = pl.BlockSpec(memory_space=pltpu.HBM)
    vmem = pl.BlockSpec(memory_space=pltpu.VMEM)
    linked, eigen = pl.pallas_call(
        kernel,
        out_shape=(
            jax.ShapeDtypeStruct((PLANES * ROWS, COLS), F32),
            jax.ShapeDtypeStruct((ROWS, COLS), F32),
        ),
        in_specs=[hbm, hbm, hbm],
        out_specs=(vmem, vmem),
        scratch_shapes=[
            pltpu.SMEM((2, NDATE), jnp.int32),
            pltpu.VMEM((5, ROWS, COLS), jnp.int32),
            pltpu.VMEM((2, ROWS, NDATE * COLS), F32),
            pltpu.VMEM((NDATE, 2, COLS), F32),
            pltpu.VMEM((3, NDATE, 2, ROWS, COLS), F32),
            pltpu.VMEM((3, NDATE, 2, COLS), F32),
            pltpu.VMEM((2, 2, ROWS, NDATE * COLS), F32),
            pltpu.VMEM((WIN, PLANES, COLS), F32),
            pltpu.VMEM((8, 144, COLS), F32),
            pltpu.VMEM((3, COLS, COLS), F32),
            pltpu.VMEM((GROUPS * COLS, COLS), BF16),
            pltpu.VMEM((GROUPS * COLS, COLS), F32),
            pltpu.VMEM((GROUPS * COLS, 2 * COLS), BF16),
            pltpu.VMEM((8, COLS, COLS), jnp.int32),
            pltpu.VMEM((8, COLS, COLS), F32),
            pltpu.SemaphoreType.DMA((6,)),
            pltpu.SemaphoreType.DMA((2,)),
            pltpu.SemaphoreType.DMA((4, 8)),
            pltpu.SemaphoreType.DMA((2, 2)),
            pltpu.SemaphoreType.DMA((2, 2)),
            pltpu.SemaphoreType.DMA((2,)),
            pltpu.SemaphoreType.DMA((2, len(FAR))),
            pltpu.SemaphoreType.DMA((2,)),
            pltpu.SemaphoreType.DMA((2,)),
        ],
        compiler_params=pltpu.CompilerParams(
            collective_id=0, has_side_effects=True, vmem_limit_bytes=48 * 1024 * 1024
        ),
        name="phase_linking",
    )(*(pltpu.with_memory_space_constraint(x, pltpu.HBM) for x in (offsets, slc[:, 0], masks)))
    linked, eigen = pl.pallas_call(
        hand_out,
        out_shape=(
            jax.ShapeDtypeStruct((PLANES * ROWS, COLS), F32),
            jax.ShapeDtypeStruct((ROWS, COLS), F32),
        ),
        in_specs=[vmem, vmem],
        out_specs=(hbm, hbm),
        scratch_shapes=[pltpu.SemaphoreType.DMA((2,))],
        name="hand_out",
    )(*(pltpu.with_memory_space_constraint(x, pltpu.VMEM) for x in (linked, eigen)))
    return linked.reshape(2, NDATE, ROWS, COLS), eigen


def solution(mesh):
    in_specs = (P(None, "date", "row", None), P(), P(None, "row", "date"))
    out_specs = (P(None, None, "row", "date"), P("row", "date"))
    return jax.shard_map(
        on_device, mesh=mesh, in_specs=in_specs, out_specs=out_specs, check_vma=False
    )
```

```python
import jax
import jax.numpy as jnp
from jax import lax
from jax.experimental import pallas as pl
from jax.experimental.pallas import tpu as pltpu
from jax.sharding import PartitionSpec as P

NDATE = 32
COLS = 128
ROWS = 8
PLANES = 2 * NDATE
EPSILON = 1e-06
MESH = pl.DeviceIdType.MESH
F32 = jnp.float32
BF16 = jnp.bfloat16


def iota(shape, axis):
    return lax.broadcasted_iota(jnp.int32, shape, axis)


def pack_rim(slc_ref, rim_ref):
    lane = iota((ROWS, COLS), 1)
    row = iota((ROWS, COLS), 0)
    for dest in range(NDATE):
        for part in range(2):
            if dest > 0:
                left = slc_ref[part, :, (dest - 1) * COLS : dest * COLS]
            else:
                left = jnp.zeros((ROWS, COLS), F32)
            if dest < NDATE - 1:
                right = slc_ref[part, :, (dest + 1) * COLS : (dest + 2) * COLS]
            else:
                right = jnp.zeros((ROWS, COLS), F32)
            both = jnp.where(lane < 8, right, left)
            spread = pltpu.roll(both, 8, 1, stride=16, stride_axis=0)
            spread = jnp.where(lane // 16 == row, spread, 0.0)
            rim_ref[dest, part : part + 1, :] = jnp.sum(spread, axis=0, keepdims=True)


def hops(step):
    return min(step[0], 4 - step[0]) + min(step[1], 4 - step[1])


CHIPS = sorted(((g, i) for g in range(4) for i in range(4)), key=hops)
FAR = CHIPS[12:]
NEAR = CHIPS[:12]
SENDS = [(g, i, k) for g, i in CHIPS for k in range(2) if (g, i, k) != (0, 0, 0)]


def peer(date, g, i, k):
    return (date // 8 + g) % 4 * 8 + (date // 2 + i) % 4 * 2 + (date + k) % 2


WIN = 16
GROUPS = 17


def split(x):
    high = x.astype(BF16).astype(F32)
    return high, x - high


def date_vectors(offs_ref, axis):
    if axis == 0:
        row = iota((8, COLS), 0)
        out = []
        for part in range(4):
            vec = jnp.zeros((8, COLS), jnp.int32)
            for s in range(8):
                vec = jnp.where(row == s, offs_ref[0, part * 8 + s] + 2, vec)
            out.append(vec)
        return out
    lane = iota((8, COLS), 1) % NDATE
    vec = jnp.zeros((8, COLS), jnp.int32)
    row_vec = jnp.zeros((8, COLS), jnp.int32)
    for s in range(NDATE):
        vec = jnp.where(lane == s, offs_ref[1, s] + 2, vec)
        row_vec = jnp.where(lane == s, offs_ref[0, s] + 2, row_vec)
    return vec, row_vec


def mix_rows(rows, steps):
    bit0, bit1, bit2 = (steps & 1) != 0, (steps & 2) != 0, steps == 4
    one = [jnp.where(bit0, rows[i + 1], rows[i]) for i in range(22)]
    two = [jnp.where(bit1, one[i + 2], one[i]) for i in range(19)]
    base = [jnp.where(bit2, rows[i + 4], two[i]) for i in range(19)]
    return [
        0.5625 * (base[i + 1] + base[i + 2]) - 0.0625 * (base[i] + base[i + 3]) for i in range(WIN)
    ]


def all_of(ref, sem):
    pltpu.make_async_copy(ref, ref, sem).wait()


def kernel(
    offs_in,
    slc_ref,
    mask_in,
    out_ref,
    eigen_ref,
    offs_ref,
    mask_ref,
    slc_here,
    rim_here,
    main_ref,
    rim_ref,
    slab,
    mixed,
    tall,
    rim_tall,
    keys,
    plain,
    sums,
    slots,
    vecs,
    own_sem,
    send_sem,
    recv_sem,
    fwd_send,
    fwd_recv,
    hop_send,
    hop_recv,
    far_send,
    far_recv,
):
    date_pos, row_pos = lax.axis_index("date"), lax.axis_index("row")
    last_date, last_row = lax.axis_size("date") - 1, lax.axis_size("row") - 1
    lane8 = iota((8, COLS), 1)
    sub8 = iota((8, COLS), 0)

    load = pltpu.make_async_copy(slc_ref, slc_here, own_sem.at[2])
    load_mask = pltpu.make_async_copy(mask_in, mask_ref, own_sem.at[3])
    load_offs = pltpu.make_async_copy(offs_in, offs_ref, own_sem.at[4])
    load.start()
    load_mask.start()
    load_offs.start()
    barrier = pltpu.get_barrier_semaphore()
    for s in (1, last_row):
        pl.semaphore_signal(
            barrier, inc=1, device_id={"row": (row_pos + s) % (last_row + 1)}, device_id_type=MESH
        )
    for g, i, k in SENDS[::-1]:
        pl.semaphore_signal(
            barrier, inc=1, device_id={"date": peer(date_pos, g, i, k)}, device_id_type=MESH
        )

    load.wait()
    pack_rim(slc_here, rim_here)
    pl.semaphore_wait(barrier, NDATE + 1)

    def part(which, date):
        return (
            (slc_here.at[:, :, pl.ds(pl.multiple_of(date * COLS, COLS), COLS)], main_ref)
            if which == 0
            else (rim_here.at[date], rim_ref)
        )

    def send(which, g, i, k):
        dest = peer(date_pos, g, i, k)
        src, ref = part(which, dest)
        return pltpu.make_async_remote_copy(
            src_ref=src,
            dst_ref=ref.at[1, date_pos],
            send_sem=send_sem.at[which],
            recv_sem=own_sem.at[1]
            if which
            else own_sem.at[5]
            if (g, i) in FAR
            else recv_sem.at[g, i],
            device_id={"date": dest},
            device_id_type=MESH,
        )

    def sends_to(side):
        return row_pos > 0 if side == 0 else row_pos < last_row

    def gets_from(side):
        return row_pos < last_row if side == 0 else row_pos > 0

    def hop(side, n):
        g, i = FAR[n]
        chip = (date_pos // 8 + g) % 4 * 4 + (date_pos // 2 + i) % 4
        cols = pl.ds(pl.multiple_of(chip * 2 * COLS, 2 * COLS), 2 * COLS)
        return pltpu.make_async_remote_copy(
            src_ref=slc_here.at[:, :, cols],
            dst_ref=slab.at[side, :, :, cols],
            send_sem=hop_send.at[side],
            recv_sem=hop_recv.at[side, n],
            device_id={"row": row_pos - 1 if side == 0 else row_pos + 1},
            device_id_type=MESH,
        )

    def far(side, n, k):
        dest = peer(date_pos, *FAR[n], k)
        return pltpu.make_async_remote_copy(
            src_ref=slab.at[side, :, :, pl.ds(pl.multiple_of(dest * COLS, COLS), COLS)],
            dst_ref=main_ref.at[2 - 2 * side, date_pos],
            send_sem=far_send.at[side],
            recv_sem=far_recv.at[side],
            device_id={"date": dest},
            device_id_type=MESH,
        )

    hops_out = [[hop(side, n) for n in range(len(FAR))] for side in range(2)]
    fars = [[far(side, n, k) for n in range(len(FAR)) for k in range(2)] for side in range(2)]
    for side in range(2):

        @pl.when(sends_to(side))
        def _(side=side):
            for copy in hops_out[side]:
                copy.start()

    mains = {step: send(0, *step) for step in SENDS}
    rims = {step: send(1, *step) for step in SENDS}
    for step in SENDS:
        mains[step].start()
        rims[step].start()
    own = []
    for which in range(2):
        src, ref = part(which, date_pos)
        own.append(
            pltpu.make_async_copy(
                src, ref.at[1, date_pos], own_sem.at[1] if which else recv_sem.at[0, 0]
            )
        )
    for copy in own:
        copy.start()

    load_mask.wait()
    load_offs.wait()
    population = jnp.zeros((8, COLS), jnp.int32)
    for w in range(5):
        population = population + lax.population_count(mask_ref[w])
    population = population.astype(F32)
    zero8 = jnp.zeros((8, COLS), jnp.int32)
    for r in range(8):
        pieces = []
        for n in range(WIN):
            i = n - r
            if 0 <= i <= 8:
                nine = (mask_ref[i // 2, r : r + 1, :] >> (9 * (i % 2))) & 511
                pieces.append(jnp.broadcast_to(nine, (8, COLS)))
            else:
                pieces.append(zero8)
        slots[r] = jnp.concatenate(pieces, axis=0).T


    def forward(side, number, first, count, ref):
        slot, to = (2, row_pos - 1) if side == 0 else (0, row_pos + 1)
        return pltpu.make_async_remote_copy(
            src_ref=ref.at[1, pl.ds(first, count)],
            dst_ref=ref.at[slot, pl.ds(first, count)],
            send_sem=fwd_send.at[side, number // len(NEAR)],
            recv_sem=fwd_recv.at[side, number // len(NEAR)],
            device_id={"row": to},
            device_id_type=MESH,
        )

    def forwards(side):
        out = []
        for number, (g, i) in enumerate(NEAR):
            first = (date_pos // 8 + 4 - g) % 4 * 8 + (date_pos // 2 + 4 - i) % 4 * 2
            out.append(forward(side, number, first, 2, main_ref))
        return out + [forward(side, len(NEAR), 0, NDATE, rim_ref)]

    before, after = forwards(0), forwards(1)
    for number in range(len(NEAR) + 1):
        if number < len(NEAR):
            g, i = NEAR[number]
            all_of(main_ref.at[1, pl.ds(0, 2)], recv_sem.at[g, i])
        else:
            all_of(rim_ref.at[1], own_sem.at[1])

        @pl.when(row_pos > 0)
        def _(number=number):
            before[number].start()
            if number < len(FAR):
                hops_out[1][number].wait_recv()
                fars[1][2 * number].start()
                fars[1][2 * number + 1].start()

        @pl.when(row_pos < last_row)
        def _(number=number):
            after[number].start()
            if number < len(FAR):
                hops_out[0][number].wait_recv()
                fars[0][2 * number].start()
                fars[0][2 * number + 1].start()

    all_of(main_ref.at[1, pl.ds(0, NDATE - 1)], send_sem.at[0])
    all_of(rim_ref.at[1, pl.ds(0, NDATE - 1)], send_sem.at[1])
    all_of(main_ref.at[1, pl.ds(0, 2 * len(FAR))], own_sem.at[5])
    for side in range(2):

        @pl.when(gets_from(side))
        def _(side=side):
            all_of(main_ref.at[1, pl.ds(0, 2 * len(FAR))], far_send.at[side])
            all_of(main_ref.at[1, pl.ds(0, 2 * len(FAR))], far_recv.at[side])
            all_of(main_ref.at[1, pl.ds(0, 2 * len(NEAR))], fwd_recv.at[side, 0])

    main_rows = main_ref.reshape(-1, COLS)
    row_steps = date_vectors(offs_ref, 0)
    col_steps, lane_row_steps = date_vectors(offs_ref, 1)
    for part in range(2):
        for eight in range(4):
            rows = []
            for i in range(23):
                slot, row = (i + 1) // 8, (i + 1) % 8
                start = ((slot * NDATE + eight * 8) * 2 + part) * ROWS + row
                x = main_rows[pl.ds(start, 8, stride=2 * ROWS), :]
                if slot == 0:
                    x = jnp.where(row_pos > 0, x, 0.0)
                if slot == 2:
                    x = jnp.where(row_pos < last_row, x, 0.0)
                rows.append(x)
            for i, x in enumerate(mix_rows(rows, row_steps[eight])):
                mixed[i, part * NDATE + eight * 8 : part * NDATE + eight * 8 + 8, :] = x

    for m in range(8):
        tall[m, 8:136, :] = jnp.concatenate([mixed[2 * m], mixed[2 * m + 1]], axis=0).T
    for side in range(2):

        @pl.when(gets_from(side))
        def _(side=side):
            all_of(rim_ref.at[1], fwd_recv.at[side, 1])

    for slot in range(3):
        x = jnp.concatenate([rim_ref[slot, :, 0, :], rim_ref[slot, :, 1, :]], axis=0)
        if slot == 0:
            x = jnp.where(row_pos > 0, x, 0.0)
        if slot == 2:
            x = jnp.where(row_pos < last_row, x, 0.0)
        rim_tall[slot] = jnp.concatenate([x, x], axis=0).T
    for side in range(2):
        rows = []
        for i in range(23):
            slot, row = (i + 1) // 8, (i + 1) % 8
            rows.append(rim_tall[slot, 16 * row + 8 * side : 16 * row + 8 * side + 8, :])
        done = mix_rows(rows, lane_row_steps)
        for m in range(8):
            tall[m, 136 * side : 136 * side + 8, :] = jnp.where(
                lane8 < PLANES, done[2 * m], done[2 * m + 1]
            )

    for m in range(8):
        row = 8 * row_pos - 4 + 2 * m + (lane8 >= PLANES).astype(jnp.int32)
        inside = (row >= 0) & (row < 8 * (last_row + 1))
        weights = []
        for s in range(8):
            w = jnp.zeros((8, COLS), F32)
            for tap, value in enumerate((-0.0625, 0.5625, 0.5625, -0.0625)):
                w = jnp.where(col_steps + tap == s, value, w)
            weights.append(jnp.where(inside, w, 0.0))
        for g in range(GROUPS):
            x = weights[0] * tall[m, 8 * g + 1 : 8 * g + 9, :]
            for s in range(1, 8):
                x = x + weights[s] * tall[m, 8 * g + 1 + s : 8 * g + 9 + s, :]
            if g == 0:
                x = jnp.where((sub8 >= 4) | (date_pos > 0), x, 0.0)
            if g == GROUPS - 1:
                x = jnp.where((sub8 < 4) | (date_pos < last_date), x, 0.0)
            other = pltpu.roll(x, PLANES, 1)
            a = jnp.where(lane8 < PLANES, x, other)
            b = jnp.where(lane8 < PLANES, other, x)
            z = jnp.concatenate([a, b], axis=0)
            high, low = split(z)
            lane16 = iota((16, COLS), 1)
            first = g * COLS + 16 * m
            keys[first : first + 16, :] = jnp.where(lane16 < PLANES, high, low).astype(BF16)
            plain[first : first + 16, :] = z

    k_in = iota((COLS, COLS), 0) // NDATE % 2
    k_out = iota((COLS, COLS), 1) // PLANES
    adder = jnp.where(k_in == k_out, 1.0, 0.0).astype(BF16)
    for g in range(GROUPS):
        rows = slice(g * COLS, (g + 1) * COLS)
        total = jnp.dot(keys[rows, :], adder, preferred_element_type=F32)
        high, low = split(plain[rows, :] * total)
        sums[rows, :COLS] = high.astype(BF16)
        sums[rows, COLS:] = low.astype(BF16)

    across = lane8 % 8 - sub8
    shift0 = jnp.where(across >= 0, across, 31)
    shift1 = jnp.where(across <= 0, across + 8, 31)
    lane64 = iota((64, COLS), 1)
    quarter = lane64 // NDATE
    outer = (quarter == 0) | (quarter == 3)
    sign_a = jnp.where(quarter % 2 == 0, 1.0, -1.0)

    def first(blk):
        q0 = blk * COLS
        bits = []
        for r in range(8):
            w = slots[r, blk * 8 : blk * 8 + 8, :]
            bits.append(jnp.concatenate([(w >> shift0) & 1, (w >> shift1) & 1], axis=1))
        mask = jnp.concatenate(bits, axis=0).astype(F32)
        u = jnp.dot(mask.astype(BF16), sums[q0 : q0 + 2 * COLS, :], preferred_element_type=F32)
        return mask, u

    def second(blk, u):
        q0 = blk * COLS
        near = keys[q0 : q0 + 2 * COLS, :]
        u = u[:, :COLS] + u[:, COLS:]
        same = jnp.where(lane64 < PLANES, u, pltpu.roll(u, PLANES, 1))
        cross = jnp.where(outer, pltpu.roll(u, 32, 1), pltpu.roll(u, 96, 1))
        v = same + sign_a * cross
        turned = sign_a * pltpu.roll(v, 32, 1)
        both = jnp.concatenate([v, turned], axis=0)
        high, low = split(both)
        left = jnp.concatenate([high, low], axis=1).astype(BF16)
        right = jnp.concatenate([near, near], axis=1)
        a = lax.dot_general(
            left, right, (((1,), (1,)), ((), ())), preferred_element_type=F32
        )
        return v, a

    def third(blk, mask, a):
        q0 = blk * COLS
        near = keys[q0 : q0 + 2 * COLS, :]
        a = a * jnp.concatenate([mask, mask], axis=0)
        high, low = split(a)
        both = jnp.concatenate([high.astype(BF16), low.astype(BF16)], axis=0)
        return jnp.dot(both, near, preferred_element_type=F32)

    def fourth(blk, v, c):
        c = c[:128] + c[128:]
        c = c + pltpu.roll(c, PLANES, 1)
        v2 = c[:64] - sign_a * pltpu.roll(c[64:], 32, 1)
        both = jnp.where(lane64 < PLANES, v2, v)
        for r in range(8):
            vecs[r, blk * 8 : blk * 8 + 8, :] = both[8 * r : 8 * r + 8, :]

    blocks = range(16)
    ones = [first(b) for b in blocks]
    twos = [second(b, ones[b][1]) for b in blocks]
    threes = [third(b, ones[b][0], twos[b][1]) for b in blocks]
    for b in blocks:
        fourth(b, twos[b][0], threes[b])

    for r in range(8):
        x = vecs[r].T
        pop = population[r : r + 1, :]
        inv = 1.0 / pop
        n1 = jnp.sum(x[PLANES:] * x[PLANES:], axis=0, keepdims=True) * (inv * inv)
        inv2 = inv * inv
        x2 = x[:PLANES] * inv2
        n2 = jnp.sum(x2 * x2, axis=0, keepdims=True)
        root2 = jnp.sqrt(n2 + EPSILON)
        root1 = jnp.sqrt(n1 + EPSILON)
        eigen_ref[r : r + 1, :] = root2 / root1
        out_ref[pl.ds(r, PLANES, stride=ROWS), :] = x2 * (jnp.sqrt(F32(NDATE)) / root2)

    for side in range(2):

        @pl.when(sends_to(side))
        def _(side=side):
            all_of(main_ref.at[1, pl.ds(0, 2 * len(FAR))], hop_send.at[side])
            all_of(main_ref.at[1, pl.ds(0, 2 * len(NEAR))], fwd_send.at[side, 0])
            all_of(rim_ref.at[1], fwd_send.at[side, 1])


def hand_out(linked_ref, eigen_ref, linked_out, eigen_out, sem):
    copies = [
        pltpu.make_async_copy(linked_ref, linked_out, sem.at[0]),
        pltpu.make_async_copy(eigen_ref, eigen_out, sem.at[1]),
    ]
    for copy in copies:
        copy.start()
    for copy in copies:
        copy.wait()


def on_device(slc, offsets, masks):
    hbm = pl.BlockSpec(memory_space=pltpu.HBM)
    vmem = pl.BlockSpec(memory_space=pltpu.VMEM)
    linked, eigen = pl.pallas_call(
        kernel,
        out_shape=(
            jax.ShapeDtypeStruct((PLANES * ROWS, COLS), F32),
            jax.ShapeDtypeStruct((ROWS, COLS), F32),
        ),
        in_specs=[hbm, hbm, hbm],
        out_specs=(vmem, vmem),
        scratch_shapes=[
            pltpu.SMEM((2, NDATE), jnp.int32),
            pltpu.VMEM((5, ROWS, COLS), jnp.int32),
            pltpu.VMEM((2, ROWS, NDATE * COLS), F32),
            pltpu.VMEM((NDATE, 2, COLS), F32),
            pltpu.VMEM((3, NDATE, 2, ROWS, COLS), F32),
            pltpu.VMEM((3, NDATE, 2, COLS), F32),
            pltpu.VMEM((2, 2, ROWS, NDATE * COLS), F32),
            pltpu.VMEM((WIN, PLANES, COLS), F32),
            pltpu.VMEM((8, 144, COLS), F32),
            pltpu.VMEM((3, COLS, COLS), F32),
            pltpu.VMEM((GROUPS * COLS, COLS), BF16),
            pltpu.VMEM((GROUPS * COLS, COLS), F32),
            pltpu.VMEM((GROUPS * COLS, 2 * COLS), BF16),
            pltpu.VMEM((8, COLS, COLS), jnp.int32),
            pltpu.VMEM((8, COLS, COLS), F32),
            pltpu.SemaphoreType.DMA((6,)),
            pltpu.SemaphoreType.DMA((2,)),
            pltpu.SemaphoreType.DMA((4, 4)),
            pltpu.SemaphoreType.DMA((2, 2)),
            pltpu.SemaphoreType.DMA((2, 2)),
            pltpu.SemaphoreType.DMA((2,)),
            pltpu.SemaphoreType.DMA((2, len(FAR))),
            pltpu.SemaphoreType.DMA((2,)),
            pltpu.SemaphoreType.DMA((2,)),
        ],
        compiler_params=pltpu.CompilerParams(
            collective_id=0, has_side_effects=True, vmem_limit_bytes=48 * 1024 * 1024
        ),
        name="phase_linking",
    )(*(pltpu.with_memory_space_constraint(x, pltpu.HBM) for x in (offsets, slc[:, 0], masks)))
    linked, eigen = pl.pallas_call(
        hand_out,
        out_shape=(
            jax.ShapeDtypeStruct((PLANES * ROWS, COLS), F32),
            jax.ShapeDtypeStruct((ROWS, COLS), F32),
        ),
        in_specs=[vmem, vmem],
        out_specs=(hbm, hbm),
        scratch_shapes=[pltpu.SemaphoreType.DMA((2,))],
        name="hand_out",
    )(*(pltpu.with_memory_space_constraint(x, pltpu.VMEM) for x in (linked, eigen)))
    return linked.reshape(2, NDATE, ROWS, COLS), eigen


def solution(mesh):
    in_specs = (P(None, "date", "row", None), P(), P(None, "row", "date"))
    out_specs = (P(None, None, "row", "date"), P("row", "date"))
    return jax.shard_map(
        on_device, mesh=mesh, in_specs=in_specs, out_specs=out_specs, check_vma=False
    )
```

```python
import jax
import jax.numpy as jnp
from jax import lax
from jax.experimental import pallas as pl
from jax.experimental.pallas import tpu as pltpu
from jax.sharding import PartitionSpec as P

NDATE = 32
COLS = 128
ROWS = 8
PLANES = 2 * NDATE
EPSILON = 1e-06
MESH = pl.DeviceIdType.MESH
F32 = jnp.float32
BF16 = jnp.bfloat16


def iota(shape, axis):
    return lax.broadcasted_iota(jnp.int32, shape, axis)


def pack_rim(slc_ref, rim_ref):
    lane = iota((ROWS, COLS), 1)
    row = iota((ROWS, COLS), 0)
    for dest in range(NDATE):
        for part in range(2):
            if dest > 0:
                left = slc_ref[part, :, (dest - 1) * COLS : dest * COLS]
            else:
                left = jnp.zeros((ROWS, COLS), F32)
            if dest < NDATE - 1:
                right = slc_ref[part, :, (dest + 1) * COLS : (dest + 2) * COLS]
            else:
                right = jnp.zeros((ROWS, COLS), F32)
            both = jnp.where(lane < 8, right, left)
            spread = pltpu.roll(both, 8, 1, stride=16, stride_axis=0)
            spread = jnp.where(lane // 16 == row, spread, 0.0)
            rim_ref[dest, part : part + 1, :] = jnp.sum(spread, axis=0, keepdims=True)


def hops(step):
    along_y, along_x = (min(n, 4 - n) for n in step)
    return along_y + along_x, along_y


CHIPS = sorted(((g, i) for g in range(4) for i in range(4)), key=hops)
FAR = CHIPS[12:]
NEAR = CHIPS[:12]
SENDS = [(g, i, k) for g, i in CHIPS for k in range(2) if (g, i, k) != (0, 0, 0)]


def peer(date, g, i, k):
    return (date // 8 + g) % 4 * 8 + (date // 2 + i) % 4 * 2 + (date + k) % 2


WIN = 16
GROUPS = 17


def split(x):
    high = x.astype(BF16).astype(F32)
    return high, x - high


def date_vectors(offs_ref, axis):
    if axis == 0:
        row = iota((8, COLS), 0)
        out = []
        for part in range(4):
            vec = jnp.zeros((8, COLS), jnp.int32)
            for s in range(8):
                vec = jnp.where(row == s, offs_ref[0, part * 8 + s] + 2, vec)
            out.append(vec)
        return out
    lane = iota((8, COLS), 1) % NDATE
    vec = jnp.zeros((8, COLS), jnp.int32)
    row_vec = jnp.zeros((8, COLS), jnp.int32)
    for s in range(NDATE):
        vec = jnp.where(lane == s, offs_ref[1, s] + 2, vec)
        row_vec = jnp.where(lane == s, offs_ref[0, s] + 2, row_vec)
    return vec, row_vec


def mix_rows(rows, steps):
    bit0, bit1, bit2 = (steps & 1) != 0, (steps & 2) != 0, steps == 4
    one = [jnp.where(bit0, rows[i + 1], rows[i]) for i in range(22)]
    two = [jnp.where(bit1, one[i + 2], one[i]) for i in range(19)]
    base = [jnp.where(bit2, rows[i + 4], two[i]) for i in range(19)]
    return [
        0.5625 * (base[i + 1] + base[i + 2]) - 0.0625 * (base[i] + base[i + 3]) for i in range(WIN)
    ]


def all_of(ref, sem):
    pltpu.make_async_copy(ref, ref, sem).wait()


def kernel(
    offs_in,
    slc_ref,
    mask_in,
    out_ref,
    eigen_ref,
    offs_ref,
    mask_ref,
    slc_here,
    rim_here,
    main_ref,
    rim_ref,
    slab,
    mixed,
    tall,
    rim_tall,
    keys,
    plain,
    sums,
    slots,
    vecs,
    own_sem,
    send_sem,
    recv_sem,
    fwd_send,
    fwd_recv,
    hop_send,
    hop_recv,
    far_send,
    far_recv,
):
    date_pos, row_pos = lax.axis_index("date"), lax.axis_index("row")
    last_date, last_row = lax.axis_size("date") - 1, lax.axis_size("row") - 1
    lane8 = iota((8, COLS), 1)
    sub8 = iota((8, COLS), 0)

    load = pltpu.make_async_copy(slc_ref, slc_here, own_sem.at[2])
    load_mask = pltpu.make_async_copy(mask_in, mask_ref, own_sem.at[3])
    load_offs = pltpu.make_async_copy(offs_in, offs_ref, own_sem.at[4])
    load.start()
    load_mask.start()
    load_offs.start()
    barrier = pltpu.get_barrier_semaphore()
    for s in (1, last_row):
        pl.semaphore_signal(
            barrier, inc=1, device_id={"row": (row_pos + s) % (last_row + 1)}, device_id_type=MESH
        )
    for g, i, k in SENDS[::-1]:
        pl.semaphore_signal(
            barrier, inc=1, device_id={"date": peer(date_pos, g, i, k)}, device_id_type=MESH
        )

    load.wait()
    pack_rim(slc_here, rim_here)
    pl.semaphore_wait(barrier, NDATE + 1)

    def part(which, date):
        return (
            (slc_here.at[:, :, pl.ds(pl.multiple_of(date * COLS, COLS), COLS)], main_ref)
            if which == 0
            else (rim_here.at[date], rim_ref)
        )

    def send(which, g, i, k):
        dest = peer(date_pos, g, i, k)
        src, ref = part(which, dest)
        return pltpu.make_async_remote_copy(
            src_ref=src,
            dst_ref=ref.at[1, date_pos],
            send_sem=send_sem.at[which],
            recv_sem=own_sem.at[1]
            if which
            else own_sem.at[5]
            if (g, i) in FAR
            else recv_sem.at[g, i],
            device_id={"date": dest},
            device_id_type=MESH,
        )

    def sends_to(side):
        return row_pos > 0 if side == 0 else row_pos < last_row

    def gets_from(side):
        return row_pos < last_row if side == 0 else row_pos > 0

    def hop(side, n):
        g, i = FAR[n]
        chip = (date_pos // 8 + g) % 4 * 4 + (date_pos // 2 + i) % 4
        cols = pl.ds(pl.multiple_of(chip * 2 * COLS, 2 * COLS), 2 * COLS)
        return pltpu.make_async_remote_copy(
            src_ref=slc_here.at[:, :, cols],
            dst_ref=slab.at[side, :, :, cols],
            send_sem=hop_send.at[side],
            recv_sem=hop_recv.at[side, n],
            device_id={"row": row_pos - 1 if side == 0 else row_pos + 1},
            device_id_type=MESH,
        )

    def far(side, n, k):
        dest = peer(date_pos, *FAR[n], k)
        return pltpu.make_async_remote_copy(
            src_ref=slab.at[side, :, :, pl.ds(pl.multiple_of(dest * COLS, COLS), COLS)],
            dst_ref=main_ref.at[2 - 2 * side, date_pos],
            send_sem=far_send.at[side],
            recv_sem=far_recv.at[side],
            device_id={"date": dest},
            device_id_type=MESH,
        )

    hops_out = [[hop(side, n) for n in range(len(FAR))] for side in range(2)]
    fars = [[far(side, n, k) for n in range(len(FAR)) for k in range(2)] for side in range(2)]
    for side in range(2):

        @pl.when(sends_to(side))
        def _(side=side):
            for copy in hops_out[side]:
                copy.start()

    mains = {step: send(0, *step) for step in SENDS}
    rims = {step: send(1, *step) for step in SENDS}
    for step in SENDS:
        mains[step].start()
        rims[step].start()
    own = []
    for which in range(2):
        src, ref = part(which, date_pos)
        own.append(
            pltpu.make_async_copy(
                src, ref.at[1, date_pos], own_sem.at[1] if which else recv_sem.at[0, 0]
            )
        )
    for copy in own:
        copy.start()

    load_mask.wait()
    load_offs.wait()
    population = jnp.zeros((8, COLS), jnp.int32)
    for w in range(5):
        population = population + lax.population_count(mask_ref[w])
    population = population.astype(F32)
    zero8 = jnp.zeros((8, COLS), jnp.int32)
    for r in range(8):
        pieces = []
        for n in range(WIN):
            i = n - r
            if 0 <= i <= 8:
                nine = (mask_ref[i // 2, r : r + 1, :] >> (9 * (i % 2))) & 511
                pieces.append(jnp.broadcast_to(nine, (8, COLS)))
            else:
                pieces.append(zero8)
        slots[r] = jnp.concatenate(pieces, axis=0).T


    def forward(side, number, first, count, ref):
        slot, to = (2, row_pos - 1) if side == 0 else (0, row_pos + 1)
        return pltpu.make_async_remote_copy(
            src_ref=ref.at[1, pl.ds(first, count)],
            dst_ref=ref.at[slot, pl.ds(first, count)],
            send_sem=fwd_send.at[side, number // len(NEAR)],
            recv_sem=fwd_recv.at[side, number // len(NEAR)],
            device_id={"row": to},
            device_id_type=MESH,
        )

    def forwards(side):
        out = []
        for number, (g, i) in enumerate(NEAR):
            first = (date_pos // 8 + 4 - g) % 4 * 8 + (date_pos // 2 + 4 - i) % 4 * 2
            out.append(forward(side, number, first, 2, main_ref))
        return out + [forward(side, len(NEAR), 0, NDATE, rim_ref)]

    before, after = forwards(0), forwards(1)
    for number in range(len(NEAR) + 1):
        if number < len(NEAR):
            g, i = NEAR[number]
            all_of(main_ref.at[1, pl.ds(0, 2)], recv_sem.at[g, i])
        else:
            all_of(rim_ref.at[1], own_sem.at[1])

        @pl.when(row_pos > 0)
        def _(number=number):
            before[number].start()
            if number < len(FAR):
                hops_out[1][number].wait_recv()
                fars[1][2 * number].start()
                fars[1][2 * number + 1].start()

        @pl.when(row_pos < last_row)
        def _(number=number):
            after[number].start()
            if number < len(FAR):
                hops_out[0][number].wait_recv()
                fars[0][2 * number].start()
                fars[0][2 * number + 1].start()

    all_of(main_ref.at[1, pl.ds(0, NDATE - 1)], send_sem.at[0])
    all_of(rim_ref.at[1, pl.ds(0, NDATE - 1)], send_sem.at[1])
    all_of(main_ref.at[1, pl.ds(0, 2 * len(FAR))], own_sem.at[5])
    for side in range(2):

        @pl.when(gets_from(side))
        def _(side=side):
            all_of(main_ref.at[1, pl.ds(0, 2 * len(FAR))], far_send.at[side])
            all_of(main_ref.at[1, pl.ds(0, 2 * len(FAR))], far_recv.at[side])
            all_of(main_ref.at[1, pl.ds(0, 2 * len(NEAR))], fwd_recv.at[side, 0])

    main_rows = main_ref.reshape(-1, COLS)
    row_steps = date_vectors(offs_ref, 0)
    col_steps, lane_row_steps = date_vectors(offs_ref, 1)
    for part in range(2):
        for eight in range(4):
            rows = []
            for i in range(23):
                slot, row = (i + 1) // 8, (i + 1) % 8
                start = ((slot * NDATE + eight * 8) * 2 + part) * ROWS + row
                x = main_rows[pl.ds(start, 8, stride=2 * ROWS), :]
                if slot == 0:
                    x = jnp.where(row_pos > 0, x, 0.0)
                if slot == 2:
                    x = jnp.where(row_pos < last_row, x, 0.0)
                rows.append(x)
            for i, x in enumerate(mix_rows(rows, row_steps[eight])):
                mixed[i, part * NDATE + eight * 8 : part * NDATE + eight * 8 + 8, :] = x

    for m in range(8):
        tall[m, 8:136, :] = jnp.concatenate([mixed[2 * m], mixed[2 * m + 1]], axis=0).T
    for side in range(2):

        @pl.when(gets_from(side))
        def _(side=side):
            all_of(rim_ref.at[1], fwd_recv.at[side, 1])

    for slot in range(3):
        x = jnp.concatenate([rim_ref[slot, :, 0, :], rim_ref[slot, :, 1, :]], axis=0)
        if slot == 0:
            x = jnp.where(row_pos > 0, x, 0.0)
        if slot == 2:
            x = jnp.where(row_pos < last_row, x, 0.0)
        rim_tall[slot] = jnp.concatenate([x, x], axis=0).T
    for side in range(2):
        rows = []
        for i in range(23):
            slot, row = (i + 1) // 8, (i + 1) % 8
            rows.append(rim_tall[slot, 16 * row + 8 * side : 16 * row + 8 * side + 8, :])
        done = mix_rows(rows, lane_row_steps)
        for m in range(8):
            tall[m, 136 * side : 136 * side + 8, :] = jnp.where(
                lane8 < PLANES, done[2 * m], done[2 * m + 1]
            )

    for m in range(8):
        row = 8 * row_pos - 4 + 2 * m + (lane8 >= PLANES).astype(jnp.int32)
        inside = (row >= 0) & (row < 8 * (last_row + 1))
        weights = []
        for s in range(8):
            w = jnp.zeros((8, COLS), F32)
            for tap, value in enumerate((-0.0625, 0.5625, 0.5625, -0.0625)):
                w = jnp.where(col_steps + tap == s, value, w)
            weights.append(jnp.where(inside, w, 0.0))
        for g in range(GROUPS):
            x = weights[0] * tall[m, 8 * g + 1 : 8 * g + 9, :]
            for s in range(1, 8):
                x = x + weights[s] * tall[m, 8 * g + 1 + s : 8 * g + 9 + s, :]
            if g == 0:
                x = jnp.where((sub8 >= 4) | (date_pos > 0), x, 0.0)
            if g == GROUPS - 1:
                x = jnp.where((sub8 < 4) | (date_pos < last_date), x, 0.0)
            other = pltpu.roll(x, PLANES, 1)
            a = jnp.where(lane8 < PLANES, x, other)
            b = jnp.where(lane8 < PLANES, other, x)
            z = jnp.concatenate([a, b], axis=0)
            high, low = split(z)
            lane16 = iota((16, COLS), 1)
            first = g * COLS + 16 * m
            keys[first : first + 16, :] = jnp.where(lane16 < PLANES, high, low).astype(BF16)
            plain[first : first + 16, :] = z

    k_in = iota((COLS, COLS), 0) // NDATE % 2
    k_out = iota((COLS, COLS), 1) // PLANES
    adder = jnp.where(k_in == k_out, 1.0, 0.0).astype(BF16)
    for g in range(GROUPS):
        rows = slice(g * COLS, (g + 1) * COLS)
        total = jnp.dot(keys[rows, :], adder, preferred_element_type=F32)
        high, low = split(plain[rows, :] * total)
        sums[rows, :COLS] = high.astype(BF16)
        sums[rows, COLS:] = low.astype(BF16)

    across = lane8 % 8 - sub8
    shift0 = jnp.where(across >= 0, across, 31)
    shift1 = jnp.where(across <= 0, across + 8, 31)
    lane64 = iota((64, COLS), 1)
    quarter = lane64 // NDATE
    outer = (quarter == 0) | (quarter == 3)
    sign_a = jnp.where(quarter % 2 == 0, 1.0, -1.0)

    def first(blk):
        q0 = blk * COLS
        bits = []
        for r in range(8):
            w = slots[r, blk * 8 : blk * 8 + 8, :]
            bits.append(jnp.concatenate([(w >> shift0) & 1, (w >> shift1) & 1], axis=1))
        mask = jnp.concatenate(bits, axis=0).astype(F32)
        u = jnp.dot(mask.astype(BF16), sums[q0 : q0 + 2 * COLS, :], preferred_element_type=F32)
        return mask, u

    def second(blk, u):
        q0 = blk * COLS
        near = keys[q0 : q0 + 2 * COLS, :]
        u = u[:, :COLS] + u[:, COLS:]
        same = jnp.where(lane64 < PLANES, u, pltpu.roll(u, PLANES, 1))
        cross = jnp.where(outer, pltpu.roll(u, 32, 1), pltpu.roll(u, 96, 1))
        v = same + sign_a * cross
        turned = sign_a * pltpu.roll(v, 32, 1)
        both = jnp.concatenate([v, turned], axis=0)
        high, low = split(both)
        left = jnp.concatenate([high, low], axis=1).astype(BF16)
        right = jnp.concatenate([near, near], axis=1)
        a = lax.dot_general(
            left, right, (((1,), (1,)), ((), ())), preferred_element_type=F32
        )
        return v, a

    def third(blk, mask, a):
        q0 = blk * COLS
        near = keys[q0 : q0 + 2 * COLS, :]
        a = a * jnp.concatenate([mask, mask], axis=0)
        high, low = split(a)
        both = jnp.concatenate([high.astype(BF16), low.astype(BF16)], axis=0)
        return jnp.dot(both, near, preferred_element_type=F32)

    def fourth(blk, v, c):
        c = c[:128] + c[128:]
        c = c + pltpu.roll(c, PLANES, 1)
        v2 = c[:64] - sign_a * pltpu.roll(c[64:], 32, 1)
        both = jnp.where(lane64 < PLANES, v2, v)
        for r in range(8):
            vecs[r, blk * 8 : blk * 8 + 8, :] = both[8 * r : 8 * r + 8, :]

    blocks = range(16)
    ones = [first(b) for b in blocks]
    twos = [second(b, ones[b][1]) for b in blocks]
    threes = [third(b, ones[b][0], twos[b][1]) for b in blocks]
    for b in blocks:
        fourth(b, twos[b][0], threes[b])

    for r in range(8):
        x = vecs[r].T
        pop = population[r : r + 1, :]
        inv = 1.0 / pop
        n1 = jnp.sum(x[PLANES:] * x[PLANES:], axis=0, keepdims=True) * (inv * inv)
        inv2 = inv * inv
        x2 = x[:PLANES] * inv2
        n2 = jnp.sum(x2 * x2, axis=0, keepdims=True)
        root2 = jnp.sqrt(n2 + EPSILON)
        root1 = jnp.sqrt(n1 + EPSILON)
        eigen_ref[r : r + 1, :] = root2 / root1
        out_ref[pl.ds(r, PLANES, stride=ROWS), :] = x2 * (jnp.sqrt(F32(NDATE)) / root2)

    for side in range(2):

        @pl.when(sends_to(side))
        def _(side=side):
            all_of(main_ref.at[1, pl.ds(0, 2 * len(FAR))], hop_send.at[side])
            all_of(main_ref.at[1, pl.ds(0, 2 * len(NEAR))], fwd_send.at[side, 0])
            all_of(rim_ref.at[1], fwd_send.at[side, 1])


def hand_out(linked_ref, eigen_ref, linked_out, eigen_out, sem):
    copies = [
        pltpu.make_async_copy(linked_ref, linked_out, sem.at[0]),
        pltpu.make_async_copy(eigen_ref, eigen_out, sem.at[1]),
    ]
    for copy in copies:
        copy.start()
    for copy in copies:
        copy.wait()


def on_device(slc, offsets, masks):
    hbm = pl.BlockSpec(memory_space=pltpu.HBM)
    vmem = pl.BlockSpec(memory_space=pltpu.VMEM)
    linked, eigen = pl.pallas_call(
        kernel,
        out_shape=(
            jax.ShapeDtypeStruct((PLANES * ROWS, COLS), F32),
            jax.ShapeDtypeStruct((ROWS, COLS), F32),
        ),
        in_specs=[hbm, hbm, hbm],
        out_specs=(vmem, vmem),
        scratch_shapes=[
            pltpu.SMEM((2, NDATE), jnp.int32),
            pltpu.VMEM((5, ROWS, COLS), jnp.int32),
            pltpu.VMEM((2, ROWS, NDATE * COLS), F32),
            pltpu.VMEM((NDATE, 2, COLS), F32),
            pltpu.VMEM((3, NDATE, 2, ROWS, COLS), F32),
            pltpu.VMEM((3, NDATE, 2, COLS), F32),
            pltpu.VMEM((2, 2, ROWS, NDATE * COLS), F32),
            pltpu.VMEM((WIN, PLANES, COLS), F32),
            pltpu.VMEM((8, 144, COLS), F32),
            pltpu.VMEM((3, COLS, COLS), F32),
            pltpu.VMEM((GROUPS * COLS, COLS), BF16),
            pltpu.VMEM((GROUPS * COLS, COLS), F32),
            pltpu.VMEM((GROUPS * COLS, 2 * COLS), BF16),
            pltpu.VMEM((8, COLS, COLS), jnp.int32),
            pltpu.VMEM((8, COLS, COLS), F32),
            pltpu.SemaphoreType.DMA((6,)),
            pltpu.SemaphoreType.DMA((2,)),
            pltpu.SemaphoreType.DMA((4, 4)),
            pltpu.SemaphoreType.DMA((2, 2)),
            pltpu.SemaphoreType.DMA((2, 2)),
            pltpu.SemaphoreType.DMA((2,)),
            pltpu.SemaphoreType.DMA((2, len(FAR))),
            pltpu.SemaphoreType.DMA((2,)),
            pltpu.SemaphoreType.DMA((2,)),
        ],
        compiler_params=pltpu.CompilerParams(
            collective_id=0, has_side_effects=True, vmem_limit_bytes=48 * 1024 * 1024
        ),
        name="phase_linking",
    )(*(pltpu.with_memory_space_constraint(x, pltpu.HBM) for x in (offsets, slc[:, 0], masks)))
    linked, eigen = pl.pallas_call(
        hand_out,
        out_shape=(
            jax.ShapeDtypeStruct((PLANES * ROWS, COLS), F32),
            jax.ShapeDtypeStruct((ROWS, COLS), F32),
        ),
        in_specs=[vmem, vmem],
        out_specs=(hbm, hbm),
        scratch_shapes=[pltpu.SemaphoreType.DMA((2,))],
        name="hand_out",
    )(*(pltpu.with_memory_space_constraint(x, pltpu.VMEM) for x in (linked, eigen)))
    return linked.reshape(2, NDATE, ROWS, COLS), eigen


def solution(mesh):
    in_specs = (P(None, "date", "row", None), P(), P(None, "row", "date"))
    out_specs = (P(None, None, "row", "date"), P("row", "date"))
    return jax.shard_map(
        on_device, mesh=mesh, in_specs=in_specs, out_specs=out_specs, check_vma=False
    )
```
